256 devices in a mesh: gx: 8 (over z), gy: 8 (over x, core), gz: 4 (over y).
Axes of the slice: x: 4, y: 4, z: 8, core: 2. Of those that a mesh axis runs over, the one named last changes fastest.
Arguments:
- velocity: float32 [3, 64, 128, 1024], P(None, 'gz', 'gx', 'gy'), may hold values from -20 to 20
- owner: int32 [262144, 1], P(('gx', 'gy', 'gz')), may hold values from 0 to 63; in each aligned block of 1024 rows (0 to 1023, 1024 to 2047, ...) at most 64 rows name the same one
- cell_x: int32 [262144], P(('gx', 'gy', 'gz')), may hold values from 0 to 14
- cell_y: int32 [262144], P(('gx', 'gy', 'gz')), may hold values from 0 to 126
- cell_z: int32 [262144], P(('gx', 'gy', 'gz')), may hold values from 0 to 14
- query_weights: float32 [3, 262144], P(None, ('gx', 'gy', 'gz')), may hold values from 0 to 1
Outputs:
- query_stress: float32 [6, 262144], P(None, ('gx', 'gy', 'gz'))
The draws below stay inside these ranges and needn't reach their ends.
Inputs may be any that keep to these rules, and one draw needn't show every extreme that they name: Among the queries held by one device, at most 64 name the same owner, and in every draw some owner is named by exactly 64 of them. `cell_x`: the corner cell plus one stays in the same brick.
All inputs are finite; a program needn't handle non-finite values.
Results may differ from the reference program's by a relative error of at most 0.0003.
Values sent between devices are 32-bit elements; how exact they have to be, the bound alone decides.
A program may use at most 64 MiB of HBM per device.

```python
import math
import jax
import jax.numpy as jnp
import numpy as np
from jax import lax

CX = 16
CY = 128
CZ = 16
Q = 1024
FW = 32
NX = 128
NY = 1024
NZ = 64
NQ = 262144
CAP = 64
N_GX = 8
N_GY = 8
N_GZ = 4


def draw_velocity(key, part):
    keys = jax.random.split(jax.random.fold_in(key, 17), 8)
    two_pi = 2.0 * math.pi
    zc = jnp.arange(NZ).astype(jnp.float32) * (two_pi / NZ)
    xc = jnp.arange(NX).astype(jnp.float32) * (two_pi / NX)
    yc = jnp.arange(NY).astype(jnp.float32) * (two_pi / NY)
    wave_z = jax.random.randint(keys[0], (3, 4), 0, 2).astype(jnp.float32)
    wave_x = jax.random.randint(keys[1], (3, 4), 1, 4).astype(jnp.float32)
    wave_y = jax.random.randint(keys[2], (3, 4), 1, 4).astype(jnp.float32)
    phases = jax.random.uniform(keys[3], (3, 4, 3), jnp.float32, 0.0, two_pi)
    amplitude = jax.random.uniform(keys[4], (3, 4), jnp.float32, -1.5, 1.5)
    large = jnp.zeros((3, NZ, NX, NY), jnp.float32)
    for mode in range(4):
        along_z = jnp.cos(wave_z[:, mode][:, None] * zc[None, :] + phases[:, mode, 0][:, None])
        along_x = jnp.cos(wave_x[:, mode][:, None] * xc[None, :] + phases[:, mode, 1][:, None])
        along_y = jnp.cos(wave_y[:, mode][:, None] * yc[None, :] + phases[:, mode, 2][:, None])
        large = large + amplitude[:, mode][:, None, None, None] * along_z[:, :, None, None] * along_x[:, None, :, None] * along_y[:, None, None, :]
    shift = jax.random.uniform(keys[5], (2,), jnp.float32, 0.0, two_pi)
    envelope = jnp.exp(0.5 * jnp.cos(xc + shift[0])[:, None] * jnp.cos(yc + shift[1])[None, :])
    noise = jnp.clip(jax.random.normal(keys[6], (3, NZ, NX, NY), jnp.float32), -4.0, 4.0)
    shared = jnp.clip(jax.random.normal(keys[7], (NZ, NX, NY), jnp.float32), -4.0, 4.0)
    return large + envelope[None, None] * (noise + 0.7 * shared[None])


def set_ends(array, own_key, least, high):
    place = [jax.random.randint(jax.random.fold_in(own_key, axis), (), 0, length) for axis, length in enumerate(array.shape)]
    widest = array.shape.index(max(array.shape))
    beside = place[:widest] + [(place[widest] + 1) % array.shape[widest]] + place[widest + 1:]
    return array.at[tuple(place)].set(least).at[tuple(beside)].set(high)


def steps_of(stream_key, dims, cuts, smallest, high):
    level, own = 1.0, jax.random.fold_in(stream_key, 6)
    for position, shards_of in cuts:
        draws = jnp.exp(jax.random.uniform(jax.random.fold_in(own, position), (shards_of,), jnp.float32, smallest / len(cuts), high / len(cuts)))
        level = level * jnp.repeat(draws, dims[position] // shards_of).reshape([-1 if axis == position else 1 for axis in range(len(dims))])
    return level


def routed_block(own_key, own, number, rows, number_of, top, bound, skew):
    order = jax.random.permutation(own_key, number_of)
    packed, usual = shares(number_of, rows * top, bound, skew, True), shares(number_of, rows * top, bound, skew, False)
    places = jnp.arange(number_of)

    def named(tallies, offset_by):
        used = int((tallies > 0).sum())
        fixed = max(1, used // 4)
        moved = fixed + (places - fixed + offset_by * (used - fixed)) % max(1, number_of - fixed)
        return jnp.zeros((number_of,), jnp.int32).at[order[jnp.where(places < fixed, places, moved)]].set(jnp.asarray(tallies, jnp.int32))

    tallies = jnp.where(number % 4 == 0, named(packed, number // 4), named(usual, number - number // 4 - 1))
    mixed = jax.random.permutation(jax.random.fold_in(own, 3), number_of)
    source_of, taker = mixed[0:number_of // 2 * 2:2], mixed[1:number_of // 2 * 2:2]
    slack = jnp.minimum(tallies[source_of] - 1, bound - tallies[taker]) // 2
    slack = jnp.where((source_of == order[0]) | (taker == order[0]) | (tallies[taker] == 0), 0, jnp.maximum(slack, 0))
    moved = jax.random.randint(jax.random.fold_in(own, 4), (number_of // 2,), 0, 1 << 20) % (slack + 1)
    tallies = tallies.at[source_of].add(-moved).at[taker].add(moved)
    members = jnp.searchsorted(jnp.cumsum(tallies), jnp.arange(rows * top), side="right").astype(jnp.int32)
    grid = members.reshape(top, rows).T
    grid = grid[jax.random.permutation(jax.random.fold_in(own, 1), rows)]
    offset_by = jax.random.randint(jax.random.fold_in(own, 2), (rows, 1), 0, top)
    return jnp.take_along_axis(grid, (jnp.arange(top)[None, :] + offset_by) % top, axis=1)


def shares(count, total, most, lean, full):
    loads = [(1 << 20) // math.isqrt(standing ** lean) + 1 for standing in range(1, count + 1)]
    largest = most if full else min(most, max(-(-total // count), total * loads[0] // sum(loads)))
    least = 1 if total - largest >= count - 1 else 0
    holding, surplus = [largest] + [least] * (count - 1), total - largest - least * (count - 1)
    while surplus > 0:
        candidates = [i for i in range(1, count) if holding[i] < largest] or [i for i in range(1, count) if holding[i] < most]
        mass, budget = sum([loads[i] for i in candidates]), surplus
        for i in candidates:
            extra = min(most - holding[i], max(1, budget * loads[i] // mass), surplus)
            holding[i] = holding[i] + extra
            surplus = surplus - extra
    return np.array(holding)


def setup_inputs(seed: int = 0) -> dict:
    key_of = jax.random.split(jax.random.key(seed), 7)
    velocity = draw_velocity(jax.random.fold_in(key_of[6], 71), 0)
    owner_keys = jax.random.split(jax.random.fold_in(key_of[1], 1), NQ // Q)
    owner_turns = jax.random.permutation(jax.random.fold_in(key_of[1], 3), NQ // Q)
    owner = jax.vmap(lambda own, number: routed_block(jax.random.fold_in(key_of[1], 2), own, number, Q, N_GX * N_GY, 1, CAP, 2))(owner_keys, owner_turns).reshape((NQ, 1))
    cell_x = set_ends(jax.random.randint(key_of[2], (NQ,), 0, CX - 1), jax.random.fold_in(key_of[2], 1), 0, (CX - 1) - 1).astype(jnp.int32)
    cell_y = set_ends(jax.random.randint(key_of[3], (NQ,), 0, CY - 1), jax.random.fold_in(key_of[3], 1), 0, (CY - 1) - 1).astype(jnp.int32)
    cell_z = set_ends(jax.random.randint(key_of[4], (NQ,), 0, CZ - 1), jax.random.fold_in(key_of[4], 1), 0, (CZ - 1) - 1).astype(jnp.int32)
    query_weights = jnp.clip(1.0 * jax.random.uniform(key_of[5], (3, NQ), jnp.float32) ** steps_of(key_of[5], (3, NQ), ((1, 256),), -0.2, 0.2), 0.0, 1.0)
    return {"velocity": velocity, "owner": owner, "cell_x": cell_x, "cell_y": cell_y, "cell_z": cell_z, "query_weights": query_weights}


PAIRS = ((0, 0), (0, 1), (0, 2), (1, 1), (1, 2), (2, 2))


def taps(radius, width):
    offsets = jnp.arange(2 * radius + 1).astype(jnp.float32) - radius
    values = jnp.exp(-6.0 * offsets * offsets / (width * width))
    return values / jnp.sum(values)


def band(length, radius, width):
    weights = taps(radius, width)
    rows = jnp.arange(length + 2 * radius)[:, None]
    cols = jnp.arange(length)[None, :]
    offset = rows - cols
    inside = (offset >= 0) & (offset <= 2 * radius)
    picked = weights[jnp.clip(offset, 0, 2 * radius)]
    return jnp.where(inside, picked, jnp.zeros_like(picked))


def filter_axis(field, axis, block, radius):
    length = field.shape[axis]
    upper = lax.slice_in_dim(field, length - radius, length, axis=axis)
    lower = lax.slice_in_dim(field, 0, radius, axis=axis)
    wide = jnp.concatenate([upper, field, lower], axis=axis)
    matrix = band(block, radius, FW).astype(field.dtype)
    pieces = []
    for number in range(length // block):
        window = lax.slice_in_dim(wide, number * block, number * block + block + 2 * radius, axis=axis)
        result = jnp.tensordot(window, matrix, axes=([axis], [0]), precision=lax.Precision.HIGHEST)
        pieces.append(jnp.moveaxis(result, -1, axis))
    return jnp.concatenate(pieces, axis=axis)


def smooth(field, radius):
    field = filter_axis(field, 0, CZ, radius)
    field = filter_axis(field, 1, CX, radius)
    return filter_axis(field, 2, CY, radius)


def reference(velocity, owner, cell_x, cell_y, cell_z, query_weights):
    radius = FW // 2
    means = [smooth(velocity[k], radius) for k in range(3)]
    holder = jnp.arange(NQ).astype(jnp.int32) // Q
    brick_z = holder % N_GZ
    brick = owner[:, 0]
    glob_x = (brick // N_GY) * CX + cell_x
    glob_y = (brick % N_GY) * CY + cell_y
    glob_z = brick_z * CZ + cell_z
    base = (glob_z * NX + glob_x) * NY + glob_y
    wx = query_weights[0]
    wy = query_weights[1]
    wz = query_weights[2]
    rows = []
    for first, second in PAIRS:
        stress = smooth(velocity[first] * velocity[second], radius) - means[first] * means[second]
        flat = stress.reshape(-1)
        total = jnp.zeros((NQ,), stress.dtype)
        for dz in (0, 1):
            for dx in (0, 1):
                for dy in (0, 1):
                    index = base + dz * NX * NY + dx * NY + dy
                    term = (wz if dz else 1.0 - wz) * (wx if dx else 1.0 - wx) * (wy if dy else 1.0 - wy)
                    total = total + term * flat[index]
        rows.append(total)
    return jnp.stack(rows)
```

```python
import functools

import jax
import jax.numpy as jnp
import numpy as np
from jax import lax
from jax.experimental import pallas as pl
from jax.experimental.pallas import tpu as pltpu
from jax.sharding import PartitionSpec as P

MESH = pl.DeviceIdType.MESH
F32 = jnp.float32
BF16 = jnp.bfloat16
FW = 32
R = FW // 2
CAP = 64
FIELDS = ((0, None), (0, 0), (1, None), (0, 1), (1, 1), (2, None), (0, 2), (1, 2), (2, 2))
PAIRS = ((0, 0), (0, 1), (0, 2), (1, 1), (1, 2), (2, 2))


def taps():
    offsets = np.arange(2 * R + 1).astype(np.float32) - np.float32(R)
    values = np.exp(np.float32(-6.0) * offsets * offsets / np.float32(FW * FW))
    return (values / values.sum(dtype=np.float32)).astype(np.float32)


def split(x):
    hi = x.astype(BF16)
    lo = (x - hi.astype(F32)).astype(BF16)
    return hi, lo


def np_split(x):
    hi = jnp.asarray(x, F32).astype(BF16)
    lo = (jnp.asarray(x, F32) - hi.astype(F32)).astype(BF16)
    return hi, lo


def tables(by):
    g = taps()

    def band(rows, cols, shift):
        m = np.arange(rows)[:, None] - np.arange(cols)[None, :] + shift
        return np.where((m >= 0) & (m <= 2 * R), g[np.clip(m, 0, 2 * R)], np.float32(0))

    sub = band(3 * R, R, 0).T
    mid = band(by, by, R)
    left = band(R, by, 0)
    right = band(R, by, by + R)
    groups = R // 2
    edge = np.zeros((groups // 2, 2 * 128, 2 * by), np.float32)
    for k in range(groups):
        part = edge[k // 2, :, (k % 2) * by : (k % 2 + 1) * by]
        part[R * k : R * k + R] = left
        part[128 + R * k : 128 + R * k + R] = right
    sh, sl = np_split(sub)
    mh, ml = np_split(mid)
    eh, el = np_split(edge)
    return (
        jnp.concatenate([sh, sl, sh], axis=1),
        jnp.concatenate([mh, mh], axis=0),
        ml,
        eh,
        el,
    )


def dot(a, b):
    return jnp.dot(a, b, preferred_element_type=F32)


def kernel(
    sizes,
    v_ref, own_ref, cx_ref, cy_ref, cz_ref, qw_ref, sub_ref, mid_ref, midl_ref, eh_hbm, el_hbm,
    out_ref,
    u, xb, yb, zf, pack, halo, eh, el,
    sendq, gotq, passq, haveq, rows, w1h, w1l, wyb,
    sth, stl, vals, sendr, gotr, passr, haver, onehot, rankhot,
    s1, r1, s2, r2, s3, r3, sa, ra, sb, rb, sc, rc, sd, rd, lsem,
):
    nx, ny, nz = sizes
    g = [float(t) for t in taps()]
    mx, my, mz = lax.axis_index("gx"), lax.axis_index("gy"), lax.axis_index("gz")
    par = lax.rem(my, 2)
    owners = nx * ny
    count = own_ref.shape[1]

    def shifted(first, step):
        on_x = par if first else 1 - par
        on_z = 1 - on_x
        return (
            lax.rem(mx + on_x * (step % nx), nx),
            my,
            lax.rem(mz + on_z * (step % nz), nz),
        )

    def y_peer(step):
        return (mx, lax.rem(my + step % ny, ny), mz)

    def x_peer(step):
        return (lax.rem(mx + step % nx, nx), my, mz)

    def remote(src, dst, ssem, rsem, dev):
        return pltpu.make_async_remote_copy(
            src_ref=src, dst_ref=dst, send_sem=ssem, recv_sem=rsem, device_id=dev, device_id_type=MESH
        )

    load_eh = pltpu.make_async_copy(eh_hbm, eh, lsem.at[0])
    load_el = pltpu.make_async_copy(el_hbm, el, lsem.at[1])
    load_eh.start()
    load_el.start()

    @pl.when(par == 0)
    def _():
        for c in range(3):
            u[c, R : 2 * R] = v_ref[c].reshape(R, R, 128)

    @pl.when(par == 1)
    def _():
        for c in range(3):
            for b in range(R):
                u[c, R + b] = v_ref[c, pl.ds(b, R, stride=R), :]

    barrier = pltpu.get_barrier_semaphore()
    for step in range(1, nx):
        pl.semaphore_signal(barrier, inc=1, device_id=x_peer(step), device_id_type=MESH)
    for step in range(1, ny):
        pl.semaphore_signal(barrier, inc=1, device_id=y_peer(step), device_id_type=MESH)
    for step in (1, nz - 1):
        pl.semaphore_signal(
            barrier, inc=1, device_id=(mx, my, lax.rem(mz + step, nz)), device_id_type=MESH
        )
    pl.semaphore_wait(barrier, nx - 1 + ny - 1 + 2)

    def first_copies(c):
        src = u.at[c, pl.ds(R, R)]
        return (
            remote(src, u.at[c, pl.ds(0, R)], s1.at[c, 0], r1.at[c, 0], shifted(True, 1)),
            remote(src, u.at[c, pl.ds(2 * R, R)], s1.at[c, 1], r1.at[c, 1], shifted(True, -1)),
        )

    def second_copies(f):
        src = xb.at[f, :, pl.ds(R, R)]
        return (
            remote(src, xb.at[f, :, pl.ds(0, R)], s2.at[f, 0], r2.at[f, 0], shifted(False, 1)),
            remote(src, xb.at[f, :, pl.ds(2 * R, R)], s2.at[f, 1], r2.at[f, 1], shifted(False, -1)),
        )

    def y_copies(f):
        return (
            remote(pack.at[0, f], halo.at[1, f], s3.at[f, 0], r3.at[f, 0], y_peer(-1)),
            remote(pack.at[1, f], halo.at[0, f], s3.at[f, 1], r3.at[f, 1], y_peer(1)),
        )

    def exchange(n, peer_of, me, src, dst, ssem, rsem):
        copies = []
        for step in range(1, n):
            copies.append(
                remote(
                    src.at[lax.rem(me + step, n)], dst.at[me], ssem.at[step], rsem.at[step], peer_of(step)
                )
            )
        return copies

    for c in range(3):
        for copy in first_copies(c):
            copy.start()

    bits_y = ny.bit_length() - 1
    own = own_ref[...]
    target = (own & (ny - 1)) * nx + (own >> bits_y)
    hot = (lax.broadcasted_iota(jnp.int32, (owners, count), 0) == target).astype(F32)
    onehot[...] = hot.astype(BF16)
    earlier = (
        lax.broadcasted_iota(jnp.int32, (128, 128), 0) < lax.broadcasted_iota(jnp.int32, (128, 128), 1)
    ).astype(BF16)
    carry = jnp.zeros((owners, 1), F32)
    ranks = []
    for block in range(count // 128):
        part = hot[:, block * 128 : block * 128 + 128]
        before = dot(part.astype(BF16), earlier) + carry
        ranks.append(jnp.sum(part * before, axis=0, keepdims=True))
        carry = carry + jnp.sum(part, axis=1, keepdims=True)
    rank = jnp.concatenate(ranks, axis=1)
    slot = lax.broadcasted_iota(jnp.int32, (CAP, count), 0).astype(F32) == rank
    rankhot[...] = slot.astype(F32)
    cell = (cz_ref[...] * R + cx_ref[...]) * 128 + cy_ref[...]

    def pieces(w):
        p0 = w.astype(BF16).astype(F32)
        p1 = (w - p0).astype(BF16).astype(F32)
        p2 = w - p0 - p1
        return p0, p1, p2

    wx = pieces(qw_ref[0:1, :])
    wy = pieces(qw_ref[1:2, :])
    wz = pieces(qw_ref[2:3, :])
    cell_hi = (cell >> 8).astype(F32)
    cell_lo = (cell & 255).astype(F32)
    zero = jnp.zeros_like(cell_lo)
    order = [
        cell_hi, wx[0], cell_lo, wx[1], zero, wx[2],
        wy[0], wz[0], wy[1], wz[1], wy[2], wz[2],
    ]
    placed = jnp.concatenate(
        [jnp.where(slot, p, jnp.zeros_like(p)).astype(BF16) for p in order], axis=0
    )
    spread = lax.dot_general(
        onehot[...], placed, (((1,), (1,)), ((), ())), preferred_element_type=F32
    )
    lane = lax.broadcasted_iota(jnp.int32, (1, 128), 1)
    scale = jnp.where(lane < CAP, 256.0, 1.0)
    head = spread[:, 0:128] * scale + spread[:, 128:256] + spread[:, 256:384]
    tail = spread[:, 384:512] + spread[:, 512:640] + spread[:, 640:768]
    for j in range(ny):
        sendq[j, 0] = head[j * nx : (j + 1) * nx]
        sendq[j, 1] = tail[j * nx : (j + 1) * nx]
    out_y = exchange(ny, y_peer, my, sendq, gotq, sa, ra)
    for copy in out_y:
        copy.start()
    gotq[my] = sendq[my]

    def first_filter(f):
        i, j = FIELDS[f]

        def chunk(n, _):
            bs = pl.multiple_of((n // 2) * 8, 8)
            h = (n % 2) * 8
            x = u[i, pl.ds(h, 40), pl.ds(bs, 8), :]
            if j is not None:
                x = x * u[j, pl.ds(h, 40), pl.ds(bs, 8), :]
            acc = x[R : R + 8] * g[R]
            for d in range(1, R + 1):
                acc = acc + (x[R - d : R + 8 - d] + x[R + d : R + 8 + d]) * g[R + d]
            xb[f, pl.ds(h, 8), pl.ds(R + bs, 8), :] = acc
            return 0

        lax.fori_loop(0, 4, chunk, 0)
        for copy in second_copies(f):
            copy.start()

    def pass_on():
        for copy in out_y:
            copy.wait_recv()
        for i in range(nx):
            for k in range(2):
                passq[i, k] = gotq[:, k, i, :]
        out_x = exchange(nx, x_peer, mx, passq, haveq, sb, rb)
        for copy in out_x:
            copy.start()
        haveq[mx] = passq[mx]
        return out_x

    field = 0
    for c in range(3):
        for copy in first_copies(c):
            copy.wait_recv()
        for _ in range(c + 2):
            first_filter(field)
            field += 1
        if c == 0:
            out_x = pass_on()

    for copy in out_x:
        copy.wait_recv()
    half = owners // 2
    table = [
        jnp.concatenate([haveq[i, k] for i in range(nx)], axis=0) for k in range(2)
    ]
    low = lane < CAP

    def paired(x, second):
        top, bottom = x[:half], x[half:]
        if second:
            return jnp.where(low, pltpu.roll(top, CAP, 1), bottom)
        return jnp.where(low, top, pltpu.roll(bottom, CAP, 1))

    q_cell = paired(table[0], False).astype(jnp.int32)
    q_wx = paired(table[0], True)
    q_wy = paired(table[1], False)
    q_wz = paired(table[1], True)
    q_cz = (q_cell >> 11).astype(F32)
    q_cx = ((q_cell >> 7) & (R - 1)).astype(F32)
    z_first = par == 0
    rows[0] = jnp.where(z_first, q_cz, q_cx)
    rows[1] = jnp.where(z_first, q_cx, q_cz)
    rows[2] = (q_cell & 127).astype(F32)
    rows[3] = jnp.where(z_first, q_wz, q_wx)
    rows[4] = jnp.where(z_first, q_wx, q_wz)
    rows[5] = q_wy
    chunks = owners * CAP // 256

    def weights(n, _):
        def row(k):
            return jnp.concatenate([rows[k, pl.ds(2 * n, 1), :], rows[k, pl.ds(2 * n + 1, 1), :]], axis=1)

        def hat(size, at, w):
            index = lax.broadcasted_iota(jnp.int32, (size, 256), 0).astype(F32)
            return jnp.where(index == at, 1.0 - w, jnp.where(index == at + 1.0, w, 0.0))

        wa = hat(R, row(0), row(3))
        wb = hat(R, row(1), row(4))
        for a in range(R):
            hi, lo = split(wa[a : a + 1] * wb)
            w1h[n, R * a : R * a + R, :] = hi
            w1l[n, R * a : R * a + R, :] = lo
        wyb[n] = hat(128, row(2), row(5))
        return 0

    lax.fori_loop(0, chunks, weights, 0)

    group = lax.broadcasted_iota(jnp.int32, (1, 128), 1) // R

    def second_filter(f, _):
        for copy in second_copies(f):
            copy.wait_recv()

        def pair(n, _):
            x = jnp.concatenate([xb[f, 2 * n], xb[f, 2 * n + 1]], axis=1)
            hi, lo = split(x)
            o = dot(sub_ref[...], jnp.concatenate([hi, hi, lo], axis=0))
            yb[f, pl.ds(pl.multiple_of(32 * n, 32), R), :] = o[:, :128]
            yb[f, pl.ds(pl.multiple_of(32 * n, 32) + R, R), :] = o[:, 128:]
            return 0

        lax.fori_loop(0, R // 2, pair, 0)
        for e in range(2):
            first = jnp.zeros((R, 128), F32)
            last = jnp.zeros((R, 128), F32)
            for k in range(R // 2):
                turned = yb[f, pl.ds(2 * k + e, R, stride=R), :]
                first = jnp.where(group == k, pltpu.roll(turned, R * k, 1) if k else turned, first)
                last = jnp.where(group == k, pltpu.roll(turned, (R * k + R) % 128, 1) if k < 7 else turned, last)
            pack[0, f, e] = first
            pack[1, f, e] = last
        for copy in y_copies(f):
            copy.start()
        hi, lo = split(yb[f])
        zf[f] = dot(jnp.concatenate([hi, lo], axis=1), mid_ref[...]) + dot(hi, midl_ref[...])
        return 0

    lax.fori_loop(0, 9, second_filter, 0)

    load_eh.wait()
    load_el.wait()

    def wait_y(f, _):
        for copy in y_copies(f):
            copy.wait_recv()
        return 0

    lax.fori_loop(0, 9, wait_y, 0)
    edges = jnp.concatenate([halo[0].reshape(9 * 32, 128), halo[1].reshape(9 * 32, 128)], axis=1)
    eg_hi, eg_lo = split(edges)
    for kk in range(R // 4):
        part = dot(eg_hi, eh[kk]) + dot(eg_lo, eh[kk]) + dot(eg_hi, el[kk])
        for k in range(2):
            at = 32 * (2 * kk + k)
            zf[:, at : at + 32, :] += part[:, 128 * k : 128 * k + 128].reshape(9, 32, 128)

    for p, (i, j) in enumerate(PAIRS):
        tau = zf[FIELDS.index((i, j))] - zf[FIELDS.index((i, None))] * zf[FIELDS.index((j, None))]
        hi, lo = split(tau.T)
        sth[128 * p : 128 * p + 128] = hi
        stl[128 * p : 128 * p + 128] = lo

    def interpolate(n, _):
        high = w1h[n]
        acc = dot(sth[...], high) + dot(stl[...], high) + dot(sth[...], w1l[n])
        wys = wyb[n]
        for p in range(6):
            v = jnp.sum(acc[128 * p : 128 * p + 128] * wys, axis=0, keepdims=True)
            vals[p, pl.ds(2 * n, 1), :] = v[:, :128]
            vals[p, pl.ds(2 * n + 1, 1), :] = v[:, 128:]
        return 0

    lax.fori_loop(0, chunks, interpolate, 0)

    for k in range(3):
        a, b = vals[2 * k], vals[2 * k + 1]
        top = jnp.where(low, a, pltpu.roll(b, CAP, 1))
        bottom = jnp.where(low, pltpu.roll(a, CAP, 1), b)
        both = jnp.concatenate([top, bottom], axis=0)
        for i in range(nx):
            sendr[i, k] = both[i * ny : (i + 1) * ny]
    back_x = exchange(nx, x_peer, mx, sendr, gotr, sc, rc)
    for copy in back_x:
        copy.start()
    gotr[mx] = sendr[mx]
    for copy in back_x:
        copy.wait_recv()
    for j in range(ny):
        for k in range(3):
            passr[j, k] = gotr[:, k, j, :]
    back_y = exchange(ny, y_peer, my, passr, haver, sd, rd)
    for copy in back_y:
        copy.start()
    haver[my] = passr[my]
    for copy in back_y:
        copy.wait_recv()
    pad = jnp.zeros((128 - owners, 128), F32)
    hot_pad = jnp.concatenate([onehot[...], jnp.zeros((128 - owners, count), BF16)], axis=0)
    hot_two = jnp.concatenate([hot_pad, hot_pad], axis=0)
    at_rank = rankhot[...]
    for k in range(3):
        piece = jnp.concatenate([haver[j, k] for j in range(ny)] + [pad], axis=0)
        hi, lo = split(piece.T)
        picked = dot(jnp.concatenate([hi, lo], axis=1), hot_two)
        for h in range(2):
            out_ref[2 * k + h : 2 * k + h + 1, :] = jnp.sum(
                picked[CAP * h : CAP * h + CAP] * at_rank, axis=0, keepdims=True
            )

    for c in range(3):
        for copy in first_copies(c):
            copy.wait_send()

    def wait_sends(f, _):
        for copy in second_copies(f) + y_copies(f):
            copy.wait_send()
        return 0

    lax.fori_loop(0, 9, wait_sends, 0)
    for copy in out_y + out_x + back_x + back_y:
        copy.wait_send()


def on_device(sizes, velocity, owner, cell_x, cell_y, cell_z, query_weights):
    nx, ny, nz = sizes
    count = owner.shape[0]
    owners = nx * ny
    half = owners // 2
    chunks = owners * CAP // 256
    vmem = pl.BlockSpec(memory_space=pltpu.VMEM)
    hbm = pl.BlockSpec(memory_space=pl.ANY)
    dma = pltpu.SemaphoreType.DMA
    return pl.pallas_call(
        functools.partial(kernel, sizes),
        out_shape=jax.ShapeDtypeStruct((6, count), F32),
        in_specs=[vmem] * 9 + [hbm] * 2,
        out_specs=vmem,
        scratch_shapes=[
            pltpu.VMEM((3, 3 * R, R, 128), F32),
            pltpu.VMEM((9, R, 3 * R, 128), F32),
            pltpu.VMEM((9, R * R, 128), F32),
            pltpu.VMEM((9, R * R, 128), F32),
            pltpu.VMEM((2, 9, 2, R, 128), F32),
            pltpu.VMEM((2, 9, 2, R, 128), F32),
            pltpu.VMEM((4, 256, 256), BF16),
            pltpu.VMEM((4, 256, 256), BF16),
            pltpu.VMEM((ny, 2, nx, 128), F32),
            pltpu.VMEM((ny, 2, nx, 128), F32),
            pltpu.VMEM((nx, 2, ny, 128), F32),
            pltpu.VMEM((nx, 2, ny, 128), F32),
            pltpu.VMEM((6, half, 128), F32),
            pltpu.VMEM((chunks, 256, 256), BF16),
            pltpu.VMEM((chunks, 256, 256), BF16),
            pltpu.VMEM((chunks, 128, 256), F32),
            pltpu.VMEM((768, 256), BF16),
            pltpu.VMEM((768, 256), BF16),
            pltpu.VMEM((6, half, 128), F32),
            pltpu.VMEM((nx, 3, ny, 128), F32),
            pltpu.VMEM((nx, 3, ny, 128), F32),
            pltpu.VMEM((ny, 3, nx, 128), F32),
            pltpu.VMEM((ny, 3, nx, 128), F32),
            pltpu.VMEM((owners, count), BF16),
            pltpu.VMEM((CAP, count), F32),
            dma((3, 2)), dma((3, 2)),
            dma((9, 2)), dma((9, 2)),
            dma((9, 2)), dma((9, 2)),
            dma((ny,)), dma((ny,)),
            dma((nx,)), dma((nx,)),
            dma((nx,)), dma((nx,)),
            dma((ny,)), dma((ny,)),
            dma((2,)),
        ],
        compiler_params=pltpu.CompilerParams(
            collective_id=0, has_side_effects=True, vmem_limit_bytes=48 * 1024 * 1024
        ),
    )(
        velocity.reshape(3, R * R, 128),
        owner.reshape(1, count),
        cell_x.reshape(1, count),
        cell_y.reshape(1, count),
        cell_z.reshape(1, count),
        query_weights,
        *tables(velocity.shape[3]),
    )


def solution(mesh):
    sizes = (mesh.shape["gx"], mesh.shape["gy"], mesh.shape["gz"])
    placed = (
        P(None, "gz", "gx", "gy"),
        P(("gx", "gy", "gz"), None),
        P(("gx", "gy", "gz")),
        P(("gx", "gy", "gz")),
        P(("gx", "gy", "gz")),
        P(None, ("gx", "gy", "gz")),
    )
    return jax.shard_map(
        functools.partial(on_device, sizes),
        mesh=mesh,
        in_specs=placed,
        out_specs=P(None, ("gx", "gy", "gz")),
        check_vma=False,
    )
```

```python
import functools

import jax
import jax.numpy as jnp
import numpy as np
from jax import lax
from jax.experimental import pallas as pl
from jax.experimental.pallas import tpu as pltpu
from jax.sharding import PartitionSpec as P

MESH = pl.DeviceIdType.MESH
F32 = jnp.float32
BF16 = jnp.bfloat16
FW = 32
R = FW // 2
CAP = 64
FIELDS = ((0, None), (0, 0), (1, None), (0, 1), (1, 1), (2, None), (0, 2), (1, 2), (2, 2))
PAIRS = ((0, 0), (0, 1), (0, 2), (1, 1), (1, 2), (2, 2))


def taps():
    offsets = np.arange(2 * R + 1).astype(np.float32) - np.float32(R)
    values = np.exp(np.float32(-6.0) * offsets * offsets / np.float32(FW * FW))
    return (values / values.sum(dtype=np.float32)).astype(np.float32)


def split(x):
    hi = x.astype(BF16)
    lo = (x - hi.astype(F32)).astype(BF16)
    return hi, lo


def np_split(x):
    hi = jnp.asarray(x, F32).astype(BF16)
    lo = (jnp.asarray(x, F32) - hi.astype(F32)).astype(BF16)
    return hi, lo


def tables(by):
    g = taps()

    def band(rows, cols, shift):
        m = np.arange(rows)[:, None] - np.arange(cols)[None, :] + shift
        return np.where((m >= 0) & (m <= 2 * R), g[np.clip(m, 0, 2 * R)], np.float32(0))

    sub = band(3 * R, R, 0).T
    mid = band(by, by, R)
    left = band(R, by, 0)
    right = band(R, by, by + R)
    groups = R // 2
    edge = np.zeros((groups // 2, 2 * 128, 2 * by), np.float32)
    for k in range(groups):
        part = edge[k // 2, :, (k % 2) * by : (k % 2 + 1) * by]
        part[R * k : R * k + R] = left
        part[128 + R * k : 128 + R * k + R] = right
    sh, sl = np_split(sub)
    mh, ml = np_split(mid)
    eh, el = np_split(edge)
    return (
        jnp.concatenate([sh, sl, sh], axis=1),
        jnp.concatenate([mh, mh], axis=0),
        ml,
        eh,
        el,
    )


def dot(a, b):
    return jnp.dot(a, b, preferred_element_type=F32)


def kernel(
    sizes,
    v_hbm, own_hbm, cx_hbm, cy_hbm, cz_hbm, qw_hbm, sub_hbm, mid_hbm, midl_hbm, eh_hbm, el_hbm,
    out_ref,
    v_ref, own_ref, cx_ref, cy_ref, cz_ref, qw_ref, sub_ref, mid_ref, midl_ref,
    u, xb, yb, zf, pack, halo, eh, el,
    sendq, gotq, passq, haveq, rows, w1h, w1l, wyb,
    sth, stl, vals, sendr, gotr, passr, haver, onehot, rankhot,
    s1, r1, s2, r2, s3, r3, sa, ra, sb, rb, sc, rc, sd, rd, lsem,
):
    nx, ny, nz = sizes
    g = [float(t) for t in taps()]
    mx, my, mz = lax.axis_index("gx"), lax.axis_index("gy"), lax.axis_index("gz")
    par = lax.rem(my, 2)
    owners = nx * ny
    count = own_ref.shape[1]

    def shifted(first, step):
        on_x = par if first else 1 - par
        on_z = 1 - on_x
        return (
            lax.rem(mx + on_x * (step % nx), nx),
            my,
            lax.rem(mz + on_z * (step % nz), nz),
        )

    def y_peer(step):
        return (mx, lax.rem(my + step % ny, ny), mz)

    def x_peer(step):
        return (lax.rem(mx + step % nx, nx), my, mz)

    def remote(src, dst, ssem, rsem, dev):
        return pltpu.make_async_remote_copy(
            src_ref=src, dst_ref=dst, send_sem=ssem, recv_sem=rsem, device_id=dev, device_id_type=MESH
        )

    loads = [
        pltpu.make_async_copy(src, dst, lsem.at[number])
        for number, (src, dst) in enumerate(
            (
                (v_hbm, v_ref),
                (own_hbm, own_ref),
                (cx_hbm, cx_ref),
                (cy_hbm, cy_ref),
                (cz_hbm, cz_ref),
                (qw_hbm, qw_ref),
                (sub_hbm, sub_ref),
                (mid_hbm, mid_ref),
                (midl_hbm, midl_ref),
                (eh_hbm, eh),
                (el_hbm, el),
            )
        )
    ]
    for load in loads:
        load.start()

    barrier = pltpu.get_barrier_semaphore()
    for step in range(1, nx):
        pl.semaphore_signal(barrier, inc=1, device_id=x_peer(step), device_id_type=MESH)
    for step in range(1, ny):
        pl.semaphore_signal(barrier, inc=1, device_id=y_peer(step), device_id_type=MESH)
    for step in (1, nz - 1):
        pl.semaphore_signal(
            barrier, inc=1, device_id=(mx, my, lax.rem(mz + step, nz)), device_id_type=MESH
        )

    loads[0].wait()

    @pl.when(par == 0)
    def _():
        for c in range(3):
            u[c, R : 2 * R] = v_ref[c].reshape(R, R, 128)

    @pl.when(par == 1)
    def _():
        for c in range(3):
            for b in range(R):
                u[c, R + b] = v_ref[c, pl.ds(b, R, stride=R), :]

    pl.semaphore_wait(barrier, nx - 1 + ny - 1 + 2)

    def first_copies(c):
        src = u.at[c, pl.ds(R, R)]
        return (
            remote(src, u.at[c, pl.ds(0, R)], s1.at[c, 0], r1.at[c, 0], shifted(True, 1)),
            remote(src, u.at[c, pl.ds(2 * R, R)], s1.at[c, 1], r1.at[c, 1], shifted(True, -1)),
        )

    def second_copies(f):
        src = xb.at[f, :, pl.ds(R, R)]
        return (
            remote(src, xb.at[f, :, pl.ds(0, R)], s2.at[f, 0], r2.at[f, 0], shifted(False, 1)),
            remote(src, xb.at[f, :, pl.ds(2 * R, R)], s2.at[f, 1], r2.at[f, 1], shifted(False, -1)),
        )

    def y_copies(f):
        return (
            remote(pack.at[0, f], halo.at[1, f], s3.at[f, 0], r3.at[f, 0], y_peer(-1)),
            remote(pack.at[1, f], halo.at[0, f], s3.at[f, 1], r3.at[f, 1], y_peer(1)),
        )

    def exchange(n, peer_of, me, src, dst, ssem, rsem):
        copies = []
        for step in range(1, n):
            copies.append(
                remote(
                    src.at[lax.rem(me + step, n)], dst.at[me], ssem.at[step], rsem.at[step], peer_of(step)
                )
            )
        return copies

    for c in range(3):
        for copy in first_copies(c):
            copy.start()

    for load in loads[1:6]:
        load.wait()
    bits_y = ny.bit_length() - 1
    own = own_ref[...]
    target = (own & (ny - 1)) * nx + (own >> bits_y)
    hot = (lax.broadcasted_iota(jnp.int32, (owners, count), 0) == target).astype(F32)
    onehot[...] = hot.astype(BF16)
    earlier = (
        lax.broadcasted_iota(jnp.int32, (128, 128), 0) < lax.broadcasted_iota(jnp.int32, (128, 128), 1)
    ).astype(BF16)
    carry = jnp.zeros((owners, 1), F32)
    ranks = []
    for block in range(count // 128):
        part = hot[:, block * 128 : block * 128 + 128]
        before = dot(part.astype(BF16), earlier) + carry
        ranks.append(jnp.sum(part * before, axis=0, keepdims=True))
        carry = carry + jnp.sum(part, axis=1, keepdims=True)
    rank = jnp.concatenate(ranks, axis=1)
    slot = lax.broadcasted_iota(jnp.int32, (CAP, count), 0).astype(F32) == rank
    rankhot[...] = slot.astype(F32)
    cell = (cz_ref[...] * R + cx_ref[...]) * 128 + cy_ref[...]

    def pieces(w):
        p0 = w.astype(BF16).astype(F32)
        p1 = (w - p0).astype(BF16).astype(F32)
        p2 = w - p0 - p1
        return p0, p1, p2

    wx = pieces(qw_ref[0:1, :])
    wy = pieces(qw_ref[1:2, :])
    wz = pieces(qw_ref[2:3, :])
    cell_hi = (cell >> 8).astype(F32)
    cell_lo = (cell & 255).astype(F32)
    zero = jnp.zeros_like(cell_lo)
    order = [
        cell_hi, wx[0], cell_lo, wx[1], zero, wx[2],
        wy[0], wz[0], wy[1], wz[1], wy[2], wz[2],
    ]
    placed = jnp.concatenate(
        [jnp.where(slot, p, jnp.zeros_like(p)).astype(BF16) for p in order], axis=0
    )
    spread = lax.dot_general(
        onehot[...], placed, (((1,), (1,)), ((), ())), preferred_element_type=F32
    )
    lane = lax.broadcasted_iota(jnp.int32, (1, 128), 1)
    scale = jnp.where(lane < CAP, 256.0, 1.0)
    head = spread[:, 0:128] * scale + spread[:, 128:256] + spread[:, 256:384]
    tail = spread[:, 384:512] + spread[:, 512:640] + spread[:, 640:768]
    for j in range(ny):
        sendq[j, 0] = head[j * nx : (j + 1) * nx]
        sendq[j, 1] = tail[j * nx : (j + 1) * nx]
    out_y = exchange(ny, y_peer, my, sendq, gotq, sa, ra)
    for copy in out_y:
        copy.start()
    gotq[my] = sendq[my]

    def first_filter(f):
        i, j = FIELDS[f]

        def chunk(n, _):
            bs = pl.multiple_of((n // 2) * 8, 8)
            h = (n % 2) * 8
            x = u[i, pl.ds(h, 40), pl.ds(bs, 8), :]
            if j is not None:
                x = x * u[j, pl.ds(h, 40), pl.ds(bs, 8), :]
            acc = x[R : R + 8] * g[R]
            for d in range(1, R + 1):
                acc = acc + (x[R - d : R + 8 - d] + x[R + d : R + 8 + d]) * g[R + d]
            xb[f, pl.ds(h, 8), pl.ds(R + bs, 8), :] = acc
            return 0

        lax.fori_loop(0, 4, chunk, 0)
        for copy in second_copies(f):
            copy.start()

    def pass_on():
        for copy in out_y:
            copy.wait_recv()
        for i in range(nx):
            for k in range(2):
                passq[i, k] = gotq[:, k, i, :]
        out_x = exchange(nx, x_peer, mx, passq, haveq, sb, rb)
        for copy in out_x:
            copy.start()
        haveq[mx] = passq[mx]
        return out_x

    field = 0
    for c in range(3):
        for copy in first_copies(c):
            copy.wait_recv()
        for _ in range(c + 2):
            first_filter(field)
            field += 1
        if c == 0:
            out_x = pass_on()

    for copy in out_x:
        copy.wait_recv()
    half = owners // 2
    table = [
        jnp.concatenate([haveq[i, k] for i in range(nx)], axis=0) for k in range(2)
    ]
    low = lane < CAP

    def paired(x, second):
        top, bottom = x[:half], x[half:]
        if second:
            return jnp.where(low, pltpu.roll(top, CAP, 1), bottom)
        return jnp.where(low, top, pltpu.roll(bottom, CAP, 1))

    q_cell = paired(table[0], False).astype(jnp.int32)
    q_wx = paired(table[0], True)
    q_wy = paired(table[1], False)
    q_wz = paired(table[1], True)
    q_cz = (q_cell >> 11).astype(F32)
    q_cx = ((q_cell >> 7) & (R - 1)).astype(F32)
    z_first = par == 0
    rows[0] = jnp.where(z_first, q_cz, q_cx)
    rows[1] = jnp.where(z_first, q_cx, q_cz)
    rows[2] = (q_cell & 127).astype(F32)
    rows[3] = jnp.where(z_first, q_wz, q_wx)
    rows[4] = jnp.where(z_first, q_wx, q_wz)
    rows[5] = q_wy
    chunks = owners * CAP // 256

    def weights(n, _):
        def row(k):
            return jnp.concatenate([rows[k, pl.ds(2 * n, 1), :], rows[k, pl.ds(2 * n + 1, 1), :]], axis=1)

        def hat(size, at, w):
            index = lax.broadcasted_iota(jnp.int32, (size, 256), 0).astype(F32)
            return jnp.where(index == at, 1.0 - w, jnp.where(index == at + 1.0, w, 0.0))

        wa = hat(R, row(0), row(3))
        wb = hat(R, row(1), row(4))
        for a in range(R):
            hi, lo = split(wa[a : a + 1] * wb)
            w1h[n, R * a : R * a + R, :] = hi
            w1l[n, R * a : R * a + R, :] = lo
        wyb[n] = hat(128, row(2), row(5))
        return 0

    lax.fori_loop(0, chunks, weights, 0)

    group = lax.broadcasted_iota(jnp.int32, (1, 128), 1) // R
    for load in loads[6:9]:
        load.wait()

    def second_filter(f, _):
        for copy in second_copies(f):
            copy.wait_recv()

        def pair(n, _):
            x = jnp.concatenate([xb[f, 2 * n], xb[f, 2 * n + 1]], axis=1)
            hi, lo = split(x)
            o = dot(sub_ref[...], jnp.concatenate([hi, hi, lo], axis=0))
            yb[f, pl.ds(pl.multiple_of(32 * n, 32), R), :] = o[:, :128]
            yb[f, pl.ds(pl.multiple_of(32 * n, 32) + R, R), :] = o[:, 128:]
            return 0

        lax.fori_loop(0, R // 2, pair, 0)
        for e in range(2):
            first = jnp.zeros((R, 128), F32)
            last = jnp.zeros((R, 128), F32)
            for k in range(R // 2):
                turned = yb[f, pl.ds(2 * k + e, R, stride=R), :]
                first = jnp.where(group == k, pltpu.roll(turned, R * k, 1) if k else turned, first)
                last = jnp.where(group == k, pltpu.roll(turned, (R * k + R) % 128, 1) if k < 7 else turned, last)
            pack[0, f, e] = first
            pack[1, f, e] = last
        for copy in y_copies(f):
            copy.start()
        hi, lo = split(yb[f])
        zf[f] = dot(jnp.concatenate([hi, lo], axis=1), mid_ref[...]) + dot(hi, midl_ref[...])
        return 0

    lax.fori_loop(0, 9, second_filter, 0)

    for load in loads[9:]:
        load.wait()

    def wait_y(f, _):
        for copy in y_copies(f):
            copy.wait_recv()
        return 0

    lax.fori_loop(0, 9, wait_y, 0)
    edges = jnp.concatenate([halo[0].reshape(9 * 32, 128), halo[1].reshape(9 * 32, 128)], axis=1)
    eg_hi, eg_lo = split(edges)
    for kk in range(R // 4):
        part = dot(eg_hi, eh[kk]) + dot(eg_lo, eh[kk]) + dot(eg_hi, el[kk])
        for k in range(2):
            at = 32 * (2 * kk + k)
            zf[:, at : at + 32, :] += part[:, 128 * k : 128 * k + 128].reshape(9, 32, 128)

    for p, (i, j) in enumerate(PAIRS):
        tau = zf[FIELDS.index((i, j))] - zf[FIELDS.index((i, None))] * zf[FIELDS.index((j, None))]
        hi, lo = split(tau.T)
        sth[128 * p : 128 * p + 128] = hi
        stl[128 * p : 128 * p + 128] = lo

    def interpolate(n, _):
        high = w1h[n]
        acc = dot(sth[...], high) + dot(stl[...], high) + dot(sth[...], w1l[n])
        wys = wyb[n]
        for p in range(6):
            v = jnp.sum(acc[128 * p : 128 * p + 128] * wys, axis=0, keepdims=True)
            vals[p, pl.ds(2 * n, 1), :] = v[:, :128]
            vals[p, pl.ds(2 * n + 1, 1), :] = v[:, 128:]
        return 0

    lax.fori_loop(0, chunks, interpolate, 0)

    for k in range(3):
        a, b = vals[2 * k], vals[2 * k + 1]
        top = jnp.where(low, a, pltpu.roll(b, CAP, 1))
        bottom = jnp.where(low, pltpu.roll(a, CAP, 1), b)
        both = jnp.concatenate([top, bottom], axis=0)
        for i in range(nx):
            sendr[i, k] = both[i * ny : (i + 1) * ny]
    back_x = exchange(nx, x_peer, mx, sendr, gotr, sc, rc)
    for copy in back_x:
        copy.start()
    gotr[mx] = sendr[mx]
    for copy in back_x:
        copy.wait_recv()
    for j in range(ny):
        for k in range(3):
            passr[j, k] = gotr[:, k, j, :]
    back_y = exchange(ny, y_peer, my, passr, haver, sd, rd)
    for copy in back_y:
        copy.start()
    haver[my] = passr[my]
    for copy in back_y:
        copy.wait_recv()
    pad = jnp.zeros((128 - owners, 128), F32)
    hot_pad = jnp.concatenate([onehot[...], jnp.zeros((128 - owners, count), BF16)], axis=0)
    hot_two = jnp.concatenate([hot_pad, hot_pad], axis=0)
    at_rank = rankhot[...]
    for k in range(3):
        piece = jnp.concatenate([haver[j, k] for j in range(ny)] + [pad], axis=0)
        hi, lo = split(piece.T)
        picked = dot(jnp.concatenate([hi, lo], axis=1), hot_two)
        for h in range(2):
            out_ref[2 * k + h : 2 * k + h + 1, :] = jnp.sum(
                picked[CAP * h : CAP * h + CAP] * at_rank, axis=0, keepdims=True
            )

    for c in range(3):
        for copy in first_copies(c):
            copy.wait_send()

    def wait_sends(f, _):
        for copy in second_copies(f) + y_copies(f):
            copy.wait_send()
        return 0

    lax.fori_loop(0, 9, wait_sends, 0)
    for copy in out_y + out_x + back_x + back_y:
        copy.wait_send()


def on_device(sizes, velocity, owner, cell_x, cell_y, cell_z, query_weights):
    nx, ny, nz = sizes
    count = owner.shape[0]
    owners = nx * ny
    half = owners // 2
    chunks = owners * CAP // 256
    vmem = pl.BlockSpec(memory_space=pltpu.VMEM)
    hbm = pl.BlockSpec(memory_space=pltpu.HBM)
    row = pltpu.VMEM((1, count), jnp.int32)
    dma = pltpu.SemaphoreType.DMA
    return pl.pallas_call(
        functools.partial(kernel, sizes),
        out_shape=jax.ShapeDtypeStruct((6, count), F32),
        in_specs=[hbm] * 11,
        out_specs=vmem,
        scratch_shapes=[
            pltpu.VMEM((3, R * R, 128), F32),
            row, row, row, row,
            pltpu.VMEM((3, count), F32),
            pltpu.VMEM((R, 9 * R), BF16),
            pltpu.VMEM((256, 128), BF16),
            pltpu.VMEM((128, 128), BF16),
            pltpu.VMEM((3, 3 * R, R, 128), F32),
            pltpu.VMEM((9, R, 3 * R, 128), F32),
            pltpu.VMEM((9, R * R, 128), F32),
            pltpu.VMEM((9, R * R, 128), F32),
            pltpu.VMEM((2, 9, 2, R, 128), F32),
            pltpu.VMEM((2, 9, 2, R, 128), F32),
            pltpu.VMEM((4, 256, 256), BF16),
            pltpu.VMEM((4, 256, 256), BF16),
            pltpu.VMEM((ny, 2, nx, 128), F32),
            pltpu.VMEM((ny, 2, nx, 128), F32),
            pltpu.VMEM((nx, 2, ny, 128), F32),
            pltpu.VMEM((nx, 2, ny, 128), F32),
            pltpu.VMEM((6, half, 128), F32),
            pltpu.VMEM((chunks, 256, 256), BF16),
            pltpu.VMEM((chunks, 256, 256), BF16),
            pltpu.VMEM((chunks, 128, 256), F32),
            pltpu.VMEM((768, 256), BF16),
            pltpu.VMEM((768, 256), BF16),
            pltpu.VMEM((6, half, 128), F32),
            pltpu.VMEM((nx, 3, ny, 128), F32),
            pltpu.VMEM((nx, 3, ny, 128), F32),
            pltpu.VMEM((ny, 3, nx, 128), F32),
            pltpu.VMEM((ny, 3, nx, 128), F32),
            pltpu.VMEM((owners, count), BF16),
            pltpu.VMEM((CAP, count), F32),
            dma((3, 2)), dma((3, 2)),
            dma((9, 2)), dma((9, 2)),
            dma((9, 2)), dma((9, 2)),
            dma((ny,)), dma((ny,)),
            dma((nx,)), dma((nx,)),
            dma((nx,)), dma((nx,)),
            dma((ny,)), dma((ny,)),
            dma((11,)),
        ],
        compiler_params=pltpu.CompilerParams(
            collective_id=0, has_side_effects=True, vmem_limit_bytes=67043328
        ),
    )(
        velocity.reshape(3, R * R, 128),
        owner.reshape(1, count),
        cell_x.reshape(1, count),
        cell_y.reshape(1, count),
        cell_z.reshape(1, count),
        query_weights,
        *tables(velocity.shape[3]),
    )


def solution(mesh):
    sizes = (mesh.shape["gx"], mesh.shape["gy"], mesh.shape["gz"])
    placed = (
        P(None, "gz", "gx", "gy"),
        P(("gx", "gy", "gz"), None),
        P(("gx", "gy", "gz")),
        P(("gx", "gy", "gz")),
        P(("gx", "gy", "gz")),
        P(None, ("gx", "gy", "gz")),
    )
    return jax.shard_map(
        functools.partial(on_device, sizes),
        mesh=mesh,
        in_specs=placed,
        out_specs=P(None, ("gx", "gy", "gz")),
        check_vma=False,
    )
```

```python
import functools

import jax
import jax.numpy as jnp
import numpy as np
from jax import lax
from jax.experimental import pallas as pl
from jax.experimental.pallas import tpu as pltpu
from jax.sharding import PartitionSpec as P

MESH = pl.DeviceIdType.MESH
F32 = jnp.float32
BF16 = jnp.bfloat16
FW = 32
R = FW // 2
CAP = 64
FIELDS = ((0, None), (0, 0), (1, None), (0, 1), (1, 1), (2, None), (0, 2), (1, 2), (2, 2))
PAIRS = ((0, 0), (0, 1), (0, 2), (1, 1), (1, 2), (2, 2))


def taps():
    offsets = np.arange(2 * R + 1).astype(np.float32) - np.float32(R)
    values = np.exp(np.float32(-6.0) * offsets * offsets / np.float32(FW * FW))
    return (values / values.sum(dtype=np.float32)).astype(np.float32)


def split(x):
    hi = x.astype(BF16)
    lo = (x - hi.astype(F32)).astype(BF16)
    return hi, lo


def np_split(x):
    hi = jnp.asarray(x, F32).astype(BF16)
    lo = (jnp.asarray(x, F32) - hi.astype(F32)).astype(BF16)
    return hi, lo


def tables(by):
    g = taps()

    def band(rows, cols, shift):
        m = np.arange(rows)[:, None] - np.arange(cols)[None, :] + shift
        return np.where((m >= 0) & (m <= 2 * R), g[np.clip(m, 0, 2 * R)], np.float32(0))

    sub = band(3 * R, R, 0).T
    mid = band(by, by, R)
    left = band(R, by, 0)
    right = band(R, by, by + R)
    groups = R // 2
    edge = np.zeros((groups // 2, 2 * 128, 2 * by), np.float32)
    for k in range(groups):
        part = edge[k // 2, :, (k % 2) * by : (k % 2 + 1) * by]
        part[R * k : R * k + R] = left
        part[128 + R * k : 128 + R * k + R] = right
    sh, sl = np_split(sub)
    mh, ml = np_split(mid)
    eh, el = np_split(edge)
    return (
        jnp.concatenate([sh, sl, sh], axis=1),
        jnp.concatenate([mh, mh], axis=0),
        ml,
        eh,
        el,
    )


def dot(a, b):
    return jnp.dot(a, b, preferred_element_type=F32)


def kernel(
    sizes,
    v_hbm, own_hbm, cx_hbm, cy_hbm, cz_hbm, qw_hbm, sub_hbm, mid_hbm, midl_hbm, eh_hbm, el_hbm,
    out_ref,
    v_ref, own_ref, cx_ref, cy_ref, cz_ref, qw_ref, sub_ref, mid_ref, midl_ref,
    u, xb, yb, zf, pack, halo, eh, el,
    sendq, gotq, passq, haveq, rows, w1h, w1l, wyb,
    sth, stl, vals, sendr, gotr, passr, haver, onehot, rankhot,
    s1, r1, s2, r2, s3, r3, sa, ra, sb, rb, sc, rc, sd, rd, lsem,
):
    nx, ny, nz = sizes
    g = [float(t) for t in taps()]
    mx, my, mz = lax.axis_index("gx"), lax.axis_index("gy"), lax.axis_index("gz")
    par = lax.rem(my, 2)
    owners = nx * ny
    count = own_ref.shape[1]

    def shifted(first, step):
        on_x = par if first else 1 - par
        on_z = 1 - on_x
        return (
            lax.rem(mx + on_x * (step % nx), nx),
            my,
            lax.rem(mz + on_z * (step % nz), nz),
        )

    def y_peer(step):
        return (mx, lax.rem(my + step % ny, ny), mz)

    def x_peer(step):
        return (lax.rem(mx + step % nx, nx), my, mz)

    def remote(src, dst, ssem, rsem, dev):
        return pltpu.make_async_remote_copy(
            src_ref=src, dst_ref=dst, send_sem=ssem, recv_sem=rsem, device_id=dev, device_id_type=MESH
        )

    loads = [
        pltpu.make_async_copy(src, dst, lsem.at[number])
        for number, (src, dst) in enumerate(
            (
                (v_hbm, v_ref),
                (own_hbm, own_ref),
                (cx_hbm, cx_ref),
                (cy_hbm, cy_ref),
                (cz_hbm, cz_ref),
                (qw_hbm, qw_ref),
                (sub_hbm, sub_ref),
                (mid_hbm, mid_ref),
                (midl_hbm, midl_ref),
                (eh_hbm, eh),
                (el_hbm, el),
            )
        )
    ]
    for load in loads:
        load.start()

    barrier = pltpu.get_barrier_semaphore()
    for step in range(1, nx):
        pl.semaphore_signal(barrier, inc=1, device_id=x_peer(step), device_id_type=MESH)
    for step in range(1, ny):
        pl.semaphore_signal(barrier, inc=1, device_id=y_peer(step), device_id_type=MESH)
    for step in (1, nz - 1):
        pl.semaphore_signal(
            barrier, inc=1, device_id=(mx, my, lax.rem(mz + step, nz)), device_id_type=MESH
        )

    loads[0].wait()

    @pl.when(par == 0)
    def _():
        for c in range(3):
            u[c, R : 2 * R] = v_ref[c].reshape(R, R, 128)

    @pl.when(par == 1)
    def _():
        for c in range(3):
            for b in range(R):
                u[c, R + b] = v_ref[c, pl.ds(b, R, stride=R), :]

    pl.semaphore_wait(barrier, nx - 1 + ny - 1 + 2)

    def first_copies(c):
        src = u.at[c, pl.ds(R, R)]
        return (
            remote(src, u.at[c, pl.ds(0, R)], s1.at[c, 0], r1.at[c, 0], shifted(True, 1)),
            remote(src, u.at[c, pl.ds(2 * R, R)], s1.at[c, 1], r1.at[c, 1], shifted(True, -1)),
        )

    def second_copies(f):
        src = xb.at[f, :, pl.ds(R, R)]
        return (
            remote(src, xb.at[f, :, pl.ds(0, R)], s2.at[f, 0], r2.at[f, 0], shifted(False, 1)),
            remote(src, xb.at[f, :, pl.ds(2 * R, R)], s2.at[f, 1], r2.at[f, 1], shifted(False, -1)),
        )

    def y_copies(f):
        return (
            remote(pack.at[0, f], halo.at[1, f], s3.at[f, 0], r3.at[f, 0], y_peer(-1)),
            remote(pack.at[1, f], halo.at[0, f], s3.at[f, 1], r3.at[f, 1], y_peer(1)),
        )

    def exchange(n, peer_of, me, src, dst, ssem, rsem):
        copies = []
        for step in range(1, n):
            copies.append(
                remote(
                    src.at[lax.rem(me + step, n)], dst.at[me], ssem.at[step], rsem.at[step], peer_of(step)
                )
            )
        return copies

    for c in range(3):
        for copy in first_copies(c):
            copy.start()

    for load in loads[1:6]:
        load.wait()
    bits_y = ny.bit_length() - 1
    own = own_ref[...]
    target = (own & (ny - 1)) * nx + (own >> bits_y)
    hot = (lax.broadcasted_iota(jnp.int32, (owners, count), 0) == target).astype(F32)
    onehot[...] = hot.astype(BF16)
    earlier = (
        lax.broadcasted_iota(jnp.int32, (128, 128), 0) < lax.broadcasted_iota(jnp.int32, (128, 128), 1)
    ).astype(BF16)
    carry = jnp.zeros((owners, 1), F32)
    ranks = []
    for block in range(count // 128):
        part = hot[:, block * 128 : block * 128 + 128]
        before = dot(part.astype(BF16), earlier) + carry
        ranks.append(jnp.sum(part * before, axis=0, keepdims=True))
        carry = carry + jnp.sum(part, axis=1, keepdims=True)
    rank = jnp.concatenate(ranks, axis=1)
    slot = lax.broadcasted_iota(jnp.int32, (CAP, count), 0).astype(F32) == rank
    rankhot[...] = slot.astype(F32)
    cell = (cz_ref[...] * R + cx_ref[...]) * 128 + cy_ref[...]

    def pieces(w):
        p0 = w.astype(BF16).astype(F32)
        p1 = (w - p0).astype(BF16).astype(F32)
        p2 = w - p0 - p1
        return p0, p1, p2

    wx = pieces(qw_ref[0:1, :])
    wy = pieces(qw_ref[1:2, :])
    wz = pieces(qw_ref[2:3, :])
    cell_hi = (cell >> 8).astype(F32)
    cell_lo = (cell & 255).astype(F32)
    zero = jnp.zeros_like(cell_lo)
    order = [
        cell_hi, wx[0], cell_lo, wx[1], zero, wx[2],
        wy[0], wz[0], wy[1], wz[1], wy[2], wz[2],
    ]
    placed = jnp.concatenate(
        [jnp.where(slot, p, jnp.zeros_like(p)).astype(BF16) for p in order], axis=0
    )
    spread = lax.dot_general(
        onehot[...], placed, (((1,), (1,)), ((), ())), preferred_element_type=F32
    )
    lane = lax.broadcasted_iota(jnp.int32, (1, 128), 1)
    scale = jnp.where(lane < CAP, 256.0, 1.0)
    head = spread[:, 0:128] * scale + spread[:, 128:256] + spread[:, 256:384]
    tail = spread[:, 384:512] + spread[:, 512:640] + spread[:, 640:768]
    for j in range(ny):
        sendq[j, 0] = head[j * nx : (j + 1) * nx]
        sendq[j, 1] = tail[j * nx : (j + 1) * nx]
    out_y = exchange(ny, y_peer, my, sendq, gotq, sa, ra)
    for copy in out_y:
        copy.start()
    gotq[my] = sendq[my]

    def first_filter(f):
        i, j = FIELDS[f]

        def chunk(n, _):
            bs = pl.multiple_of((n // 2) * 8, 8)
            h = (n % 2) * 8
            x = u[i, pl.ds(h, 40), pl.ds(bs, 8), :]
            if j is not None:
                x = x * u[j, pl.ds(h, 40), pl.ds(bs, 8), :]
            acc = x[R : R + 8] * g[R]
            for d in range(1, R + 1):
                acc = acc + (x[R - d : R + 8 - d] + x[R + d : R + 8 + d]) * g[R + d]
            xb[f, pl.ds(h, 8), pl.ds(R + bs, 8), :] = acc
            return 0

        lax.fori_loop(0, 4, chunk, 0)
        for copy in second_copies(f):
            copy.start()

    def pass_on():
        for copy in out_y:
            copy.wait_recv()
        for i in range(nx):
            for k in range(2):
                passq[i, k] = gotq[:, k, i, :]
        out_x = exchange(nx, x_peer, mx, passq, haveq, sb, rb)
        for copy in out_x:
            copy.start()
        haveq[mx] = passq[mx]
        return out_x

    field = 0
    for c in range(3):
        for copy in first_copies(c):
            copy.wait_recv()
        for _ in range(c + 2):
            first_filter(field)
            field += 1
        if c == 0:
            out_x = pass_on()

    for copy in out_x:
        copy.wait_recv()
    half = owners // 2
    table = [
        jnp.concatenate([haveq[i, k] for i in range(nx)], axis=0) for k in range(2)
    ]
    low = lane < CAP

    def paired(x, second):
        top, bottom = x[:half], x[half:]
        if second:
            return jnp.where(low, pltpu.roll(top, CAP, 1), bottom)
        return jnp.where(low, top, pltpu.roll(bottom, CAP, 1))

    q_cell = paired(table[0], False).astype(jnp.int32)
    q_wx = paired(table[0], True)
    q_wy = paired(table[1], False)
    q_wz = paired(table[1], True)
    q_cz = (q_cell >> 11).astype(F32)
    q_cx = ((q_cell >> 7) & (R - 1)).astype(F32)
    z_first = par == 0
    rows[0] = jnp.where(z_first, q_cz, q_cx)
    rows[1] = jnp.where(z_first, q_cx, q_cz)
    rows[2] = (q_cell & 127).astype(F32)
    rows[3] = jnp.where(z_first, q_wz, q_wx)
    rows[4] = jnp.where(z_first, q_wx, q_wz)
    rows[5] = q_wy
    chunks = owners * CAP // 256

    def weights(n, _):
        def row(k):
            return jnp.concatenate([rows[k, pl.ds(2 * n, 1), :], rows[k, pl.ds(2 * n + 1, 1), :]], axis=1)

        def hat(size, at, w):
            index = lax.broadcasted_iota(jnp.int32, (size, 256), 0).astype(F32)
            return jnp.where(index == at, 1.0 - w, jnp.where(index == at + 1.0, w, 0.0))

        wa = hat(R, row(0), row(3))
        wb = hat(R, row(1), row(4))
        for a in range(R):
            hi, lo = split(wa[a : a + 1] * wb)
            w1h[n, R * a : R * a + R, :] = hi
            w1l[n, R * a : R * a + R, :] = lo
        wyb[n] = hat(128, row(2), row(5))
        return 0

    lax.fori_loop(0, chunks, weights, 0)

    group = lax.broadcasted_iota(jnp.int32, (1, 128), 1) // R
    for load in loads[6:9]:
        load.wait()

    def second_filter(f, _):
        for copy in second_copies(f):
            copy.wait_recv()

        def pair(n, _):
            x = jnp.concatenate([xb[f, 2 * n], xb[f, 2 * n + 1]], axis=1)
            hi, lo = split(x)
            o = dot(sub_ref[...], jnp.concatenate([hi, hi, lo], axis=0))
            yb[f, pl.ds(pl.multiple_of(32 * n, 32), R), :] = o[:, :128]
            yb[f, pl.ds(pl.multiple_of(32 * n, 32) + R, R), :] = o[:, 128:]
            return 0

        lax.fori_loop(0, R // 2, pair, 0, unroll=True)
        for e in range(2):
            first = jnp.zeros((R, 128), F32)
            last = jnp.zeros((R, 128), F32)
            for k in range(R // 2):
                turned = yb[f, pl.ds(2 * k + e, R, stride=R), :]
                first = jnp.where(group == k, pltpu.roll(turned, R * k, 1) if k else turned, first)
                last = jnp.where(group == k, pltpu.roll(turned, (R * k + R) % 128, 1) if k < 7 else turned, last)
            pack[0, f, e] = first
            pack[1, f, e] = last
        for copy in y_copies(f):
            copy.start()
        hi, lo = split(yb[f])
        zf[f] = dot(jnp.concatenate([hi, lo], axis=1), mid_ref[...]) + dot(hi, midl_ref[...])
        return 0

    lax.fori_loop(0, 9, second_filter, 0)

    for load in loads[9:]:
        load.wait()

    def wait_y(f, _):
        for copy in y_copies(f):
            copy.wait_recv()
        return 0

    lax.fori_loop(0, 9, wait_y, 0)
    edges = jnp.concatenate([halo[0].reshape(9 * 32, 128), halo[1].reshape(9 * 32, 128)], axis=1)
    eg_hi, eg_lo = split(edges)
    for kk in range(R // 4):
        part = dot(eg_hi, eh[kk]) + dot(eg_lo, eh[kk]) + dot(eg_hi, el[kk])
        for k in range(2):
            at = 32 * (2 * kk + k)
            zf[:, at : at + 32, :] += part[:, 128 * k : 128 * k + 128].reshape(9, 32, 128)

    for p, (i, j) in enumerate(PAIRS):
        tau = zf[FIELDS.index((i, j))] - zf[FIELDS.index((i, None))] * zf[FIELDS.index((j, None))]
        hi, lo = split(tau.T)
        sth[128 * p : 128 * p + 128] = hi
        stl[128 * p : 128 * p + 128] = lo

    def interpolate(n, _):
        high = w1h[n]
        acc = dot(sth[...], high) + dot(stl[...], high) + dot(sth[...], w1l[n])
        wys = wyb[n]
        for p in range(6):
            v = jnp.sum(acc[128 * p : 128 * p + 128] * wys, axis=0, keepdims=True)
            vals[p, pl.ds(2 * n, 1), :] = v[:, :128]
            vals[p, pl.ds(2 * n + 1, 1), :] = v[:, 128:]
        return 0

    lax.fori_loop(0, chunks, interpolate, 0)

    for k in range(3):
        a, b = vals[2 * k], vals[2 * k + 1]
        top = jnp.where(low, a, pltpu.roll(b, CAP, 1))
        bottom = jnp.where(low, pltpu.roll(a, CAP, 1), b)
        both = jnp.concatenate([top, bottom], axis=0)
        for i in range(nx):
            sendr[i, k] = both[i * ny : (i + 1) * ny]
    back_x = exchange(nx, x_peer, mx, sendr, gotr, sc, rc)
    for copy in back_x:
        copy.start()
    gotr[mx] = sendr[mx]
    for copy in back_x:
        copy.wait_recv()
    for j in range(ny):
        for k in range(3):
            passr[j, k] = gotr[:, k, j, :]
    back_y = exchange(ny, y_peer, my, passr, haver, sd, rd)
    for copy in back_y:
        copy.start()
    haver[my] = passr[my]
    for copy in back_y:
        copy.wait_recv()
    pad = jnp.zeros((128 - owners, 128), F32)
    hot_pad = jnp.concatenate([onehot[...], jnp.zeros((128 - owners, count), BF16)], axis=0)
    hot_two = jnp.concatenate([hot_pad, hot_pad], axis=0)
    at_rank = rankhot[...]
    for k in range(3):
        piece = jnp.concatenate([haver[j, k] for j in range(ny)] + [pad], axis=0)
        hi, lo = split(piece.T)
        picked = dot(jnp.concatenate([hi, lo], axis=1), hot_two)
        for h in range(2):
            out_ref[2 * k + h : 2 * k + h + 1, :] = jnp.sum(
                picked[CAP * h : CAP * h + CAP] * at_rank, axis=0, keepdims=True
            )

    for c in range(3):
        for copy in first_copies(c):
            copy.wait_send()

    def wait_sends(f, _):
        for copy in second_copies(f) + y_copies(f):
            copy.wait_send()
        return 0

    lax.fori_loop(0, 9, wait_sends, 0)
    for copy in out_y + out_x + back_x + back_y:
        copy.wait_send()


def on_device(sizes, velocity, owner, cell_x, cell_y, cell_z, query_weights):
    nx, ny, nz = sizes
    count = owner.shape[0]
    owners = nx * ny
    half = owners // 2
    chunks = owners * CAP // 256
    vmem = pl.BlockSpec(memory_space=pltpu.VMEM)
    hbm = pl.BlockSpec(memory_space=pltpu.HBM)
    row = pltpu.VMEM((1, count), jnp.int32)
    dma = pltpu.SemaphoreType.DMA
    return pl.pallas_call(
        functools.partial(kernel, sizes),
        out_shape=jax.ShapeDtypeStruct((6, count), F32),
        in_specs=[hbm] * 11,
        out_specs=vmem,
        scratch_shapes=[
            pltpu.VMEM((3, R * R, 128), F32),
            row, row, row, row,
            pltpu.VMEM((3, count), F32),
            pltpu.VMEM((R, 9 * R), BF16),
            pltpu.VMEM((256, 128), BF16),
            pltpu.VMEM((128, 128), BF16),
            pltpu.VMEM((3, 3 * R, R, 128), F32),
            pltpu.VMEM((9, R, 3 * R, 128), F32),
            pltpu.VMEM((9, R * R, 128), F32),
            pltpu.VMEM((9, R * R, 128), F32),
            pltpu.VMEM((2, 9, 2, R, 128), F32),
            pltpu.VMEM((2, 9, 2, R, 128), F32),
            pltpu.VMEM((4, 256, 256), BF16),
            pltpu.VMEM((4, 256, 256), BF16),
            pltpu.VMEM((ny, 2, nx, 128), F32),
            pltpu.VMEM((ny, 2, nx, 128), F32),
            pltpu.VMEM((nx, 2, ny, 128), F32),
            pltpu.VMEM((nx, 2, ny, 128), F32),
            pltpu.VMEM((6, half, 128), F32),
            pltpu.VMEM((chunks, 256, 256), BF16),
            pltpu.VMEM((chunks, 256, 256), BF16),
            pltpu.VMEM((chunks, 128, 256), F32),
            pltpu.VMEM((768, 256), BF16),
            pltpu.VMEM((768, 256), BF16),
            pltpu.VMEM((6, half, 128), F32),
            pltpu.VMEM((nx, 3, ny, 128), F32),
            pltpu.VMEM((nx, 3, ny, 128), F32),
            pltpu.VMEM((ny, 3, nx, 128), F32),
            pltpu.VMEM((ny, 3, nx, 128), F32),
            pltpu.VMEM((owners, count), BF16),
            pltpu.VMEM((CAP, count), F32),
            dma((3, 2)), dma((3, 2)),
            dma((9, 2)), dma((9, 2)),
            dma((9, 2)), dma((9, 2)),
            dma((ny,)), dma((ny,)),
            dma((nx,)), dma((nx,)),
            dma((nx,)), dma((nx,)),
            dma((ny,)), dma((ny,)),
            dma((11,)),
        ],
        compiler_params=pltpu.CompilerParams(
            collective_id=0, has_side_effects=True, vmem_limit_bytes=67043328
        ),
    )(
        velocity.reshape(3, R * R, 128),
        owner.reshape(1, count),
        cell_x.reshape(1, count),
        cell_y.reshape(1, count),
        cell_z.reshape(1, count),
        query_weights,
        *tables(velocity.shape[3]),
    )


def solution(mesh):
    sizes = (mesh.shape["gx"], mesh.shape["gy"], mesh.shape["gz"])
    placed = (
        P(None, "gz", "gx", "gy"),
        P(("gx", "gy", "gz"), None),
        P(("gx", "gy", "gz")),
        P(("gx", "gy", "gz")),
        P(("gx", "gy", "gz")),
        P(None, ("gx", "gy", "gz")),
    )
    return jax.shard_map(
        functools.partial(on_device, sizes),
        mesh=mesh,
        in_specs=placed,
        out_specs=P(None, ("gx", "gy", "gz")),
        check_vma=False,
    )
```

```python
import functools

import jax
import jax.numpy as jnp
import numpy as np
from jax import lax
from jax.experimental import pallas as pl
from jax.experimental.pallas import tpu as pltpu
from jax.sharding import PartitionSpec as P

MESH = pl.DeviceIdType.MESH
F32 = jnp.float32
BF16 = jnp.bfloat16
FW = 32
R = FW // 2
CAP = 64
FIELDS = ((0, None), (0, 0), (1, None), (0, 1), (1, 1), (2, None), (0, 2), (1, 2), (2, 2))
PAIRS = ((0, 0), (0, 1), (0, 2), (1, 1), (1, 2), (2, 2))


def taps():
    offsets = np.arange(2 * R + 1).astype(np.float32) - np.float32(R)
    values = np.exp(np.float32(-6.0) * offsets * offsets / np.float32(FW * FW))
    return (values / values.sum(dtype=np.float32)).astype(np.float32)


def split(x):
    hi = x.astype(BF16)
    lo = (x - hi.astype(F32)).astype(BF16)
    return hi, lo


def np_split(x):
    hi = jnp.asarray(x, F32).astype(BF16)
    lo = (jnp.asarray(x, F32) - hi.astype(F32)).astype(BF16)
    return hi, lo


def tables(by):
    g = taps()

    def band(rows, cols, shift):
        m = np.arange(rows)[:, None] - np.arange(cols)[None, :] + shift
        return np.where((m >= 0) & (m <= 2 * R), g[np.clip(m, 0, 2 * R)], np.float32(0))

    sub = band(3 * R, R, 0).T
    mid = band(by, by, R)
    left = band(R, by, 0)
    right = band(R, by, by + R)
    groups = R // 2
    edge = np.zeros((groups // 2, 2 * 128, 2 * by), np.float32)
    for k in range(groups):
        part = edge[k // 2, :, (k % 2) * by : (k % 2 + 1) * by]
        part[R * k : R * k + R] = left
        part[128 + R * k : 128 + R * k + R] = right
    sh, sl = np_split(sub)
    mh, ml = np_split(mid)
    eh, el = np_split(edge)
    return (
        jnp.concatenate([sh, sl, sh], axis=1),
        jnp.concatenate([mh, mh], axis=0),
        ml,
        eh,
        el,
    )


def dot(a, b):
    return jnp.dot(a, b, preferred_element_type=F32)


def kernel(
    sizes,
    v_hbm, own_hbm, cx_hbm, cy_hbm, cz_hbm, qw_hbm, sub_hbm, mid_hbm, midl_hbm, eh_hbm, el_hbm,
    out_ref,
    v_ref, own_ref, cx_ref, cy_ref, cz_ref, qw_ref, sub_ref, mid_ref, midl_ref,
    u, xb, yb, zf, pack, halo, eh, el,
    sendq, gotq, passq, haveq, rows, w1h, w1l, wyb,
    sth, stl, sendr, haver, onehot, rankhot,
    s1, r1, s2, r2, s3, r3, sa, ra, sb, rb, sc, rc, lsem,
):
    nx, ny, nz = sizes
    g = [float(t) for t in taps()]
    mx, my, mz = lax.axis_index("gx"), lax.axis_index("gy"), lax.axis_index("gz")
    par = lax.rem(my, 2)
    owners = nx * ny
    count = own_ref.shape[1]

    def shifted(first, step):
        on_x = par if first else 1 - par
        on_z = 1 - on_x
        return (
            lax.rem(mx + on_x * (step % nx), nx),
            my,
            lax.rem(mz + on_z * (step % nz), nz),
        )

    def y_peer(step):
        return (mx, lax.rem(my + step % ny, ny), mz)

    def x_peer(step):
        return (lax.rem(mx + step % nx, nx), my, mz)

    def remote(src, dst, ssem, rsem, dev):
        return pltpu.make_async_remote_copy(
            src_ref=src, dst_ref=dst, send_sem=ssem, recv_sem=rsem, device_id=dev, device_id_type=MESH
        )

    loads = [
        pltpu.make_async_copy(src, dst, lsem.at[number])
        for number, (src, dst) in enumerate(
            (
                (v_hbm, v_ref),
                (own_hbm, own_ref),
                (cx_hbm, cx_ref),
                (cy_hbm, cy_ref),
                (cz_hbm, cz_ref),
                (qw_hbm, qw_ref),
                (sub_hbm, sub_ref),
                (mid_hbm, mid_ref),
                (midl_hbm, midl_ref),
                (eh_hbm, eh),
                (el_hbm, el),
            )
        )
    ]
    for load in loads:
        load.start()

    barrier = pltpu.get_barrier_semaphore()
    for step in range(1, nx):
        pl.semaphore_signal(barrier, inc=1, device_id=x_peer(step), device_id_type=MESH)
    for step in range(1, ny):
        pl.semaphore_signal(barrier, inc=1, device_id=y_peer(step), device_id_type=MESH)
    for step in (1, nz - 1):
        pl.semaphore_signal(
            barrier, inc=1, device_id=(mx, my, lax.rem(mz + step, nz)), device_id_type=MESH
        )

    loads[0].wait()

    @pl.when(par == 0)
    def _():
        for c in range(3):
            u[c, R : 2 * R] = v_ref[c].reshape(R, R, 128)

    @pl.when(par == 1)
    def _():
        for c in range(3):
            for b in range(R):
                u[c, R + b] = v_ref[c, pl.ds(b, R, stride=R), :]

    pl.semaphore_wait(barrier, nx - 1 + ny - 1 + 2)

    def first_copies(c):
        src = u.at[c, pl.ds(R, R)]
        return (
            remote(src, u.at[c, pl.ds(0, R)], s1.at[c, 0], r1.at[c, 0], shifted(True, 1)),
            remote(src, u.at[c, pl.ds(2 * R, R)], s1.at[c, 1], r1.at[c, 1], shifted(True, -1)),
        )

    def second_copies(f):
        src = xb.at[f, :, pl.ds(R, R)]
        return (
            remote(src, xb.at[f, :, pl.ds(0, R)], s2.at[f, 0], r2.at[f, 0], shifted(False, 1)),
            remote(src, xb.at[f, :, pl.ds(2 * R, R)], s2.at[f, 1], r2.at[f, 1], shifted(False, -1)),
        )

    def y_copies(f):
        return (
            remote(pack.at[0, f], halo.at[1, f], s3.at[f, 0], r3.at[f, 0], y_peer(-1)),
            remote(pack.at[1, f], halo.at[0, f], s3.at[f, 1], r3.at[f, 1], y_peer(1)),
        )

    def exchange(n, peer_of, me, src, dst, place, ssem, rsem):
        copies = []
        for step in range(1, n):
            copies.append(
                remote(
                    src.at[lax.rem(me + step, n)], dst.at[place[step]], ssem.at[step], rsem.at[step], peer_of(step)
                )
            )
        return copies

    far_y = [ny // 2 + m if h == 0 else ny // 2 - 1 - m for m in range(ny // 2) for h in range(2)]
    place_y = [far_y.index(step) for step in range(ny)]

    for c in range(3):
        for copy in first_copies(c):
            copy.start()

    for load in loads[1:6]:
        load.wait()
    bits_y = ny.bit_length() - 1
    own = own_ref[...]
    target = (own & (ny - 1)) * nx + (own >> bits_y)
    hot = (lax.broadcasted_iota(jnp.int32, (owners, count), 0) == target).astype(F32)
    onehot[...] = hot.astype(BF16)
    earlier = (
        lax.broadcasted_iota(jnp.int32, (128, 128), 0) < lax.broadcasted_iota(jnp.int32, (128, 128), 1)
    ).astype(BF16)
    carry = jnp.zeros((owners, 1), F32)
    ranks = []
    for block in range(count // 128):
        part = hot[:, block * 128 : block * 128 + 128]
        before = dot(part.astype(BF16), earlier) + carry
        ranks.append(jnp.sum(part * before, axis=0, keepdims=True))
        carry = carry + jnp.sum(part, axis=1, keepdims=True)
    rank = jnp.concatenate(ranks, axis=1)
    slot = lax.broadcasted_iota(jnp.int32, (CAP, count), 0).astype(F32) == rank
    rankhot[...] = slot.astype(F32)
    cell = (cz_ref[...] * R + cx_ref[...]) * 128 + cy_ref[...]

    def pieces(w):
        p0 = w.astype(BF16).astype(F32)
        p1 = (w - p0).astype(BF16).astype(F32)
        p2 = w - p0 - p1
        return p0, p1, p2

    wx = pieces(qw_ref[0:1, :])
    wy = pieces(qw_ref[1:2, :])
    wz = pieces(qw_ref[2:3, :])
    cell_hi = (cell >> 8).astype(F32)
    cell_lo = (cell & 255).astype(F32)
    zero = jnp.zeros_like(cell_lo)
    order = [
        cell_hi, wx[0], cell_lo, wx[1], zero, wx[2],
        wy[0], wz[0], wy[1], wz[1], wy[2], wz[2],
    ]
    placed = jnp.concatenate(
        [jnp.where(slot, p, jnp.zeros_like(p)).astype(BF16) for p in order], axis=0
    )
    spread = lax.dot_general(
        onehot[...], placed, (((1,), (1,)), ((), ())), preferred_element_type=F32
    )
    lane = lax.broadcasted_iota(jnp.int32, (1, 128), 1)
    scale = jnp.where(lane < CAP, 256.0, 1.0)
    head = spread[:, 0:128] * scale + spread[:, 128:256] + spread[:, 256:384]
    tail = spread[:, 384:512] + spread[:, 512:640] + spread[:, 640:768]
    for j in range(ny):
        sendq[j, 0] = head[j * nx : (j + 1) * nx]
        sendq[j, 1] = tail[j * nx : (j + 1) * nx]
    out_y = exchange(ny, y_peer, my, sendq, gotq, place_y, sa, ra)
    for copy in out_y:
        copy.start()
    gotq[place_y[0]] = sendq[my]

    def first_filter(f):
        i, j = FIELDS[f]

        def chunk(n, _):
            bs = pl.multiple_of((n // 2) * 8, 8)
            h = (n % 2) * 8
            x = u[i, pl.ds(h, 40), pl.ds(bs, 8), :]
            if j is not None:
                x = x * u[j, pl.ds(h, 40), pl.ds(bs, 8), :]
            acc = x[R : R + 8] * g[R]
            for d in range(1, R + 1):
                acc = acc + (x[R - d : R + 8 - d] + x[R + d : R + 8 + d]) * g[R + d]
            xb[f, pl.ds(h, 8), pl.ds(R + bs, 8), :] = acc
            return 0

        lax.fori_loop(0, 4, chunk, 0)
        for copy in second_copies(f):
            copy.start()

    def pass_on():
        for copy in out_y:
            copy.wait_recv()
        for i in range(nx):
            for k in range(2):
                passq[i, k] = gotq[:, k, i, :]
        out_x = exchange(nx, x_peer, mx, passq, haveq, list(range(nx)), sb, rb)
        for copy in out_x:
            copy.start()
        haveq[0] = passq[mx]
        return out_x

    field = 0
    for c in range(3):
        for copy in first_copies(c):
            copy.wait_recv()
        for _ in range(c + 2):
            first_filter(field)
            field += 1
        if c == 0:
            out_x = pass_on()

    for copy in out_x:
        copy.wait_recv()
    half = owners // 2
    tops = [
        jnp.concatenate([haveq[nx // 2 + i, k] for i in range(nx // 2)], axis=0) for k in range(2)
    ]
    bottoms = [
        jnp.concatenate([haveq[nx // 2 - 1 - i, k] for i in range(nx // 2)], axis=0) for k in range(2)
    ]
    low = lane < CAP

    def paired(k, second):
        top, bottom = tops[k], bottoms[k]
        if second:
            return jnp.where(low, pltpu.roll(top, CAP, 1), bottom)
        return jnp.where(low, top, pltpu.roll(bottom, CAP, 1))

    q_cell = paired(0, False).astype(jnp.int32)
    q_wx = paired(0, True)
    q_wy = paired(1, False)
    q_wz = paired(1, True)
    q_cz = (q_cell >> 11).astype(F32)
    q_cx = ((q_cell >> 7) & (R - 1)).astype(F32)
    z_first = par == 0
    rows[0] = jnp.where(z_first, q_cz, q_cx)
    rows[1] = jnp.where(z_first, q_cx, q_cz)
    rows[2] = (q_cell & 127).astype(F32)
    rows[3] = jnp.where(z_first, q_wz, q_wx)
    rows[4] = jnp.where(z_first, q_wx, q_wz)
    rows[5] = q_wy
    chunks = owners * CAP // 256

    def weights(n, _):
        def row(k):
            return jnp.concatenate([rows[k, pl.ds(2 * n, 1), :], rows[k, pl.ds(2 * n + 1, 1), :]], axis=1)

        def hat(size, at, w):
            index = lax.broadcasted_iota(jnp.int32, (size, 256), 0).astype(F32)
            return jnp.where(index == at, 1.0 - w, jnp.where(index == at + 1.0, w, 0.0))

        wa = hat(R, row(0), row(3))
        wb = hat(R, row(1), row(4))
        for a in range(R):
            hi, lo = split(wa[a : a + 1] * wb)
            w1h[n, R * a : R * a + R, :] = hi
            w1l[n, R * a : R * a + R, :] = lo
        wyb[n] = hat(128, row(2), row(5))
        return 0

    lax.fori_loop(0, chunks, weights, 0)

    group = lax.broadcasted_iota(jnp.int32, (1, 128), 1) // R
    for load in loads[6:9]:
        load.wait()

    def second_filter(f, _):
        for copy in second_copies(f):
            copy.wait_recv()

        def pair(n, _):
            x = jnp.concatenate([xb[f, 2 * n], xb[f, 2 * n + 1]], axis=1)
            hi, lo = split(x)
            o = dot(sub_ref[...], jnp.concatenate([hi, hi, lo], axis=0))
            yb[f, pl.ds(pl.multiple_of(32 * n, 32), R), :] = o[:, :128]
            yb[f, pl.ds(pl.multiple_of(32 * n, 32) + R, R), :] = o[:, 128:]
            return 0

        lax.fori_loop(0, R // 2, pair, 0, unroll=True)
        for e in range(2):
            first = jnp.zeros((R, 128), F32)
            last = jnp.zeros((R, 128), F32)
            for k in range(R // 2):
                turned = yb[f, pl.ds(2 * k + e, R, stride=R), :]
                first = jnp.where(group == k, pltpu.roll(turned, R * k, 1) if k else turned, first)
                last = jnp.where(group == k, pltpu.roll(turned, (R * k + R) % 128, 1) if k < 7 else turned, last)
            pack[0, f, e] = first
            pack[1, f, e] = last
        for copy in y_copies(f):
            copy.start()
        hi, lo = split(yb[f])
        zf[f] = dot(jnp.concatenate([hi, lo], axis=1), mid_ref[...]) + dot(hi, midl_ref[...])
        return 0

    lax.fori_loop(0, 9, second_filter, 0)

    for load in loads[9:]:
        load.wait()

    def wait_y(f, _):
        for copy in y_copies(f):
            copy.wait_recv()
        return 0

    lax.fori_loop(0, 9, wait_y, 0)
    edges = jnp.concatenate([halo[0].reshape(9 * 32, 128), halo[1].reshape(9 * 32, 128)], axis=1)
    eg_hi, eg_lo = split(edges)
    for kk in range(R // 4):
        part = dot(eg_hi, eh[kk]) + dot(eg_lo, eh[kk]) + dot(eg_hi, el[kk])
        for k in range(2):
            at = 32 * (2 * kk + k)
            zf[:, at : at + 32, :] += part[:, 128 * k : 128 * k + 128].reshape(9, 32, 128)

    for p, (i, j) in enumerate(PAIRS):
        tau = zf[FIELDS.index((i, j))] - zf[FIELDS.index((i, None))] * zf[FIELDS.index((j, None))]
        hi, lo = split(tau.T)
        sth[128 * p : 128 * p + 128] = hi
        stl[128 * p : 128 * p + 128] = lo

    me = my * nx + mx
    per = ny // 2

    def back(n, h, side):
        step_x = nx // 2 + n // per if side == 0 else nx // 2 - 1 - n // per
        step_y = ny // 2 + lax.rem(n, per) if h == 0 else ny // 2 - 1 - lax.rem(n, per)
        holder = (lax.rem(mx + nx - step_x, nx), lax.rem(my + ny - step_y, ny), mz)
        at = 2 * n + h
        return remote(
            sendr.at[at, side], haver.at[me], sc.at[at, side], rc.at[at, side], holder
        )

    def each_back(n, act):
        for h in range(2):
            for side in range(2):
                if h == 1 and side == 1:

                    @pl.when(n < chunks - 1)
                    def _():
                        act(back(n, 1, 1))

                else:
                    act(back(n, h, side))

    def interpolate(n, _):
        high = w1h[n]
        acc = dot(sth[...], high) + dot(stl[...], high) + dot(sth[...], w1l[n])
        wys = wyb[n]
        v = [
            jnp.sum(acc[128 * p : 128 * p + 128] * wys, axis=0, keepdims=True) for p in range(6)
        ]
        for h in range(2):
            for k in range(3):
                a = v[2 * k][:, 128 * h : 128 * h + 128]
                b = v[2 * k + 1][:, 128 * h : 128 * h + 128]
                sendr[2 * n + h, 0, k : k + 1, :] = jnp.where(low, a, pltpu.roll(b, CAP, 1))
                sendr[2 * n + h, 1, k : k + 1, :] = jnp.where(low, pltpu.roll(a, CAP, 1), b)
        each_back(n, lambda copy: copy.start())
        return 0

    lax.fori_loop(0, chunks, interpolate, 0)
    haver[me] = sendr[half - 1, 1]

    def wait_back(n, _):
        each_back(n, lambda copy: copy.wait_recv())
        return 0

    lax.fori_loop(0, chunks, wait_back, 0)
    pad = jnp.zeros((128 - owners, 128), F32)
    hot_pad = jnp.concatenate([onehot[...], jnp.zeros((128 - owners, count), BF16)], axis=0)
    hot_two = jnp.concatenate([hot_pad, hot_pad], axis=0)
    at_rank = rankhot[...]
    for k in range(3):
        piece = jnp.concatenate([haver[:, k, :], pad], axis=0)
        hi, lo = split(piece.T)
        picked = dot(jnp.concatenate([hi, lo], axis=1), hot_two)
        for h in range(2):
            out_ref[2 * k + h : 2 * k + h + 1, :] = jnp.sum(
                picked[CAP * h : CAP * h + CAP] * at_rank, axis=0, keepdims=True
            )

    for c in range(3):
        for copy in first_copies(c):
            copy.wait_send()

    def wait_sends(f, _):
        for copy in second_copies(f) + y_copies(f):
            copy.wait_send()
        return 0

    lax.fori_loop(0, 9, wait_sends, 0)
    for copy in out_y + out_x:
        copy.wait_send()

    def wait_sent(n, _):
        each_back(n, lambda copy: copy.wait_send())
        return 0

    lax.fori_loop(0, chunks, wait_sent, 0)


def on_device(sizes, velocity, owner, cell_x, cell_y, cell_z, query_weights):
    nx, ny, nz = sizes
    count = owner.shape[0]
    owners = nx * ny
    half = owners // 2
    chunks = owners * CAP // 256
    vmem = pl.BlockSpec(memory_space=pltpu.VMEM)
    hbm = pl.BlockSpec(memory_space=pltpu.HBM)
    row = pltpu.VMEM((1, count), jnp.int32)
    dma = pltpu.SemaphoreType.DMA
    return pl.pallas_call(
        functools.partial(kernel, sizes),
        out_shape=jax.ShapeDtypeStruct((6, count), F32),
        in_specs=[hbm] * 11,
        out_specs=vmem,
        scratch_shapes=[
            pltpu.VMEM((3, R * R, 128), F32),
            row, row, row, row,
            pltpu.VMEM((3, count), F32),
            pltpu.VMEM((R, 9 * R), BF16),
            pltpu.VMEM((256, 128), BF16),
            pltpu.VMEM((128, 128), BF16),
            pltpu.VMEM((3, 3 * R, R, 128), F32),
            pltpu.VMEM((9, R, 3 * R, 128), F32),
            pltpu.VMEM((9, R * R, 128), F32),
            pltpu.VMEM((9, R * R, 128), F32),
            pltpu.VMEM((2, 9, 2, R, 128), F32),
            pltpu.VMEM((2, 9, 2, R, 128), F32),
            pltpu.VMEM((4, 256, 256), BF16),
            pltpu.VMEM((4, 256, 256), BF16),
            pltpu.VMEM((ny, 2, nx, 128), F32),
            pltpu.VMEM((ny, 2, nx, 128), F32),
            pltpu.VMEM((nx, 2, ny, 128), F32),
            pltpu.VMEM((nx, 2, ny, 128), F32),
            pltpu.VMEM((6, half, 128), F32),
            pltpu.VMEM((chunks, 256, 256), BF16),
            pltpu.VMEM((chunks, 256, 256), BF16),
            pltpu.VMEM((chunks, 128, 256), F32),
            pltpu.VMEM((768, 256), BF16),
            pltpu.VMEM((768, 256), BF16),
            pltpu.VMEM((half, 2, 3, 128), F32),
            pltpu.VMEM((owners, 3, 128), F32),
            pltpu.VMEM((owners, count), BF16),
            pltpu.VMEM((CAP, count), F32),
            dma((3, 2)), dma((3, 2)),
            dma((9, 2)), dma((9, 2)),
            dma((9, 2)), dma((9, 2)),
            dma((ny,)), dma((ny,)),
            dma((nx,)), dma((nx,)),
            dma((half, 2)), dma((half, 2)),
            dma((11,)),
        ],
        compiler_params=pltpu.CompilerParams(
            collective_id=0, has_side_effects=True, vmem_limit_bytes=67043328
        ),
    )(
        velocity.reshape(3, R * R, 128),
        owner.reshape(1, count),
        cell_x.reshape(1, count),
        cell_y.reshape(1, count),
        cell_z.reshape(1, count),
        query_weights,
        *tables(velocity.shape[3]),
    )


def solution(mesh):
    sizes = (mesh.shape["gx"], mesh.shape["gy"], mesh.shape["gz"])
    placed = (
        P(None, "gz", "gx", "gy"),
        P(("gx", "gy", "gz"), None),
        P(("gx", "gy", "gz")),
        P(("gx", "gy", "gz")),
        P(("gx", "gy", "gz")),
        P(None, ("gx", "gy", "gz")),
    )
    return jax.shard_map(
        functools.partial(on_device, sizes),
        mesh=mesh,
        in_specs=placed,
        out_specs=P(None, ("gx", "gy", "gz")),
        check_vma=False,
    )
```

```python
import functools

import jax
import jax.numpy as jnp
import numpy as np
from jax import lax
from jax.experimental import pallas as pl
from jax.experimental.pallas import tpu as pltpu
from jax.sharding import PartitionSpec as P

MESH = pl.DeviceIdType.MESH
F32 = jnp.float32
BF16 = jnp.bfloat16
FW = 32
R = FW // 2
CAP = 64
FIELDS = ((0, None), (0, 0), (1, None), (0, 1), (1, 1), (2, None), (0, 2), (1, 2), (2, 2))
PAIRS = ((0, 0), (0, 1), (0, 2), (1, 1), (1, 2), (2, 2))
DONE = ((0, 0), (0, 1), (1, 1), (0, 2), (1, 2), (2, 2))


def taps():
    offsets = np.arange(2 * R + 1).astype(np.float32) - np.float32(R)
    values = np.exp(np.float32(-6.0) * offsets * offsets / np.float32(FW * FW))
    return (values / values.sum(dtype=np.float32)).astype(np.float32)


def split(x):
    hi = x.astype(BF16)
    lo = (x - hi.astype(F32)).astype(BF16)
    return hi, lo


def np_split(x):
    hi = jnp.asarray(x, F32).astype(BF16)
    lo = (jnp.asarray(x, F32) - hi.astype(F32)).astype(BF16)
    return hi, lo


def tables(by):
    g = taps()

    def band(rows, cols, shift):
        m = np.arange(rows)[:, None] - np.arange(cols)[None, :] + shift
        return np.where((m >= 0) & (m <= 2 * R), g[np.clip(m, 0, 2 * R)], np.float32(0))

    sub = band(3 * R, R, 0).T
    mid = band(by, by, R)
    left = band(R, by, 0)
    right = band(R, by, by + R)
    edge = np.zeros((256, 256), np.float32)
    for k in range(R // 2):
        edge[128 + R * k : 128 + R * k + R, 32 * k : 32 * k + R] = right[:, by - R :]
        edge[R * k : R * k + R, 32 * k + R : 32 * k + 32] = left[:, :R]
    sh, sl = np_split(sub)
    mh, ml = np_split(mid)
    eh, el = np_split(edge)
    return (
        jnp.concatenate([sh, sl, sh], axis=1),
        jnp.concatenate([mh, mh], axis=0),
        ml,
        eh,
        el,
    )


def dot(a, b):
    return jnp.dot(a, b, preferred_element_type=F32)


def kernel(
    sizes,
    v_hbm, own_hbm, cx_hbm, cy_hbm, cz_hbm, qw_hbm, sub_hbm, mid_hbm, midl_hbm, eh_hbm, el_hbm,
    out_ref,
    v_ref, own_ref, cx_ref, cy_ref, cz_ref, qw_ref, sub_ref, mid_ref, midl_ref,
    u, xb, yb, zf, pack, halo, eh, el,
    sendq, gotq, passq, haveq, rows, w1, wyb,
    st, vals, sendr, haver, onehot, rankhot,
    s1, r1, s2, r2, s3, r3, sa, ra, sb, rb, sc, rc, lsem,
):
    nx, ny, nz = sizes
    g = [float(t) for t in taps()]
    mx, my, mz = lax.axis_index("gx"), lax.axis_index("gy"), lax.axis_index("gz")
    par = lax.rem(my, 2)
    owners = nx * ny
    count = own_ref.shape[1]

    def shifted(first, step):
        on_x = par if first else 1 - par
        on_z = 1 - on_x
        return (
            lax.rem(mx + on_x * (step % nx), nx),
            my,
            lax.rem(mz + on_z * (step % nz), nz),
        )

    def y_peer(step):
        return (mx, lax.rem(my + step % ny, ny), mz)

    def x_peer(step):
        return (lax.rem(mx + step % nx, nx), my, mz)

    def remote(src, dst, ssem, rsem, dev):
        return pltpu.make_async_remote_copy(
            src_ref=src, dst_ref=dst, send_sem=ssem, recv_sem=rsem, device_id=dev, device_id_type=MESH
        )

    loads = [
        pltpu.make_async_copy(src, dst, lsem.at[number])
        for number, (src, dst) in enumerate(
            (
                (v_hbm, v_ref),
                (own_hbm, own_ref),
                (cx_hbm, cx_ref),
                (cy_hbm, cy_ref),
                (cz_hbm, cz_ref),
                (qw_hbm, qw_ref),
                (sub_hbm, sub_ref),
                (mid_hbm, mid_ref),
                (midl_hbm, midl_ref),
                (eh_hbm, eh),
                (el_hbm, el),
            )
        )
    ]
    for load in loads:
        load.start()

    barrier = pltpu.get_barrier_semaphore()
    for step in range(1, nx):
        pl.semaphore_signal(barrier, inc=1, device_id=x_peer(step), device_id_type=MESH)
    for step in range(1, ny):
        pl.semaphore_signal(barrier, inc=1, device_id=y_peer(step), device_id_type=MESH)
    for step in (1, nz - 1):
        pl.semaphore_signal(
            barrier, inc=1, device_id=(mx, my, lax.rem(mz + step, nz)), device_id_type=MESH
        )

    loads[0].wait()

    @pl.when(par == 0)
    def _():
        for c in range(3):
            u[c, R : 2 * R] = v_ref[c].reshape(R, R, 128)

    @pl.when(par == 1)
    def _():
        for c in range(3):
            for b in range(R):
                u[c, R + b] = v_ref[c, pl.ds(b, R, stride=R), :]

    pl.semaphore_wait(barrier, nx - 1 + ny - 1 + 2)

    def first_copies(c):
        src = u.at[c, pl.ds(R, R)]
        return (
            remote(src, u.at[c, pl.ds(0, R)], s1.at[c, 0], r1.at[c, 0], shifted(True, 1)),
            remote(src, u.at[c, pl.ds(2 * R, R)], s1.at[c, 1], r1.at[c, 1], shifted(True, -1)),
        )

    def second_copies(f):
        src = xb.at[f, :, pl.ds(R, R)]
        return (
            remote(src, xb.at[f, :, pl.ds(0, R)], s2.at[f, 0], r2.at[f, 0], shifted(False, 1)),
            remote(src, xb.at[f, :, pl.ds(2 * R, R)], s2.at[f, 1], r2.at[f, 1], shifted(False, -1)),
        )

    def y_copies(f):
        return (
            remote(pack.at[0, f], halo.at[1, f], s3.at[f, 0], r3.at[f, 0], y_peer(-1)),
            remote(pack.at[1, f], halo.at[0, f], s3.at[f, 1], r3.at[f, 1], y_peer(1)),
        )

    def exchange(n, peer_of, me, src, dst, place, ssem, rsem):
        copies = []
        for step in range(1, n):
            copies.append(
                remote(
                    src.at[lax.rem(me + step, n)], dst.at[place[step]], ssem.at[step], rsem.at[step], peer_of(step)
                )
            )
        return copies

    far_y = [ny // 2 + m if h == 0 else ny // 2 - 1 - m for m in range(ny // 2) for h in range(2)]
    place_y = [far_y.index(step) for step in range(ny)]

    for c in range(3):
        for copy in first_copies(c):
            copy.start()

    for load in loads[1:6]:
        load.wait()
    bits_y = ny.bit_length() - 1
    own = own_ref[...]
    target = (own & (ny - 1)) * nx + (own >> bits_y)
    hot = (lax.broadcasted_iota(jnp.int32, (owners, count), 0) == target).astype(F32)
    onehot[...] = hot.astype(BF16)
    earlier = (
        lax.broadcasted_iota(jnp.int32, (128, 128), 0) < lax.broadcasted_iota(jnp.int32, (128, 128), 1)
    ).astype(BF16)
    carry = jnp.zeros((owners, 1), F32)
    ranks = []
    for block in range(count // 128):
        part = hot[:, block * 128 : block * 128 + 128]
        before = dot(part.astype(BF16), earlier) + carry
        ranks.append(jnp.sum(part * before, axis=0, keepdims=True))
        carry = carry + jnp.sum(part, axis=1, keepdims=True)
    rank = jnp.concatenate(ranks, axis=1)
    slot = lax.broadcasted_iota(jnp.int32, (CAP, count), 0).astype(F32) == rank
    rankhot[...] = slot.astype(F32)
    cell = (cz_ref[...] * R + cx_ref[...]) * 128 + cy_ref[...]

    def pieces(w):
        p0 = w.astype(BF16).astype(F32)
        p1 = (w - p0).astype(BF16).astype(F32)
        p2 = w - p0 - p1
        return p0, p1, p2

    wx = pieces(qw_ref[0:1, :])
    wy = pieces(qw_ref[1:2, :])
    wz = pieces(qw_ref[2:3, :])
    cell_hi = (cell >> 8).astype(F32)
    cell_lo = (cell & 255).astype(F32)
    zero = jnp.zeros_like(cell_lo)
    order = [
        cell_hi, wx[0], cell_lo, wx[1], zero, wx[2],
        wy[0], wz[0], wy[1], wz[1], wy[2], wz[2],
    ]
    placed = jnp.concatenate(
        [jnp.where(slot, p, jnp.zeros_like(p)).astype(BF16) for p in order], axis=0
    )
    spread = lax.dot_general(
        onehot[...], placed, (((1,), (1,)), ((), ())), preferred_element_type=F32
    )
    lane = lax.broadcasted_iota(jnp.int32, (1, 128), 1)
    scale = jnp.where(lane < CAP, 256.0, 1.0)
    head = spread[:, 0:128] * scale + spread[:, 128:256] + spread[:, 256:384]
    tail = spread[:, 384:512] + spread[:, 512:640] + spread[:, 640:768]
    for j in range(ny):
        sendq[j, 0] = head[j * nx : (j + 1) * nx]
        sendq[j, 1] = tail[j * nx : (j + 1) * nx]
    out_y = exchange(ny, y_peer, my, sendq, gotq, place_y, sa, ra)
    for copy in out_y:
        copy.start()
    gotq[place_y[0]] = sendq[my]

    def first_filter(f):
        i, j = FIELDS[f]

        def chunk(n, _):
            bs = pl.multiple_of((n // 2) * 8, 8)
            h = (n % 2) * 8
            x = u[i, pl.ds(h, 40), pl.ds(bs, 8), :]
            if j is not None:
                x = x * u[j, pl.ds(h, 40), pl.ds(bs, 8), :]
            acc = x[R : R + 8] * g[R]
            for d in range(1, R + 1):
                acc = acc + (x[R - d : R + 8 - d] + x[R + d : R + 8 + d]) * g[R + d]
            xb[f, pl.ds(h, 8), pl.ds(R + bs, 8), :] = acc
            return 0

        lax.fori_loop(0, 4, chunk, 0)
        for copy in second_copies(f):
            copy.start()

    def pass_on():
        for copy in out_y:
            copy.wait_recv()
        for i in range(nx):
            for k in range(2):
                passq[i, k] = gotq[:, k, i, :]
        out_x = exchange(nx, x_peer, mx, passq, haveq, list(range(nx)), sb, rb)
        for copy in out_x:
            copy.start()
        haveq[0] = passq[mx]
        return out_x

    field = 0
    for c in range(3):
        for copy in first_copies(c):
            copy.wait_recv()
        for _ in range(c + 2):
            first_filter(field)
            field += 1
        if c == 0:
            out_x = pass_on()

    half = owners // 2
    low = lane < CAP
    chunks = owners * CAP // 256

    def slot_weights():
        for copy in out_x:
            copy.wait_recv()
        tops = [
            jnp.concatenate([haveq[nx // 2 + i, k] for i in range(nx // 2)], axis=0) for k in range(2)
        ]
        bottoms = [
            jnp.concatenate([haveq[nx // 2 - 1 - i, k] for i in range(nx // 2)], axis=0) for k in range(2)
        ]

        def paired(k, second):
            top, bottom = tops[k], bottoms[k]
            if second:
                return jnp.where(low, pltpu.roll(top, CAP, 1), bottom)
            return jnp.where(low, top, pltpu.roll(bottom, CAP, 1))

        q_cell = paired(0, False).astype(jnp.int32)
        q_wx = paired(0, True)
        q_wy = paired(1, False)
        q_wz = paired(1, True)
        q_cz = (q_cell >> 11).astype(F32)
        q_cx = ((q_cell >> 7) & (R - 1)).astype(F32)
        z_first = par == 0
        rows[0] = jnp.where(z_first, q_cz, q_cx)
        rows[1] = jnp.where(z_first, q_cx, q_cz)
        rows[2] = (q_cell & 127).astype(F32)
        rows[3] = jnp.where(z_first, q_wz, q_wx)
        rows[4] = jnp.where(z_first, q_wx, q_wz)
        rows[5] = q_wy

        def weights(n, _):
            def row(k):
                return jnp.concatenate([rows[k, pl.ds(2 * n, 1), :], rows[k, pl.ds(2 * n + 1, 1), :]], axis=1)

            def index(size):
                return lax.broadcasted_iota(jnp.int32, (size, 256), 0).astype(F32)

            def eighth(x):
                return jnp.floor(x * 256.0 + 0.5) * (1.0 / 256.0)

            ca, cb, cy = row(0), row(1), row(2)
            wa, wb, wy = eighth(row(3)), eighth(row(4)), row(5)
            both = eighth(wa * wb)
            ib = index(R)
            lower, upper = ib == cb, ib == cb + 1.0
            near = jnp.where(lower, 1.0 - wa - wb + both, jnp.where(upper, wb - both, 0.0))
            far = jnp.where(lower, wa - both, jnp.where(upper, both, 0.0))
            for a in range(R):
                part = jnp.where(ca == float(a), near, jnp.where(ca == float(a - 1), far, 0.0))
                w1[n, R * a : R * a + R, :] = part.astype(BF16)
            iy = index(128)
            wyb[n] = jnp.where(iy == cy, 1.0 - wy, jnp.where(iy == cy + 1.0, wy, 0.0))
            return 0

        lax.fori_loop(0, chunks, weights, 0)

    group = lane // R
    for load in loads[6:]:
        load.wait()

    def second_filter(f, _):
        for copy in second_copies(f):
            copy.wait_recv()

        def pair(n, _):
            x = jnp.concatenate([xb[f, 2 * n], xb[f, 2 * n + 1]], axis=1)
            hi, lo = split(x)
            o = dot(sub_ref[...], jnp.concatenate([hi, hi, lo], axis=0))
            yb[f, pl.ds(pl.multiple_of(32 * n, 32), R), :] = o[:, :128]
            yb[f, pl.ds(pl.multiple_of(32 * n, 32) + R, R), :] = o[:, 128:]
            return 0

        lax.fori_loop(0, R // 2, pair, 0, unroll=True)
        for e in range(2):
            first = jnp.zeros((R, 128), F32)
            last = jnp.zeros((R, 128), F32)
            for k in range(R // 2):
                turned = yb[f, pl.ds(2 * k + e, R, stride=R), :]
                first = jnp.where(group == k, pltpu.roll(turned, R * k, 1) if k else turned, first)
                last = jnp.where(group == k, pltpu.roll(turned, (R * k + R) % 128, 1) if k < 7 else turned, last)
            pack[0, f, e] = first
            pack[1, f, e] = last
        for copy in y_copies(f):
            copy.start()
        hi, lo = split(yb[f])
        zf[f] = dot(jnp.concatenate([hi, lo], axis=1), mid_ref[...]) + dot(hi, midl_ref[...])
        return 0

    rim = (lane >= 128 - R) | (lane < R)

    def finish(first, end):
        def wait_y(f, _):
            for copy in y_copies(f):
                copy.wait_recv()
            return 0

        lax.fori_loop(first, end, wait_y, 0)
        n = end - first
        edges = jnp.concatenate(
            [halo[side, first:end].reshape(32 * n, 128) for side in range(2)], axis=1
        )
        hi, lo = split(edges)
        part = dot(hi, eh[...]) + dot(lo, eh[...]) + dot(hi, el[...])
        for k in range(R // 2):
            q, r = k // 4, k % 4
            turned = pltpu.roll(part[:, 128 * q : 128 * q + 128], (128 - R - 32 * r) % 128, 1)
            zf[first:end, 32 * k : 32 * k + 32, :] += jnp.where(rim, turned, 0.0).reshape(n, 32, 128)

    def stress(first, end):
        for d in range(first, end):
            i, j = DONE[d]
            tau = zf[FIELDS.index((i, j))] - zf[FIELDS.index((i, None))] * zf[FIELDS.index((j, None))]
            hi, lo = split(tau.T)
            st[d, :128] = hi
            st[d, 128:] = lo

    def at_queries(n, first, end):
        acc = dot(st[first:end].reshape(256 * (end - first), 256), w1[n])
        wys = wyb[n]
        found = []
        for d in range(end - first):
            both = acc[256 * d : 256 * d + 128] + acc[256 * d + 128 : 256 * d + 256]
            found.append(jnp.sum(both * wys, axis=0, keepdims=True))
        return found

    block = min(4, chunks)

    def interpolate(first, end, number):
        for n in range(block):
            n = block * number + n
            for d, v in enumerate(at_queries(n, first, end)):
                p = PAIRS.index(DONE[first + d])
                vals[p, pl.ds(2 * n, 1), :] = v[:, :128]
                vals[p, pl.ds(2 * n + 1, 1), :] = v[:, 128:]

    def interpolate_early(start, stop):
        def step(number, _):
            interpolate(0, 3, number)
            return 0

        lax.fori_loop(start, stop, step, 0)

    me = my * nx + mx
    per = ny // 2

    def back(n, h, side):
        step_x = nx // 2 + n // per if side == 0 else nx // 2 - 1 - n // per
        step_y = ny // 2 + lax.rem(n, per) if h == 0 else ny // 2 - 1 - lax.rem(n, per)
        holder = (lax.rem(mx + nx - step_x, nx), lax.rem(my + ny - step_y, ny), mz)
        at = 2 * n + h
        return remote(
            sendr.at[at, side], haver.at[me], sc.at[at, side], rc.at[at, side], holder
        )

    def each_back(n, act):
        for h in range(2):
            for side in range(2):
                if h == 1 and side == 1:

                    @pl.when(n < chunks - 1)
                    def _():
                        act(back(n, 1, 1))

                else:
                    act(back(n, h, side))

    def send_back(number, _):
        interpolate(3, 6, number)

        def send(n, _):
            for h in range(2):
                at = 2 * n + h
                for k in range(3):
                    a, b = vals[2 * k, pl.ds(at, 1), :], vals[2 * k + 1, pl.ds(at, 1), :]
                    sendr[at, 0, k : k + 1, :] = jnp.where(low, a, pltpu.roll(b, CAP, 1))
                    sendr[at, 1, k : k + 1, :] = jnp.where(low, pltpu.roll(a, CAP, 1), b)
            each_back(n, lambda copy: copy.start())
            return 0

        lax.fori_loop(block * number, block * number + block, send, 0)
        return 0

    def second_filters(first, end):
        lax.fori_loop(first, end, second_filter, 0)

    second_filters(0, 3)
    slot_weights()
    second_filters(3, 6)
    finish(0, 5)
    stress(0, 3)
    interpolate_early(0, chunks // block // 2)
    second_filters(6, 9)
    interpolate_early(chunks // block // 2, chunks // block)
    finish(5, 9)
    stress(3, 6)
    lax.fori_loop(0, chunks // block, send_back, 0)
    haver[me] = sendr[half - 1, 1]

    def wait_back(n, _):
        each_back(n, lambda copy: copy.wait_recv())
        return 0

    lax.fori_loop(0, chunks, wait_back, 0)
    pad = jnp.zeros((128 - owners, 128), F32)
    hot_pad = jnp.concatenate([onehot[...], jnp.zeros((128 - owners, count), BF16)], axis=0)
    hot_two = jnp.concatenate([hot_pad, hot_pad], axis=0)
    at_rank = rankhot[...]
    for k in range(3):
        piece = jnp.concatenate([haver[:, k, :], pad], axis=0)
        hi, lo = split(piece.T)
        picked = dot(jnp.concatenate([hi, lo], axis=1), hot_two)
        for h in range(2):
            out_ref[2 * k + h : 2 * k + h + 1, :] = jnp.sum(
                picked[CAP * h : CAP * h + CAP] * at_rank, axis=0, keepdims=True
            )

    for c in range(3):
        for copy in first_copies(c):
            copy.wait_send()

    def wait_sends(f, _):
        for copy in second_copies(f) + y_copies(f):
            copy.wait_send()
        return 0

    lax.fori_loop(0, 9, wait_sends, 0)
    for copy in out_y + out_x:
        copy.wait_send()

    def wait_sent(n, _):
        each_back(n, lambda copy: copy.wait_send())
        return 0

    lax.fori_loop(0, chunks, wait_sent, 0)


def on_device(sizes, velocity, owner, cell_x, cell_y, cell_z, query_weights):
    nx, ny, nz = sizes
    count = owner.shape[0]
    owners = nx * ny
    half = owners // 2
    chunks = owners * CAP // 256
    vmem = pl.BlockSpec(memory_space=pltpu.VMEM)
    hbm = pl.BlockSpec(memory_space=pltpu.HBM)
    row = pltpu.VMEM((1, count), jnp.int32)
    dma = pltpu.SemaphoreType.DMA
    return pl.pallas_call(
        functools.partial(kernel, sizes),
        out_shape=jax.ShapeDtypeStruct((6, count), F32),
        in_specs=[hbm] * 11,
        out_specs=vmem,
        scratch_shapes=[
            pltpu.VMEM((3, R * R, 128), F32),
            row, row, row, row,
            pltpu.VMEM((3, count), F32),
            pltpu.VMEM((R, 9 * R), BF16),
            pltpu.VMEM((256, 128), BF16),
            pltpu.VMEM((128, 128), BF16),
            pltpu.VMEM((3, 3 * R, R, 128), F32),
            pltpu.VMEM((9, R, 3 * R, 128), F32),
            pltpu.VMEM((9, R * R, 128), F32),
            pltpu.VMEM((9, R * R, 128), F32),
            pltpu.VMEM((2, 9, 2, R, 128), F32),
            pltpu.VMEM((2, 9, 2, R, 128), F32),
            pltpu.VMEM((256, 256), BF16),
            pltpu.VMEM((256, 256), BF16),
            pltpu.VMEM((ny, 2, nx, 128), F32),
            pltpu.VMEM((ny, 2, nx, 128), F32),
            pltpu.VMEM((nx, 2, ny, 128), F32),
            pltpu.VMEM((nx, 2, ny, 128), F32),
            pltpu.VMEM((6, half, 128), F32),
            pltpu.VMEM((chunks, 256, 256), BF16),
            pltpu.VMEM((chunks, 128, 256), F32),
            pltpu.VMEM((6, 256, 256), BF16),
            pltpu.VMEM((6, half, 128), F32),
            pltpu.VMEM((half, 2, 3, 128), F32),
            pltpu.VMEM((owners, 3, 128), F32),
            pltpu.VMEM((owners, count), BF16),
            pltpu.VMEM((CAP, count), F32),
            dma((3, 2)), dma((3, 2)),
            dma((9, 2)), dma((9, 2)),
            dma((9, 2)), dma((9, 2)),
            dma((ny,)), dma((ny,)),
            dma((nx,)), dma((nx,)),
            dma((half, 2)), dma((half, 2)),
            dma((11,)),
        ],
        compiler_params=pltpu.CompilerParams(
            collective_id=0, has_side_effects=True, vmem_limit_bytes=67043328
        ),
    )(
        velocity.reshape(3, R * R, 128),
        owner.reshape(1, count),
        cell_x.reshape(1, count),
        cell_y.reshape(1, count),
        cell_z.reshape(1, count),
        query_weights,
        *tables(velocity.shape[3]),
    )


def solution(mesh):
    sizes = (mesh.shape["gx"], mesh.shape["gy"], mesh.shape["gz"])
    placed = (
        P(None, "gz", "gx", "gy"),
        P(("gx", "gy", "gz"), None),
        P(("gx", "gy", "gz")),
        P(("gx", "gy", "gz")),
        P(("gx", "gy", "gz")),
        P(None, ("gx", "gy", "gz")),
    )
    return jax.shard_map(
        functools.partial(on_device, sizes),
        mesh=mesh,
        in_specs=placed,
        out_specs=P(None, ("gx", "gy", "gz")),
        check_vma=False,
    )
```

```python
import functools

import jax
import jax.numpy as jnp
import numpy as np
from jax import lax
from jax.experimental import pallas as pl
from jax.experimental.pallas import tpu as pltpu
from jax.sharding import PartitionSpec as P

MESH = pl.DeviceIdType.MESH
F32 = jnp.float32
BF16 = jnp.bfloat16
FW = 32
R = FW // 2
CAP = 64
FIELDS = ((0, None), (0, 0), (1, None), (0, 1), (1, 1), (2, None), (0, 2), (1, 2), (2, 2))
PAIRS = ((0, 0), (0, 1), (0, 2), (1, 1), (1, 2), (2, 2))
DONE = ((0, 0), (0, 1), (1, 1), (0, 2), (1, 2), (2, 2))


def taps():
    offsets = np.arange(2 * R + 1).astype(np.float32) - np.float32(R)
    values = np.exp(np.float32(-6.0) * offsets * offsets / np.float32(FW * FW))
    return (values / values.sum(dtype=np.float32)).astype(np.float32)


def split(x):
    hi = x.astype(BF16)
    lo = (x - hi.astype(F32)).astype(BF16)
    return hi, lo


def np_split(x):
    hi = jnp.asarray(x, F32).astype(BF16)
    lo = (jnp.asarray(x, F32) - hi.astype(F32)).astype(BF16)
    return hi, lo


def tables(by):
    g = taps()

    def band(rows, cols, shift):
        m = np.arange(rows)[:, None] - np.arange(cols)[None, :] + shift
        return np.where((m >= 0) & (m <= 2 * R), g[np.clip(m, 0, 2 * R)], np.float32(0))

    sub = band(3 * R, R, 0).T
    mid = band(by, by, R)
    left = band(R, by, 0)
    right = band(R, by, by + R)
    edge = np.zeros((256, 256), np.float32)
    for k in range(R // 2):
        edge[128 + R * k : 128 + R * k + R, 32 * k : 32 * k + R] = right[:, by - R :]
        edge[R * k : R * k + R, 32 * k + R : 32 * k + 32] = left[:, :R]
    sh, sl = np_split(sub)
    mh, ml = np_split(mid)
    eh, el = np_split(edge)
    return (
        jnp.concatenate([sh, sl, sh], axis=1),
        jnp.concatenate([mh, mh], axis=0),
        ml,
        eh,
        el,
    )


def dot(a, b):
    return jnp.dot(a, b, preferred_element_type=F32)


def kernel(
    sizes,
    v_hbm, own_hbm, cx_hbm, cy_hbm, cz_hbm, qw_hbm, sub_hbm, mid_hbm, midl_hbm, eh_hbm, el_hbm,
    out_ref,
    v_ref, own_ref, cx_ref, cy_ref, cz_ref, qw_ref, sub_ref, mid_ref, midl_ref,
    u, xb, yb, zf, pack, halo, eh, el,
    sendq, gotq, passq, haveq, rows, w1, wyb,
    st, vals, sendr, haver, onehot, rankhot,
    s1, r1, s2, r2, s3, r3, sa, ra, sb, rb, sc, rc, lsem, token,
):
    nx, ny, nz = sizes
    g = [float(t) for t in taps()]
    mx, my, mz = lax.axis_index("gx"), lax.axis_index("gy"), lax.axis_index("gz")
    par = lax.rem(my, 2)
    owners = nx * ny
    count = own_ref.shape[1]

    def shifted(first, step):
        on_x = par if first else 1 - par
        on_z = 1 - on_x
        return (
            lax.rem(mx + on_x * (step % nx), nx),
            my,
            lax.rem(mz + on_z * (step % nz), nz),
        )

    def y_peer(step):
        return (mx, lax.rem(my + step % ny, ny), mz)

    def x_peer(step):
        return (lax.rem(mx + step % nx, nx), my, mz)

    def remote(src, dst, ssem, rsem, dev):
        return pltpu.make_async_remote_copy(
            src_ref=src, dst_ref=dst, send_sem=ssem, recv_sem=rsem, device_id=dev, device_id_type=MESH
        )

    loads = [
        pltpu.make_async_copy(src, dst, lsem.at[number])
        for number, (src, dst) in enumerate(
            (
                (v_hbm.at[0], v_ref.at[0]),
                (v_hbm.at[1], v_ref.at[1]),
                (v_hbm.at[2], v_ref.at[2]),
                (own_hbm, own_ref),
                (cx_hbm, cx_ref),
                (cy_hbm, cy_ref),
                (cz_hbm, cz_ref),
                (qw_hbm, qw_ref),
                (sub_hbm, sub_ref),
                (mid_hbm, mid_ref),
                (midl_hbm, midl_ref),
                (eh_hbm, eh),
                (el_hbm, el),
            )
        )
    ]
    for load in loads:
        load.start()

    barrier = pltpu.get_barrier_semaphore()
    near = (x_peer(1), x_peer(-1), y_peer(1), y_peer(-1))
    for peer in near + ((mx, my, lax.rem(mz + 1, nz)), (mx, my, lax.rem(mz + nz - 1, nz))):
        pl.semaphore_signal(barrier, inc=1, device_id=peer, device_id_type=MESH)

    rounds = max(nx, ny) // 2 - 1

    def tell(r):
        for peer in near:
            pl.semaphore_signal(token.at[r], inc=1, device_id=peer, device_id_type=MESH)

    def hear(r):
        pl.semaphore_wait(token.at[r], len(near))

    def first_copies(c):
        src = u.at[c, pl.ds(R, R)]
        return (
            remote(src, u.at[c, pl.ds(0, R)], s1.at[c, 0], r1.at[c, 0], shifted(True, 1)),
            remote(src, u.at[c, pl.ds(2 * R, R)], s1.at[c, 1], r1.at[c, 1], shifted(True, -1)),
        )

    def second_copies(f):
        src = xb.at[f, :, pl.ds(R, R)]
        return (
            remote(src, xb.at[f, :, pl.ds(0, R)], s2.at[f, 0], r2.at[f, 0], shifted(False, 1)),
            remote(src, xb.at[f, :, pl.ds(2 * R, R)], s2.at[f, 1], r2.at[f, 1], shifted(False, -1)),
        )

    def y_copies(f):
        return (
            remote(pack.at[0, f], halo.at[1, f], s3.at[f, 0], r3.at[f, 0], y_peer(-1)),
            remote(pack.at[1, f], halo.at[0, f], s3.at[f, 1], r3.at[f, 1], y_peer(1)),
        )

    def exchange(n, peer_of, me, src, dst, place, ssem, rsem):
        copies = []
        for step in range(1, n):
            copies.append(
                remote(
                    src.at[lax.rem(me + step, n)], dst.at[place[step]], ssem.at[step], rsem.at[step], peer_of(step)
                )
            )
        return copies

    far_x = [nx // 2 + m if h == 0 else nx // 2 - 1 - m for m in range(nx // 2) for h in range(2)]
    place_x = [far_x.index(step) for step in range(nx)]
    order_y = [ny // 2 + i for i in range(ny // 2)] + [ny // 2 - 1 - i for i in range(ny // 2)]
    place_y = [order_y.index(step) for step in range(ny)]

    for c in range(3):
        loads[c].wait()

        @pl.when(par == 0)
        def _():
            u[c, R : 2 * R] = v_ref[c].reshape(R, R, 128)

        @pl.when(par == 1)
        def _():
            for b in range(R):
                u[c, R + b] = v_ref[c, pl.ds(b, R, stride=R), :]

        if c == 0:
            pl.semaphore_wait(barrier, len(near) + 2)
            if rounds:
                tell(0)
        for copy in first_copies(c):
            copy.start()

    for load in loads[3:8]:
        load.wait()
    hot = (lax.broadcasted_iota(jnp.int32, (owners, count), 0) == own_ref[...]).astype(F32)
    onehot[...] = hot.astype(BF16)
    earlier = (
        lax.broadcasted_iota(jnp.int32, (128, 128), 0) < lax.broadcasted_iota(jnp.int32, (128, 128), 1)
    ).astype(BF16)
    carry = jnp.zeros((owners, 1), F32)
    ranks = []
    for block in range(count // 128):
        part = hot[:, block * 128 : block * 128 + 128]
        before = dot(part.astype(BF16), earlier) + carry
        ranks.append(jnp.sum(part * before, axis=0, keepdims=True))
        carry = carry + jnp.sum(part, axis=1, keepdims=True)
    rank = jnp.concatenate(ranks, axis=1)
    slot = lax.broadcasted_iota(jnp.int32, (CAP, count), 0).astype(F32) == rank
    rankhot[...] = slot.astype(F32)
    cell = (cz_ref[...] * R + cx_ref[...]) * 128 + cy_ref[...]

    def pieces(w):
        p0 = w.astype(BF16).astype(F32)
        p1 = (w - p0).astype(BF16).astype(F32)
        p2 = w - p0 - p1
        return p0, p1, p2

    wx = pieces(qw_ref[0:1, :])
    wy = pieces(qw_ref[1:2, :])
    wz = pieces(qw_ref[2:3, :])
    cell_hi = (cell >> 8).astype(F32)
    cell_lo = (cell & 255).astype(F32)
    zero = jnp.zeros_like(cell_lo)
    order = [
        cell_hi, wx[0], cell_lo, wx[1], zero, wx[2],
        wy[0], wz[0], wy[1], wz[1], wy[2], wz[2],
    ]
    placed = jnp.concatenate(
        [jnp.where(slot, p, jnp.zeros_like(p)).astype(BF16) for p in order], axis=0
    )
    spread = lax.dot_general(
        onehot[...], placed, (((1,), (1,)), ((), ())), preferred_element_type=F32
    )
    lane = lax.broadcasted_iota(jnp.int32, (1, 128), 1)
    scale = jnp.where(lane < CAP, 256.0, 1.0)
    head = spread[:, 0:128] * scale + spread[:, 128:256] + spread[:, 256:384]
    tail = spread[:, 384:512] + spread[:, 512:640] + spread[:, 640:768]
    for i in range(nx):
        sendq[i, 0] = head[i * ny : (i + 1) * ny]
        sendq[i, 1] = tail[i * ny : (i + 1) * ny]
    out_x = exchange(nx, x_peer, mx, sendq, gotq, place_x, sa, ra)
    gotq[place_x[0]] = sendq[mx]
    if rounds:
        hear(0)
    if rounds > 1:
        tell(1)

    def first_filter(f):
        i, j = FIELDS[f]

        def chunk(n, _):
            bs = pl.multiple_of((n // 2) * 8, 8)
            h = (n % 2) * 8
            x = u[i, pl.ds(h, 40), pl.ds(bs, 8), :]
            if j is not None:
                x = x * u[j, pl.ds(h, 40), pl.ds(bs, 8), :]
            acc = x[R : R + 8] * g[R]
            for d in range(1, R + 1):
                acc = acc + (x[R - d : R + 8 - d] + x[R + d : R + 8 + d]) * g[R + d]
            xb[f, pl.ds(h, 8), pl.ds(R + bs, 8), :] = acc
            return 0

        lax.fori_loop(0, 4, chunk, 0)
        for copy in second_copies(f):
            copy.start()

    field = 0
    for c in range(3):
        for copy in first_copies(c):
            copy.wait_recv()
        for _ in range(c + 2):
            if field == 0:
                for r in range(1, rounds - 1):
                    hear(r)
                    tell(r + 1)
            first_filter(field)
            if field == 0:
                if rounds > 1:
                    hear(rounds - 1)
                for copy in out_x:
                    copy.start()
            field += 1

    for copy in out_x:
        copy.wait_recv()
    for j in range(ny):
        for k in range(2):
            passq[j, k] = gotq[:, k, j, :]
    out_y = exchange(ny, y_peer, my, passq, haveq, place_y, sb, rb)
    for copy in out_y:
        copy.start()
    haveq[place_y[0]] = passq[my]

    half = owners // 2
    low = lane < CAP
    chunks = owners * CAP // 256

    def slot_weights():
        for copy in out_y:
            copy.wait_recv()
        def table(k, start):
            return jnp.concatenate(
                [haveq[start : start + ny // 2, k, i, :] for i in range(nx)], axis=0
            )

        tops = [table(k, 0) for k in range(2)]
        bottoms = [table(k, ny // 2) for k in range(2)]

        def paired(k, second):
            top, bottom = tops[k], bottoms[k]
            if second:
                return jnp.where(low, pltpu.roll(top, CAP, 1), bottom)
            return jnp.where(low, top, pltpu.roll(bottom, CAP, 1))

        q_cell = paired(0, False).astype(jnp.int32)
        q_wx = paired(0, True)
        q_wy = paired(1, False)
        q_wz = paired(1, True)
        q_cz = (q_cell >> 11).astype(F32)
        q_cx = ((q_cell >> 7) & (R - 1)).astype(F32)
        z_first = par == 0
        rows[0] = jnp.where(z_first, q_cz, q_cx)
        rows[1] = jnp.where(z_first, q_cx, q_cz)
        rows[2] = (q_cell & 127).astype(F32)
        rows[3] = jnp.where(z_first, q_wz, q_wx)
        rows[4] = jnp.where(z_first, q_wx, q_wz)
        rows[5] = q_wy

        def weights(n, _):
            def row(k):
                return jnp.concatenate([rows[k, pl.ds(2 * n, 1), :], rows[k, pl.ds(2 * n + 1, 1), :]], axis=1)

            def index(size):
                return lax.broadcasted_iota(jnp.int32, (size, 256), 0).astype(F32)

            def eighth(x):
                return jnp.floor(x * 256.0 + 0.5) * (1.0 / 256.0)

            ca, cb, cy = row(0), row(1), row(2)
            wa, wb, wy = eighth(row(3)), eighth(row(4)), row(5)
            both = eighth(wa * wb)
            ib = index(R)
            lower, upper = ib == cb, ib == cb + 1.0
            near = jnp.where(lower, 1.0 - wa - wb + both, jnp.where(upper, wb - both, 0.0))
            far = jnp.where(lower, wa - both, jnp.where(upper, both, 0.0))
            for a in range(R):
                part = jnp.where(ca == float(a), near, jnp.where(ca == float(a - 1), far, 0.0))
                w1[n, R * a : R * a + R, :] = part.astype(BF16)
            iy = index(128)
            wyb[n] = jnp.where(iy == cy, 1.0 - wy, jnp.where(iy == cy + 1.0, wy, 0.0))
            return 0

        lax.fori_loop(0, chunks, weights, 0)

    group = lane // R
    for load in loads[8:]:
        load.wait()

    def second_filter(f, _):
        for copy in second_copies(f):
            copy.wait_recv()

        def pair(n, _):
            x = jnp.concatenate([xb[f, 2 * n], xb[f, 2 * n + 1]], axis=1)
            hi, lo = split(x)
            o = dot(sub_ref[...], jnp.concatenate([hi, hi, lo], axis=0))
            yb[f, pl.ds(pl.multiple_of(32 * n, 32), R), :] = o[:, :128]
            yb[f, pl.ds(pl.multiple_of(32 * n, 32) + R, R), :] = o[:, 128:]
            return 0

        lax.fori_loop(0, R // 2, pair, 0, unroll=True)
        for e in range(2):
            first = jnp.zeros((R, 128), F32)
            last = jnp.zeros((R, 128), F32)
            for k in range(R // 2):
                turned = yb[f, pl.ds(2 * k + e, R, stride=R), :]
                first = jnp.where(group == k, pltpu.roll(turned, R * k, 1) if k else turned, first)
                last = jnp.where(group == k, pltpu.roll(turned, (R * k + R) % 128, 1) if k < 7 else turned, last)
            pack[0, f, e] = first
            pack[1, f, e] = last
        for copy in y_copies(f):
            copy.start()
        hi, lo = split(yb[f])
        zf[f] = dot(jnp.concatenate([hi, lo], axis=1), mid_ref[...]) + dot(hi, midl_ref[...])
        return 0

    rim = (lane >= 128 - R) | (lane < R)

    def finish(first, end):
        def wait_y(f, _):
            for copy in y_copies(f):
                copy.wait_recv()
            return 0

        lax.fori_loop(first, end, wait_y, 0)
        n = end - first
        edges = jnp.concatenate(
            [halo[side, first:end].reshape(32 * n, 128) for side in range(2)], axis=1
        )
        hi, lo = split(edges)
        part = dot(hi, eh[...]) + dot(lo, eh[...]) + dot(hi, el[...])
        for k in range(R // 2):
            q, r = k // 4, k % 4
            turned = pltpu.roll(part[:, 128 * q : 128 * q + 128], (128 - R - 32 * r) % 128, 1)
            zf[first:end, 32 * k : 32 * k + 32, :] += jnp.where(rim, turned, 0.0).reshape(n, 32, 128)

    def stress(first, end):
        for d in range(first, end):
            i, j = DONE[d]
            tau = zf[FIELDS.index((i, j))] - zf[FIELDS.index((i, None))] * zf[FIELDS.index((j, None))]
            hi, lo = split(tau.T)
            st[d, :128] = hi
            st[d, 128:] = lo

    def at_queries(n, first, end):
        acc = dot(st[first:end].reshape(256 * (end - first), 256), w1[n])
        wys = wyb[n]
        found = []
        for d in range(end - first):
            both = acc[256 * d : 256 * d + 128] + acc[256 * d + 128 : 256 * d + 256]
            found.append(jnp.sum(both * wys, axis=0, keepdims=True))
        return found

    block = min(4, chunks)

    def interpolate(first, end, number):
        for n in range(block):
            n = block * number + n
            for d, v in enumerate(at_queries(n, first, end)):
                p = PAIRS.index(DONE[first + d])
                vals[p, pl.ds(2 * n, 1), :] = v[:, :128]
                vals[p, pl.ds(2 * n + 1, 1), :] = v[:, 128:]

    def interpolate_early(start, stop):
        def step(number, _):
            interpolate(0, 3, number)
            return 0

        lax.fori_loop(start, stop, step, 0)

    me = mx * ny + my
    per = ny // 2

    def back(n, h, side):
        at = 2 * n + h
        x, y = at // per, lax.rem(at, per)
        step_x = nx // 2 + (1 - 2 * lax.rem(x, 2)) * ((x + 1) // 2)
        step_y = ny // 2 + y if side == 0 else ny // 2 - 1 - y
        holder = (lax.rem(mx + nx - step_x, nx), lax.rem(my + ny - step_y, ny), mz)
        return remote(
            sendr.at[at, side], haver.at[me], sc.at[at, side], rc.at[at, side], holder
        )

    def each_back(n, act):
        for h in range(2):
            for side in range(2):
                if h == 1 and side == 1:

                    @pl.when(n < chunks - 1)
                    def _():
                        act(back(n, 1, 1))

                else:
                    act(back(n, h, side))

    def send_back(number, _):
        interpolate(3, 6, number)

        def send(n, _):
            for h in range(2):
                at = 2 * n + h
                for k in range(3):
                    a, b = vals[2 * k, pl.ds(at, 1), :], vals[2 * k + 1, pl.ds(at, 1), :]
                    sendr[at, 0, k : k + 1, :] = jnp.where(low, a, pltpu.roll(b, CAP, 1))
                    sendr[at, 1, k : k + 1, :] = jnp.where(low, pltpu.roll(a, CAP, 1), b)
            each_back(n, lambda copy: copy.start())
            return 0

        lax.fori_loop(block * number, block * number + block, send, 0)
        return 0

    def second_filters(first, end):
        lax.fori_loop(first, end, second_filter, 0)

    second_filters(0, 5)
    slot_weights()
    second_filters(5, 6)
    finish(0, 5)
    stress(0, 3)
    interpolate_early(0, chunks // block // 2)
    second_filters(6, 9)
    interpolate_early(chunks // block // 2, chunks // block)
    finish(5, 9)
    stress(3, 6)
    lax.fori_loop(0, chunks // block, send_back, 0)
    haver[me] = sendr[half - 1, 1]

    for c in range(3):
        for copy in first_copies(c):
            copy.wait_send()

    def wait_sends(f, _):
        for copy in second_copies(f) + y_copies(f):
            copy.wait_send()
        return 0

    lax.fori_loop(0, 9, wait_sends, 0)
    for copy in out_y + out_x:
        copy.wait_send()

    def wait_sent(n, _):
        each_back(n, lambda copy: copy.wait_send())
        return 0

    lax.fori_loop(0, chunks, wait_sent, 0)

    def wait_back(n, _):
        each_back(n, lambda copy: copy.wait_recv())
        return 0

    lax.fori_loop(0, chunks, wait_back, 0)
    pad = jnp.zeros((128 - owners, 128), F32)
    hot_pad = jnp.concatenate([onehot[...], jnp.zeros((128 - owners, count), BF16)], axis=0)
    hot_two = jnp.concatenate([hot_pad, hot_pad], axis=0)
    at_rank = rankhot[...]
    for k in range(3):
        piece = jnp.concatenate([haver[:, k, :], pad], axis=0)
        hi, lo = split(piece.T)
        picked = dot(jnp.concatenate([hi, lo], axis=1), hot_two)
        for h in range(2):
            out_ref[2 * k + h : 2 * k + h + 1, :] = jnp.sum(
                picked[CAP * h : CAP * h + CAP] * at_rank, axis=0, keepdims=True
            )


def on_device(sizes, velocity, owner, cell_x, cell_y, cell_z, query_weights):
    nx, ny, nz = sizes
    count = owner.shape[0]
    owners = nx * ny
    half = owners // 2
    chunks = owners * CAP // 256
    vmem = pl.BlockSpec(memory_space=pltpu.VMEM)
    hbm = pl.BlockSpec(memory_space=pltpu.HBM)
    row = pltpu.VMEM((1, count), jnp.int32)
    dma = pltpu.SemaphoreType.DMA
    return pl.pallas_call(
        functools.partial(kernel, sizes),
        out_shape=jax.ShapeDtypeStruct((6, count), F32),
        in_specs=[hbm] * 11,
        out_specs=vmem,
        scratch_shapes=[
            pltpu.VMEM((3, R * R, 128), F32),
            row, row, row, row,
            pltpu.VMEM((3, count), F32),
            pltpu.VMEM((R, 9 * R), BF16),
            pltpu.VMEM((256, 128), BF16),
            pltpu.VMEM((128, 128), BF16),
            pltpu.VMEM((3, 3 * R, R, 128), F32),
            pltpu.VMEM((9, R, 3 * R, 128), F32),
            pltpu.VMEM((9, R * R, 128), F32),
            pltpu.VMEM((9, R * R, 128), F32),
            pltpu.VMEM((2, 9, 2, R, 128), F32),
            pltpu.VMEM((2, 9, 2, R, 128), F32),
            pltpu.VMEM((256, 256), BF16),
            pltpu.VMEM((256, 256), BF16),
            pltpu.VMEM((nx, 2, ny, 128), F32),
            pltpu.VMEM((nx, 2, ny, 128), F32),
            pltpu.VMEM((ny, 2, nx, 128), F32),
            pltpu.VMEM((ny, 2, nx, 128), F32),
            pltpu.VMEM((6, half, 128), F32),
            pltpu.VMEM((chunks, 256, 256), BF16),
            pltpu.VMEM((chunks, 128, 256), F32),
            pltpu.VMEM((6, 256, 256), BF16),
            pltpu.VMEM((6, half, 128), F32),
            pltpu.VMEM((half, 2, 3, 128), F32),
            pltpu.VMEM((owners, 3, 128), F32),
            pltpu.VMEM((owners, count), BF16),
            pltpu.VMEM((CAP, count), F32),
            dma((3, 2)), dma((3, 2)),
            dma((9, 2)), dma((9, 2)),
            dma((9, 2)), dma((9, 2)),
            dma((nx,)), dma((nx,)),
            dma((ny,)), dma((ny,)),
            dma((half, 2)), dma((half, 2)),
            dma((13,)),
            pltpu.SemaphoreType.REGULAR((max(1, max(nx, ny) // 2 - 1),)),
        ],
        compiler_params=pltpu.CompilerParams(
            collective_id=0, has_side_effects=True, vmem_limit_bytes=40 * 1024 * 1024
        ),
    )(
        *[
            pltpu.with_memory_space_constraint(x, pltpu.HBM)
            for x in (
                velocity.reshape(3, R * R, 128),
                owner.reshape(1, count),
                cell_x.reshape(1, count),
                cell_y.reshape(1, count),
                cell_z.reshape(1, count),
                query_weights,
                *tables(velocity.shape[3]),
            )
        ]
    )


def solution(mesh):
    sizes = (mesh.shape["gx"], mesh.shape["gy"], mesh.shape["gz"])
    placed = (
        P(None, "gz", "gx", "gy"),
        P(("gx", "gy", "gz"), None),
        P(("gx", "gy", "gz")),
        P(("gx", "gy", "gz")),
        P(("gx", "gy", "gz")),
        P(None, ("gx", "gy", "gz")),
    )
    return jax.shard_map(
        functools.partial(on_device, sizes),
        mesh=mesh,
        in_specs=placed,
        out_specs=P(None, ("gx", "gy", "gz")),
        check_vma=False,
    )
```

```python
import functools

import jax
import jax.numpy as jnp
import numpy as np
from jax import lax
from jax.experimental import pallas as pl
from jax.experimental.pallas import tpu as pltpu
from jax.sharding import PartitionSpec as P

MESH = pl.DeviceIdType.MESH
F32 = jnp.float32
BF16 = jnp.bfloat16
FW = 32
R = FW // 2
CAP = 64
FIELDS = ((0, None), (0, 0), (1, None), (0, 1), (1, 1), (2, None), (0, 2), (1, 2), (2, 2))
PAIRS = ((0, 0), (0, 1), (0, 2), (1, 1), (1, 2), (2, 2))
DONE = ((0, 0), (0, 1), (1, 1), (0, 2), (1, 2), (2, 2))


def taps():
    offsets = np.arange(2 * R + 1).astype(np.float32) - np.float32(R)
    values = np.exp(np.float32(-6.0) * offsets * offsets / np.float32(FW * FW))
    return (values / values.sum(dtype=np.float32)).astype(np.float32)


def split(x):
    hi = x.astype(BF16)
    lo = (x - hi.astype(F32)).astype(BF16)
    return hi, lo


def np_split(x):
    hi = jnp.asarray(x, F32).astype(BF16)
    lo = (jnp.asarray(x, F32) - hi.astype(F32)).astype(BF16)
    return hi, lo


def tables(by):
    g = taps()

    def band(rows, cols, shift):
        m = np.arange(rows)[:, None] - np.arange(cols)[None, :] + shift
        return np.where((m >= 0) & (m <= 2 * R), g[np.clip(m, 0, 2 * R)], np.float32(0))

    sub = band(3 * R, R, 0).T
    mid = band(by, by, R)
    left = band(R, by, 0)
    right = band(R, by, by + R)
    edge = np.zeros((256, 256), np.float32)
    for k in range(R // 2):
        edge[128 + R * k : 128 + R * k + R, 32 * k : 32 * k + R] = right[:, by - R :]
        edge[R * k : R * k + R, 32 * k + R : 32 * k + 32] = left[:, :R]
    sh, sl = np_split(sub)
    mh, ml = np_split(mid)
    eh, el = np_split(edge)
    return (
        jnp.concatenate([sh, sl, sh], axis=1),
        jnp.concatenate([mh, mh], axis=0),
        ml,
        eh,
        el,
    )


def dot(a, b):
    return jnp.dot(a, b, preferred_element_type=F32)


def kernel(
    sizes,
    v_hbm, own_hbm, cx_hbm, cy_hbm, cz_hbm, qw_hbm, sub_hbm, mid_hbm, midl_hbm, eh_hbm, el_hbm,
    out_ref,
    v_ref, own_ref, cx_ref, cy_ref, cz_ref, qw_ref, sub_ref, mid_ref, midl_ref,
    u, xb, yb, zf, pack, halo, eh, el,
    sendq, gotq, passq, haveq, rows, w1, wyb,
    st, vals, sendr, haver, onehot, rankhot,
    s1, r1, s2, r2, s3, r3, sa, ra, sb, rb, sc, rc, lsem, token,
):
    nx, ny, nz = sizes
    g = [float(t) for t in taps()]
    mx, my, mz = lax.axis_index("gx"), lax.axis_index("gy"), lax.axis_index("gz")
    par = lax.rem(my, 2)
    owners = nx * ny
    count = own_ref.shape[1]

    def shifted(first, step):
        on_x = par if first else 1 - par
        on_z = 1 - on_x
        return (
            lax.rem(mx + on_x * (step % nx), nx),
            my,
            lax.rem(mz + on_z * (step % nz), nz),
        )

    def y_peer(step):
        return (mx, lax.rem(my + step % ny, ny), mz)

    def x_peer(step):
        return (lax.rem(mx + step % nx, nx), my, mz)

    def remote(src, dst, ssem, rsem, dev):
        return pltpu.make_async_remote_copy(
            src_ref=src, dst_ref=dst, send_sem=ssem, recv_sem=rsem, device_id=dev, device_id_type=MESH
        )

    loads = [
        pltpu.make_async_copy(src, dst, lsem.at[number])
        for number, (src, dst) in enumerate(
            (
                (v_hbm.at[0], v_ref.at[0]),
                (v_hbm.at[1], v_ref.at[1]),
                (v_hbm.at[2], v_ref.at[2]),
                (own_hbm, own_ref),
                (cx_hbm, cx_ref),
                (cy_hbm, cy_ref),
                (cz_hbm, cz_ref),
                (qw_hbm, qw_ref),
                (sub_hbm, sub_ref),
                (mid_hbm, mid_ref),
                (midl_hbm, midl_ref),
                (eh_hbm, eh),
                (el_hbm, el),
            )
        )
    ]
    for load in loads:
        load.start()

    barrier = pltpu.get_barrier_semaphore()
    near = (x_peer(1), x_peer(-1), y_peer(1), y_peer(-1))
    for peer in near + ((mx, my, lax.rem(mz + 1, nz)), (mx, my, lax.rem(mz + nz - 1, nz))):
        pl.semaphore_signal(barrier, inc=1, device_id=peer, device_id_type=MESH)

    rounds = max(nx, ny) // 2 - 1

    def tell(r):
        for peer in near:
            pl.semaphore_signal(token.at[r], inc=1, device_id=peer, device_id_type=MESH)

    def hear(r):
        pl.semaphore_wait(token.at[r], len(near))

    def first_copies(c):
        src = u.at[c, pl.ds(R, R)]
        return (
            remote(src, u.at[c, pl.ds(0, R)], s1.at[c, 0], r1.at[c, 0], shifted(True, 1)),
            remote(src, u.at[c, pl.ds(2 * R, R)], s1.at[c, 1], r1.at[c, 1], shifted(True, -1)),
        )

    def second_copies(f):
        src = xb.at[f, :, pl.ds(R, R)]
        return (
            remote(src, xb.at[f, :, pl.ds(0, R)], s2.at[f, 0], r2.at[f, 0], shifted(False, 1)),
            remote(src, xb.at[f, :, pl.ds(2 * R, R)], s2.at[f, 1], r2.at[f, 1], shifted(False, -1)),
        )

    def y_copies(f):
        return (
            remote(pack.at[0, f], halo.at[1, f], s3.at[f, 0], r3.at[f, 0], y_peer(-1)),
            remote(pack.at[1, f], halo.at[0, f], s3.at[f, 1], r3.at[f, 1], y_peer(1)),
        )

    def exchange(n, peer_of, me, src, dst, place, ssem, rsem):
        copies = []
        for step in range(1, n):
            copies.append(
                remote(
                    src.at[lax.rem(me + step, n)], dst.at[place[step]], ssem.at[step], rsem.at[step], peer_of(step)
                )
            )
        return copies

    far_x = [nx // 2 + m if h == 0 else nx // 2 - 1 - m for m in range(nx // 2) for h in range(2)]
    place_x = [far_x.index(step) for step in range(nx)]
    order_y = [ny // 2 + i for i in range(ny // 2)] + [ny // 2 - 1 - i for i in range(ny // 2)]
    place_y = [order_y.index(step) for step in range(ny)]

    for c in range(3):
        loads[c].wait()

        @pl.when(par == 0)
        def _():
            u[c, R : 2 * R] = v_ref[c].reshape(R, R, 128)

        @pl.when(par == 1)
        def _():
            for b in range(R):
                u[c, R + b] = v_ref[c, pl.ds(b, R, stride=R), :]

        if c == 0:
            pl.semaphore_wait(barrier, len(near) + 2)
            if rounds:
                tell(0)
        for copy in first_copies(c):
            copy.start()

    for load in loads[3:8]:
        load.wait()
    hot = (lax.broadcasted_iota(jnp.int32, (owners, count), 0) == own_ref[...]).astype(F32)
    onehot[...] = hot.astype(BF16)
    earlier = (
        lax.broadcasted_iota(jnp.int32, (128, 128), 0) < lax.broadcasted_iota(jnp.int32, (128, 128), 1)
    ).astype(BF16)
    carry = jnp.zeros((owners, 1), F32)
    ranks = []
    for block in range(count // 128):
        part = hot[:, block * 128 : block * 128 + 128]
        before = dot(part.astype(BF16), earlier) + carry
        ranks.append(jnp.sum(part * before, axis=0, keepdims=True))
        carry = carry + jnp.sum(part, axis=1, keepdims=True)
    rank = jnp.concatenate(ranks, axis=1)
    slot = lax.broadcasted_iota(jnp.int32, (CAP, count), 0).astype(F32) == rank
    rankhot[...] = slot.astype(F32)
    cell = (cz_ref[...] * R + cx_ref[...]) * 128 + cy_ref[...]

    def pieces(w):
        p0 = w.astype(BF16).astype(F32)
        p1 = (w - p0).astype(BF16).astype(F32)
        p2 = w - p0 - p1
        return p0, p1, p2

    wx = pieces(qw_ref[0:1, :])
    wy = pieces(qw_ref[1:2, :])
    wz = pieces(qw_ref[2:3, :])
    cell_hi = (cell >> 8).astype(F32)
    cell_lo = (cell & 255).astype(F32)
    zero = jnp.zeros_like(cell_lo)
    order = [
        cell_hi, wx[0], cell_lo, wx[1], zero, wx[2],
        wy[0], wz[0], wy[1], wz[1], wy[2], wz[2],
    ]
    placed = jnp.concatenate(
        [jnp.where(slot, p, jnp.zeros_like(p)).astype(BF16) for p in order], axis=0
    )
    spread = lax.dot_general(
        onehot[...], placed, (((1,), (1,)), ((), ())), preferred_element_type=F32
    )
    lane = lax.broadcasted_iota(jnp.int32, (1, 128), 1)
    scale = jnp.where(lane < CAP, 256.0, 1.0)
    head = spread[:, 0:128] * scale + spread[:, 128:256] + spread[:, 256:384]
    tail = spread[:, 384:512] + spread[:, 512:640] + spread[:, 640:768]
    for i in range(nx):
        sendq[i, 0] = head[i * ny : (i + 1) * ny]
        sendq[i, 1] = tail[i * ny : (i + 1) * ny]
    out_x = exchange(nx, x_peer, mx, sendq, gotq, place_x, sa, ra)
    gotq[place_x[0]] = sendq[mx]
    if rounds:
        hear(0)
    if rounds > 1:
        tell(1)

    def first_filter(f):
        i, j = FIELDS[f]

        def chunk(n, _):
            bs = pl.multiple_of((n // 2) * 8, 8)
            h = (n % 2) * 8
            x = u[i, pl.ds(h, 40), pl.ds(bs, 8), :]
            if j is not None:
                x = x * u[j, pl.ds(h, 40), pl.ds(bs, 8), :]
            acc = x[R : R + 8] * g[R]
            for d in range(1, R + 1):
                acc = acc + (x[R - d : R + 8 - d] + x[R + d : R + 8 + d]) * g[R + d]
            xb[f, pl.ds(h, 8), pl.ds(R + bs, 8), :] = acc
            return 0

        lax.fori_loop(0, 4, chunk, 0)
        for copy in second_copies(f):
            copy.start()

    field = 0
    for c in range(3):
        for copy in first_copies(c):
            copy.wait_recv()
        for _ in range(c + 2):
            if field == 0:
                for r in range(1, rounds - 1):
                    hear(r)
                    tell(r + 1)
            first_filter(field)
            if field == 0:
                if rounds > 1:
                    hear(rounds - 1)
                for copy in out_x:
                    copy.start()
            field += 1

    for copy in out_x:
        copy.wait_recv()
    for j in range(ny):
        for k in range(2):
            passq[j, k] = gotq[:, k, j, :]
    out_y = exchange(ny, y_peer, my, passq, haveq, place_y, sb, rb)
    for copy in out_y:
        copy.start()
    haveq[place_y[0]] = passq[my]

    half = owners // 2
    low = lane < CAP
    chunks = owners * CAP // 256

    def slot_weights():
        for copy in out_y:
            copy.wait_recv()
        def table(k, start):
            return jnp.concatenate(
                [haveq[start : start + ny // 2, k, i, :] for i in range(nx)], axis=0
            )

        tops = [table(k, 0) for k in range(2)]
        bottoms = [table(k, ny // 2) for k in range(2)]

        def paired(k, second):
            top, bottom = tops[k], bottoms[k]
            if second:
                return jnp.where(low, pltpu.roll(top, CAP, 1), bottom)
            return jnp.where(low, top, pltpu.roll(bottom, CAP, 1))

        q_cell = paired(0, False).astype(jnp.int32)
        q_wx = paired(0, True)
        q_wy = paired(1, False)
        q_wz = paired(1, True)
        q_cz = (q_cell >> 11).astype(F32)
        q_cx = ((q_cell >> 7) & (R - 1)).astype(F32)
        z_first = par == 0
        rows[0] = jnp.where(z_first, q_cz, q_cx)
        rows[1] = jnp.where(z_first, q_cx, q_cz)
        rows[2] = (q_cell & 127).astype(F32)
        rows[3] = jnp.where(z_first, q_wz, q_wx)
        rows[4] = jnp.where(z_first, q_wx, q_wz)
        rows[5] = q_wy

        def weights(n, _):
            def row(k):
                return jnp.concatenate([rows[k, pl.ds(2 * n, 1), :], rows[k, pl.ds(2 * n + 1, 1), :]], axis=1)

            def index(size):
                return lax.broadcasted_iota(jnp.int32, (size, 256), 0).astype(F32)

            def eighth(x):
                return jnp.floor(x * 256.0 + 0.5) * (1.0 / 256.0)

            ca, cb, cy = row(0), row(1), row(2)
            wa, wb, wy = eighth(row(3)), eighth(row(4)), row(5)
            both = eighth(wa * wb)
            ib = index(R)
            lower, upper = ib == cb, ib == cb + 1.0
            near = jnp.where(lower, 1.0 - wa - wb + both, jnp.where(upper, wb - both, 0.0))
            far = jnp.where(lower, wa - both, jnp.where(upper, both, 0.0))
            for a in range(R):
                part = jnp.where(ca == float(a), near, jnp.where(ca == float(a - 1), far, 0.0))
                w1[n, R * a : R * a + R, :] = part.astype(BF16)
            iy = index(128)
            wyb[n] = jnp.where(iy == cy, 1.0 - wy, jnp.where(iy == cy + 1.0, wy, 0.0))
            return 0

        lax.fori_loop(0, chunks, weights, 0)

    group = lane // R
    for load in loads[8:]:
        load.wait()

    def second_filter(f, _):
        for copy in second_copies(f):
            copy.wait_recv()

        def pair(n, _):
            x = jnp.concatenate([xb[f, 2 * n], xb[f, 2 * n + 1]], axis=1)
            hi, lo = split(x)
            o = dot(sub_ref[...], jnp.concatenate([hi, hi, lo], axis=0))
            yb[f, pl.ds(pl.multiple_of(32 * n, 32), R), :] = o[:, :128]
            yb[f, pl.ds(pl.multiple_of(32 * n, 32) + R, R), :] = o[:, 128:]
            return 0

        lax.fori_loop(0, R // 2, pair, 0, unroll=True)
        for e in range(2):
            first = jnp.zeros((R, 128), F32)
            last = jnp.zeros((R, 128), F32)
            for k in range(R // 2):
                turned = yb[f, pl.ds(2 * k + e, R, stride=R), :]
                first = jnp.where(group == k, pltpu.roll(turned, R * k, 1) if k else turned, first)
                last = jnp.where(group == k, pltpu.roll(turned, (R * k + R) % 128, 1) if k < 7 else turned, last)
            pack[0, f, e] = first
            pack[1, f, e] = last
        for copy in y_copies(f):
            copy.start()
        hi, lo = split(yb[f])
        zf[f] = dot(jnp.concatenate([hi, lo], axis=1), mid_ref[...]) + dot(hi, midl_ref[...])
        return 0

    rim = (lane >= 128 - R) | (lane < R)

    def finish(first, end):
        def wait_y(f, _):
            for copy in y_copies(f):
                copy.wait_recv()
            return 0

        lax.fori_loop(first, end, wait_y, 0)
        n = end - first
        edges = jnp.concatenate(
            [halo[side, first:end].reshape(32 * n, 128) for side in range(2)], axis=1
        )
        hi, lo = split(edges)
        part = dot(hi, eh[...]) + dot(lo, eh[...]) + dot(hi, el[...])
        for k in range(R // 2):
            q, r = k // 4, k % 4
            turned = pltpu.roll(part[:, 128 * q : 128 * q + 128], (128 - R - 32 * r) % 128, 1)
            zf[first:end, 32 * k : 32 * k + 32, :] += jnp.where(rim, turned, 0.0).reshape(n, 32, 128)

    def stress(first, end):
        for d in range(first, end):
            i, j = DONE[d]
            tau = zf[FIELDS.index((i, j))] - zf[FIELDS.index((i, None))] * zf[FIELDS.index((j, None))]
            hi, lo = split(tau.T)
            st[d, :128] = hi
            st[d, 128:] = lo

    def at_queries(n, first, end):
        acc = dot(st[first:end].reshape(256 * (end - first), 256), w1[n])
        wys = wyb[n]
        found = []
        for d in range(end - first):
            both = acc[256 * d : 256 * d + 128] + acc[256 * d + 128 : 256 * d + 256]
            found.append(jnp.sum(both * wys, axis=0, keepdims=True))
        return found

    block = min(4, chunks)

    def pack_row(at, k, a, b):
        sendr[at, 0, k : k + 1, :] = jnp.where(low, a, pltpu.roll(b, CAP, 1))
        sendr[at, 1, k : k + 1, :] = jnp.where(low, pltpu.roll(a, CAP, 1), b)

    def interpolate(first, end, number):
        for n in range(block):
            n = block * number + n
            found = at_queries(n, first, end)
            for h in range(2):
                at = 2 * n + h
                v = [w[:, 128 * h : 128 * h + 128] for w in found]
                if first == 0:
                    pack_row(at, 0, v[0], v[1])
                    vals[pl.ds(at, 1), :] = v[2]
                else:
                    pack_row(at, 1, vals[pl.ds(at, 1), :], v[0])
                    pack_row(at, 2, v[1], v[2])

    def interpolate_early(start, stop):
        def step(number, _):
            interpolate(0, 3, number)
            return 0

        lax.fori_loop(start, stop, step, 0)

    me = mx * ny + my
    per = ny // 2

    def back(n, h, side):
        at = 2 * n + h
        x, y = at // per, lax.rem(at, per)
        step_x = nx // 2 + (1 - 2 * lax.rem(x, 2)) * ((x + 1) // 2)
        step_y = ny // 2 + y if side == 0 else ny // 2 - 1 - y
        holder = (lax.rem(mx + nx - step_x, nx), lax.rem(my + ny - step_y, ny), mz)
        return remote(
            sendr.at[at, side], haver.at[me], sc.at[at, side], rc.at[at, side], holder
        )

    def each_back(n, act):
        for h in range(2):
            for side in range(2):
                if h == 1 and side == 1:

                    @pl.when(n < chunks - 1)
                    def _():
                        act(back(n, 1, 1))

                else:
                    act(back(n, h, side))

    def send_back(number, _):
        interpolate(3, 6, number)

        def send(n, _):
            each_back(n, lambda copy: copy.start())
            return 0

        lax.fori_loop(block * number, block * number + block, send, 0)
        return 0

    def second_filters(first, end):
        lax.fori_loop(first, end, second_filter, 0)

    second_filters(0, 6)
    slot_weights()
    finish(0, 5)
    stress(0, 3)
    second_filters(6, 9)
    interpolate_early(0, chunks // block)
    finish(5, 9)
    stress(3, 6)
    lax.fori_loop(0, chunks // block, send_back, 0)
    haver[me] = sendr[half - 1, 1]

    for c in range(3):
        for copy in first_copies(c):
            copy.wait_send()

    def wait_sends(f, _):
        for copy in second_copies(f) + y_copies(f):
            copy.wait_send()
        return 0

    lax.fori_loop(0, 9, wait_sends, 0)
    for copy in out_y + out_x:
        copy.wait_send()

    def wait_sent(n, _):
        each_back(n, lambda copy: copy.wait_send())
        return 0

    lax.fori_loop(0, chunks, wait_sent, 0)

    def wait_back(n, _):
        each_back(n, lambda copy: copy.wait_recv())
        return 0

    lax.fori_loop(0, chunks, wait_back, 0)
    hot_two = jnp.concatenate([onehot[...], onehot[...]], axis=0)
    at_rank = rankhot[...]
    for k in range(3):
        piece = haver[:, k, :]
        hi = piece.astype(BF16).astype(F32)
        both = jnp.concatenate([hi, piece - hi], axis=0).T.astype(BF16)
        picked = dot(both, hot_two)
        for h in range(2):
            p = PAIRS.index(DONE[2 * k + h])
            out_ref[p : p + 1, :] = jnp.sum(
                picked[CAP * h : CAP * h + CAP] * at_rank, axis=0, keepdims=True
            )


def on_device(sizes, velocity, owner, cell_x, cell_y, cell_z, query_weights):
    nx, ny, nz = sizes
    count = owner.shape[0]
    owners = nx * ny
    half = owners // 2
    chunks = owners * CAP // 256
    vmem = pl.BlockSpec(memory_space=pltpu.VMEM)
    hbm = pl.BlockSpec(memory_space=pltpu.HBM)
    row = pltpu.VMEM((1, count), jnp.int32)
    dma = pltpu.SemaphoreType.DMA
    return pl.pallas_call(
        functools.partial(kernel, sizes),
        out_shape=jax.ShapeDtypeStruct((6, count), F32),
        in_specs=[hbm] * 11,
        out_specs=vmem,
        scratch_shapes=[
            pltpu.VMEM((3, R * R, 128), F32),
            row, row, row, row,
            pltpu.VMEM((3, count), F32),
            pltpu.VMEM((R, 9 * R), BF16),
            pltpu.VMEM((256, 128), BF16),
            pltpu.VMEM((128, 128), BF16),
            pltpu.VMEM((3, 3 * R, R, 128), F32),
            pltpu.VMEM((9, R, 3 * R, 128), F32),
            pltpu.VMEM((9, R * R, 128), F32),
            pltpu.VMEM((9, R * R, 128), F32),
            pltpu.VMEM((2, 9, 2, R, 128), F32),
            pltpu.VMEM((2, 9, 2, R, 128), F32),
            pltpu.VMEM((256, 256), BF16),
            pltpu.VMEM((256, 256), BF16),
            pltpu.VMEM((nx, 2, ny, 128), F32),
            pltpu.VMEM((nx, 2, ny, 128), F32),
            pltpu.VMEM((ny, 2, nx, 128), F32),
            pltpu.VMEM((ny, 2, nx, 128), F32),
            pltpu.VMEM((6, half, 128), F32),
            pltpu.VMEM((chunks, 256, 256), BF16),
            pltpu.VMEM((chunks, 128, 256), F32),
            pltpu.VMEM((6, 256, 256), BF16),
            pltpu.VMEM((half, 128), F32),
            pltpu.VMEM((half, 2, 3, 128), F32),
            pltpu.VMEM((owners, 3, 128), F32),
            pltpu.VMEM((owners, count), BF16),
            pltpu.VMEM((CAP, count), F32),
            dma((3, 2)), dma((3, 2)),
            dma((9, 2)), dma((9, 2)),
            dma((9, 2)), dma((9, 2)),
            dma((nx,)), dma((nx,)),
            dma((ny,)), dma((ny,)),
            dma((half, 2)), dma((half, 2)),
            dma((13,)),
            pltpu.SemaphoreType.REGULAR((max(1, max(nx, ny) // 2 - 1),)),
        ],
        compiler_params=pltpu.CompilerParams(
            collective_id=0, has_side_effects=True, vmem_limit_bytes=40 * 1024 * 1024
        ),
    )(
        *[
            pltpu.with_memory_space_constraint(x, pltpu.HBM)
            for x in (
                velocity.reshape(3, R * R, 128),
                owner.reshape(1, count),
                cell_x.reshape(1, count),
                cell_y.reshape(1, count),
                cell_z.reshape(1, count),
                query_weights,
                *tables(velocity.shape[3]),
            )
        ]
    )


def solution(mesh):
    sizes = (mesh.shape["gx"], mesh.shape["gy"], mesh.shape["gz"])
    placed = (
        P(None, "gz", "gx", "gy"),
        P(("gx", "gy", "gz"), None),
        P(("gx", "gy", "gz")),
        P(("gx", "gy", "gz")),
        P(("gx", "gy", "gz")),
        P(None, ("gx", "gy", "gz")),
    )
    return jax.shard_map(
        functools.partial(on_device, sizes),
        mesh=mesh,
        in_specs=placed,
        out_specs=P(None, ("gx", "gy", "gz")),
        check_vma=False,
    )
```

```python
import functools

import jax
import jax.numpy as jnp
import numpy as np
from jax import lax
from jax.experimental import pallas as pl
from jax.experimental.pallas import tpu as pltpu
from jax.sharding import PartitionSpec as P

MESH = pl.DeviceIdType.MESH
F32 = jnp.float32
BF16 = jnp.bfloat16
FW = 32
R = FW // 2
CAP = 64
FIELDS = ((0, None), (0, 0), (1, None), (0, 1), (1, 1), (2, None), (0, 2), (1, 2), (2, 2))
PAIRS = ((0, 0), (0, 1), (0, 2), (1, 1), (1, 2), (2, 2))
DONE = ((0, 0), (0, 1), (1, 1), (0, 2), (1, 2), (2, 2))


def taps():
    offsets = np.arange(2 * R + 1).astype(np.float32) - np.float32(R)
    values = np.exp(np.float32(-6.0) * offsets * offsets / np.float32(FW * FW))
    return (values / values.sum(dtype=np.float32)).astype(np.float32)


def split(x):
    hi = x.astype(BF16)
    lo = (x - hi.astype(F32)).astype(BF16)
    return hi, lo


def np_split(x):
    hi = jnp.asarray(x, F32).astype(BF16)
    lo = (jnp.asarray(x, F32) - hi.astype(F32)).astype(BF16)
    return hi, lo


def tables(by):
    g = taps()

    def band(rows, cols, shift):
        m = np.arange(rows)[:, None] - np.arange(cols)[None, :] + shift
        return np.where((m >= 0) & (m <= 2 * R), g[np.clip(m, 0, 2 * R)], np.float32(0))

    sub = band(3 * R, R, 0).T
    mid = band(by, by, R)
    left = band(R, by, 0)
    right = band(R, by, by + R)
    edge = np.zeros((256, 256), np.float32)
    for k in range(R // 2):
        edge[128 + R * k : 128 + R * k + R, 32 * k : 32 * k + R] = right[:, by - R :]
        edge[R * k : R * k + R, 32 * k + R : 32 * k + 32] = left[:, :R]
    sh, sl = np_split(sub)
    mh, ml = np_split(mid)
    eh, el = np_split(edge)
    return (
        jnp.concatenate([sh, sl, sh], axis=1),
        jnp.concatenate([mh, mh], axis=0),
        ml,
        eh,
        el,
    )


def dot(a, b):
    return jnp.dot(a, b, preferred_element_type=F32)


def kernel(
    sizes,
    v_hbm, own_hbm, cx_hbm, cy_hbm, cz_hbm, qw_hbm, sub_hbm, mid_hbm, midl_hbm, eh_hbm, el_hbm,
    out_ref,
    v_ref, own_ref, cx_ref, cy_ref, cz_ref, qw_ref, sub_ref, mid_ref, midl_ref,
    u, xb, yb, zf, pack, halo, eh, el,
    sendq, gotq, passq, haveq, rows, w1, wyb,
    st, vals, sendr, haver, onehot, rankhot,
    s1, r1, s2, r2, s3, r3, sa, ra, sb, rb, sc, rc, lsem, token, clear,
):
    nx, ny, nz = sizes
    g = [float(t) for t in taps()]
    mx, my, mz = lax.axis_index("gx"), lax.axis_index("gy"), lax.axis_index("gz")
    par = lax.rem(my, 2)
    owners = nx * ny
    count = own_ref.shape[1]

    def shifted(first, step):
        on_x = par if first else 1 - par
        on_z = 1 - on_x
        return (
            lax.rem(mx + on_x * (step % nx), nx),
            my,
            lax.rem(mz + on_z * (step % nz), nz),
        )

    def y_peer(step):
        return (mx, lax.rem(my + ny + step, ny), mz)

    def x_peer(step):
        return (lax.rem(mx + step % nx, nx), my, mz)

    def remote(src, dst, ssem, rsem, dev):
        return pltpu.make_async_remote_copy(
            src_ref=src, dst_ref=dst, send_sem=ssem, recv_sem=rsem, device_id=dev, device_id_type=MESH
        )

    loads = [
        pltpu.make_async_copy(src, dst, lsem.at[number])
        for number, (src, dst) in enumerate(
            (
                (v_hbm.at[0], v_ref.at[0]),
                (v_hbm.at[1], v_ref.at[1]),
                (v_hbm.at[2], v_ref.at[2]),
                (own_hbm, own_ref),
                (cx_hbm, cx_ref),
                (cy_hbm, cy_ref),
                (cz_hbm, cz_ref),
                (qw_hbm, qw_ref),
                (sub_hbm, sub_ref),
                (mid_hbm, mid_ref),
                (midl_hbm, midl_ref),
                (eh_hbm, eh),
                (el_hbm, el),
            )
        )
    ]
    for load in loads:
        load.start()

    barrier = pltpu.get_barrier_semaphore()
    near = (x_peer(1), x_peer(-1), y_peer(1), y_peer(-1))
    for peer in near + ((mx, my, lax.rem(mz + 1, nz)), (mx, my, lax.rem(mz + nz - 1, nz))):
        pl.semaphore_signal(barrier, inc=1, device_id=peer, device_id_type=MESH)

    rounds = max(nx, ny) // 2 - 1

    def tell(r):
        for peer in near:
            pl.semaphore_signal(token.at[r], inc=1, device_id=peer, device_id_type=MESH)

    def hear(r):
        pl.semaphore_wait(token.at[r], len(near))

    def first_copies(c):
        src = u.at[c, pl.ds(R, R)]
        return (
            remote(src, u.at[c, pl.ds(0, R)], s1.at[c, 0], r1.at[c, 0], shifted(True, 1)),
            remote(src, u.at[c, pl.ds(2 * R, R)], s1.at[c, 1], r1.at[c, 1], shifted(True, -1)),
        )

    def second_copies(f):
        src = xb.at[f, :, pl.ds(R, R)]
        return (
            remote(src, xb.at[f, :, pl.ds(0, R)], s2.at[f, 0], r2.at[f, 0], shifted(False, 1)),
            remote(src, xb.at[f, :, pl.ds(2 * R, R)], s2.at[f, 1], r2.at[f, 1], shifted(False, -1)),
        )

    def y_copies(f):
        return (
            remote(pack.at[0, f], halo.at[1, f], s3.at[f, 0], r3.at[f, 0], y_peer(-1)),
            remote(pack.at[1, f], halo.at[0, f], s3.at[f, 1], r3.at[f, 1], y_peer(1)),
        )

    def exchange(n, peer_of, me, src, dst, place, ssem, rsem):
        copies = []
        for step in range(1, n):
            copies.append(
                remote(
                    src.at[lax.rem(me + step, n)], dst.at[place[step]], ssem.at[step], rsem.at[step], peer_of(step)
                )
            )
        return copies

    far_x = [nx // 2 + m if h == 0 else nx // 2 - 1 - m for m in range(nx // 2) for h in range(2)]
    place_x = [far_x.index(step) for step in range(nx)]
    order_y = [ny // 2 + i for i in range(ny // 2)] + [ny // 2 - 1 - i for i in range(ny // 2)]
    place_y = [order_y.index(step) for step in range(ny)]

    for c in range(3):
        loads[c].wait()

        @pl.when(par == 0)
        def _():
            u[c, R : 2 * R] = v_ref[c].reshape(R, R, 128)

        @pl.when(par == 1)
        def _():
            for b in range(R):
                u[c, R + b] = v_ref[c, pl.ds(b, R, stride=R), :]

        if c == 0:
            pl.semaphore_wait(barrier, len(near) + 2)
            if rounds:
                tell(0)
        for copy in first_copies(c):
            copy.start()

    for load in loads[3:8]:
        load.wait()
    hot = (lax.broadcasted_iota(jnp.int32, (owners, count), 0) == own_ref[...]).astype(F32)
    onehot[...] = hot.astype(BF16)
    earlier = (
        lax.broadcasted_iota(jnp.int32, (128, 128), 0) < lax.broadcasted_iota(jnp.int32, (128, 128), 1)
    ).astype(BF16)
    carry = jnp.zeros((owners, 1), F32)
    ranks = []
    for block in range(count // 128):
        part = hot[:, block * 128 : block * 128 + 128]
        before = dot(part.astype(BF16), earlier) + carry
        ranks.append(jnp.sum(part * before, axis=0, keepdims=True))
        carry = carry + jnp.sum(part, axis=1, keepdims=True)
    rank = jnp.concatenate(ranks, axis=1)
    slot = lax.broadcasted_iota(jnp.int32, (CAP, count), 0).astype(F32) == rank
    rankhot[...] = slot.astype(F32)
    cell = (cz_ref[...] * R + cx_ref[...]) * 128 + cy_ref[...]

    def pieces(w):
        p0 = w.astype(BF16).astype(F32)
        p1 = (w - p0).astype(BF16).astype(F32)
        p2 = w - p0 - p1
        return p0, p1, p2

    wx = pieces(qw_ref[0:1, :])
    wy = pieces(qw_ref[1:2, :])
    wz = pieces(qw_ref[2:3, :])
    cell_hi = (cell >> 8).astype(F32)
    cell_lo = (cell & 255).astype(F32)
    zero = jnp.zeros_like(cell_lo)
    order = [
        cell_hi, wx[0], cell_lo, wx[1], zero, wx[2],
        wy[0], wz[0], wy[1], wz[1], wy[2], wz[2],
    ]
    placed = jnp.concatenate(
        [jnp.where(slot, p, jnp.zeros_like(p)).astype(BF16) for p in order], axis=0
    )
    spread = lax.dot_general(
        onehot[...], placed, (((1,), (1,)), ((), ())), preferred_element_type=F32
    )
    lane = lax.broadcasted_iota(jnp.int32, (1, 128), 1)
    scale = jnp.where(lane < CAP, 256.0, 1.0)
    head = spread[:, 0:128] * scale + spread[:, 128:256] + spread[:, 256:384]
    tail = spread[:, 384:512] + spread[:, 512:640] + spread[:, 640:768]
    for i in range(nx):
        sendq[i, 0] = head[i * ny : (i + 1) * ny]
        sendq[i, 1] = tail[i * ny : (i + 1) * ny]
    out_x = exchange(nx, x_peer, mx, sendq, gotq, place_x, sa, ra)
    gotq[place_x[0]] = sendq[mx]
    if rounds:
        hear(0)
    if rounds > 1:
        tell(1)

    for copy in first_copies(0):
        copy.wait_send()
    pl.semaphore_signal(clear, inc=1, device_id=y_peer(1 - 2 * par), device_id_type=MESH)

    def first_filter(f):
        i, j = FIELDS[f]

        def chunk(n, _):
            bs = pl.multiple_of((n // 2) * 8, 8)
            h = (n % 2) * 8
            x = u[i, pl.ds(h, 40), pl.ds(bs, 8), :]
            if j is not None:
                x = x * u[j, pl.ds(h, 40), pl.ds(bs, 8), :]
            acc = x[R : R + 8] * g[R]
            for d in range(1, R + 1):
                acc = acc + (x[R - d : R + 8 - d] + x[R + d : R + 8 + d]) * g[R + d]
            xb[f, pl.ds(h, 8), pl.ds(R + bs, 8), :] = acc
            return 0

        lax.fori_loop(0, 4, chunk, 0)
        for copy in second_copies(f):
            copy.start()

    field = 0
    for c in range(3):
        for copy in first_copies(c):
            copy.wait_recv()
        for _ in range(c + 2):
            if field == 0:
                for r in range(1, rounds - 1):
                    hear(r)
                    tell(r + 1)
                pl.semaphore_wait(clear, 1)
            first_filter(field)
            if field == 1:
                if rounds > 1:
                    hear(rounds - 1)
                for copy in out_x:
                    copy.start()
            field += 1

    for copy in out_x:
        copy.wait_recv()
    for j in range(ny):
        for k in range(2):
            passq[j, k] = gotq[:, k, j, :]
    out_y = exchange(ny, y_peer, my, passq, haveq, place_y, sb, rb)
    for copy in out_y:
        copy.start()
    haveq[place_y[0]] = passq[my]

    def hops(chunk):
        step = far_x[2 * chunk // (ny // 2)]
        return min(step, nx - step) + min(2, ny // 4) - 2 * chunk % (ny // 2) // 2

    order = sorted(range(owners * CAP // 256), key=lambda chunk: -hops(chunk))
    codes = [
        int(np.uint32(sum(c << (4 * i) for i, c in enumerate(order[at : at + 8]))).astype(np.int32))
        for at in range(0, len(order), 8)
    ]

    def natural(n):
        code = codes[0] if len(codes) == 1 else jnp.where(n < 8, codes[0], codes[1])
        return lax.shift_right_logical(jnp.int32(code), 4 * (n & 7)) & 15

    def quotient(a, b):
        return a >> (b.bit_length() - 1) if b & (b - 1) == 0 else lax.div(a, b)

    def remainder(a, b):
        return a & (b - 1) if b & (b - 1) == 0 else lax.rem(a, b)

    half = owners // 2
    low = lane < CAP
    chunks = owners * CAP // 256

    def slot_weights():
        for copy in out_y:
            copy.wait_recv()
        def table(k, start):
            return jnp.concatenate(
                [haveq[start : start + ny // 2, k, i, :] for i in range(nx)], axis=0
            )

        tops = [table(k, 0) for k in range(2)]
        bottoms = [table(k, ny // 2) for k in range(2)]

        def paired(k, second):
            top, bottom = tops[k], bottoms[k]
            if second:
                return jnp.where(low, pltpu.roll(top, CAP, 1), bottom)
            return jnp.where(low, top, pltpu.roll(bottom, CAP, 1))

        q_cell = paired(0, False).astype(jnp.int32)
        q_wx = paired(0, True)
        q_wy = paired(1, False)
        q_wz = paired(1, True)
        q_cz = (q_cell >> 11).astype(F32)
        q_cx = ((q_cell >> 7) & (R - 1)).astype(F32)
        z_first = par == 0
        rows[0] = jnp.where(z_first, q_cz, q_cx)
        rows[1] = jnp.where(z_first, q_cx, q_cz)
        rows[2] = (q_cell & 127).astype(F32)
        rows[3] = jnp.where(z_first, q_wz, q_wx)
        rows[4] = jnp.where(z_first, q_wx, q_wz)
        rows[5] = q_wy

        def weights(n, _):
            at = natural(n)

            def row(k):
                return jnp.concatenate([rows[k, pl.ds(2 * at, 1), :], rows[k, pl.ds(2 * at + 1, 1), :]], axis=1)

            def index(size):
                return lax.broadcasted_iota(jnp.int32, (size, 256), 0).astype(F32)

            def eighth(x):
                return jnp.floor(x * 256.0 + 0.5) * (1.0 / 256.0)

            ca, cb, cy = row(0), row(1), row(2)
            wa, wb, wy = eighth(row(3)), eighth(row(4)), row(5)
            both = eighth(wa * wb)
            ib = index(R)
            lower, upper = ib == cb, ib == cb + 1.0
            near = jnp.where(lower, 1.0 - wa - wb + both, jnp.where(upper, wb - both, 0.0))
            far = jnp.where(lower, wa - both, jnp.where(upper, both, 0.0))
            for a in range(R):
                part = jnp.where(ca == float(a), near, jnp.where(ca == float(a - 1), far, 0.0))
                w1[n, R * a : R * a + R, :] = part.astype(BF16)
            iy = index(128)
            wyb[n] = jnp.where(iy == cy, 1.0 - wy, jnp.where(iy == cy + 1.0, wy, 0.0))
            return 0

        lax.fori_loop(0, chunks, weights, 0)

    group = lane // R
    for load in loads[8:]:
        load.wait()

    def second_filter(f, _):
        for copy in second_copies(f):
            copy.wait_recv()

        def pair(n, _):
            x = jnp.concatenate([xb[f, 2 * n], xb[f, 2 * n + 1]], axis=1)
            hi, lo = split(x)
            o = dot(sub_ref[...], jnp.concatenate([hi, hi, lo], axis=0))
            yb[f, pl.ds(pl.multiple_of(32 * n, 32), R), :] = o[:, :128]
            yb[f, pl.ds(pl.multiple_of(32 * n, 32) + R, R), :] = o[:, 128:]
            return 0

        lax.fori_loop(0, R // 2, pair, 0, unroll=True)
        for e in range(2):
            first = jnp.zeros((R, 128), F32)
            last = jnp.zeros((R, 128), F32)
            for k in range(R // 2):
                turned = yb[f, pl.ds(2 * k + e, R, stride=R), :]
                first = jnp.where(group == k, pltpu.roll(turned, R * k, 1) if k else turned, first)
                last = jnp.where(group == k, pltpu.roll(turned, (R * k + R) % 128, 1) if k < 7 else turned, last)
            pack[0, f, e] = first
            pack[1, f, e] = last
        for copy in y_copies(f):
            copy.start()
        hi, lo = split(yb[f])
        zf[f] = dot(jnp.concatenate([hi, lo], axis=1), mid_ref[...]) + dot(hi, midl_ref[...])
        return 0

    rim = (lane >= 128 - R) | (lane < R)

    def finish(first, end):
        def wait_y(f, _):
            for copy in y_copies(f):
                copy.wait_recv()
            return 0

        lax.fori_loop(first, end, wait_y, 0)
        n = end - first
        edges = jnp.concatenate(
            [halo[side, first:end].reshape(32 * n, 128) for side in range(2)], axis=1
        )
        hi, lo = split(edges)
        part = dot(hi, eh[...]) + dot(lo, eh[...]) + dot(hi, el[...])
        for k in range(R // 2):
            q, r = k // 4, k % 4
            turned = pltpu.roll(part[:, 128 * q : 128 * q + 128], (128 - R - 32 * r) % 128, 1)
            zf[first:end, 32 * k : 32 * k + 32, :] += jnp.where(rim, turned, 0.0).reshape(n, 32, 128)

    def stress(first, end):
        for d in range(first, end):
            i, j = DONE[d]
            tau = zf[FIELDS.index((i, j))] - zf[FIELDS.index((i, None))] * zf[FIELDS.index((j, None))]
            hi, lo = split(tau.T)
            st[d, :128] = hi
            st[d, 128:] = lo

    def at_queries(n, first, end):
        acc = dot(st[first:end].reshape(256 * (end - first), 256), w1[n])
        wys = wyb[n]
        found = []
        for d in range(end - first):
            both = acc[256 * d : 256 * d + 128] + acc[256 * d + 128 : 256 * d + 256]
            found.append(jnp.sum(both * wys, axis=0, keepdims=True))
        return found

    block = min(4, chunks)

    def pack_row(at, k, a, b):
        sendr[at, 0, k : k + 1, :] = jnp.where(low, a, pltpu.roll(b, CAP, 1))
        sendr[at, 1, k : k + 1, :] = jnp.where(low, pltpu.roll(a, CAP, 1), b)

    def interpolate(first, end, number):
        for n in range(block):
            n = block * number + n
            found = at_queries(n, first, end)
            for h in range(2):
                at = 2 * n + h
                v = [w[:, 128 * h : 128 * h + 128] for w in found]
                if first == 0:
                    pack_row(at, 0, v[0], v[1])
                    vals[pl.ds(at, 1), :] = v[2]
                else:
                    pack_row(at, 1, vals[pl.ds(at, 1), :], v[0])
                    pack_row(at, 2, v[1], v[2])

    def interpolate_early(start, stop):
        def step(number, _):
            interpolate(0, 3, number)
            return 0

        lax.fori_loop(start, stop, step, 0)

    me = mx * ny + my
    per = ny // 2

    def back(n, h, side):
        at = 2 * n + h
        where = 2 * natural(n) + h
        x, y = quotient(where, per), remainder(where, per)
        step_x = nx // 2 + (1 - 2 * (x & 1)) * ((x + 1) >> 1)
        step_y = ny // 2 + y if side == 0 else ny // 2 - 1 - y
        holder = (remainder(mx + nx - step_x, nx), remainder(my + ny - step_y, ny), mz)
        return remote(
            sendr.at[at, side], haver.at[me], sc.at[at, side], rc.at[at, side], holder
        )

    def each_back(n, act):
        for h in range(2):
            for side in range(2):
                if h == 1 and side == 1:

                    @pl.when(n < chunks - 1)
                    def _():
                        act(back(n, 1, 1))

                else:
                    act(back(n, h, side))

    def send_back(number, _):
        interpolate(3, 6, number)

        def send(n, _):
            each_back(n, lambda copy: copy.start())
            return 0

        lax.fori_loop(block * number, block * number + block, send, 0)
        return 0

    def second_filters(first, end):
        lax.fori_loop(first, end, second_filter, 0)

    second_filters(0, 6)
    slot_weights()
    finish(0, 5)
    stress(0, 3)
    second_filters(6, 9)
    interpolate_early(0, chunks // block)
    finish(5, 9)
    stress(3, 6)
    lax.fori_loop(0, chunks // block, send_back, 0)
    haver[me] = sendr[half - 1, 1]

    for c in range(1, 3):
        for copy in first_copies(c):
            copy.wait_send()

    def wait_sends(f, _):
        for copy in second_copies(f) + y_copies(f):
            copy.wait_send()
        return 0

    lax.fori_loop(0, 9, wait_sends, 0)
    for copy in out_y + out_x:
        copy.wait_send()

    def wait_sent(n, _):
        each_back(n, lambda copy: copy.wait_send())
        return 0

    lax.fori_loop(0, chunks, wait_sent, 0)

    def wait_back(n, _):
        each_back(n, lambda copy: copy.wait_recv())
        return 0

    lax.fori_loop(0, chunks, wait_back, 0)
    hot_two = jnp.concatenate([onehot[...], onehot[...]], axis=0)
    at_rank = rankhot[...]
    for k in range(3):
        piece = haver[:, k, :]
        hi = piece.astype(BF16).astype(F32)
        both = jnp.concatenate([hi, piece - hi], axis=0).T.astype(BF16)
        picked = dot(both, hot_two)
        for h in range(2):
            p = PAIRS.index(DONE[2 * k + h])
            out_ref[p : p + 1, :] = jnp.sum(
                picked[CAP * h : CAP * h + CAP] * at_rank, axis=0, keepdims=True
            )


def on_device(sizes, velocity, owner, cell_x, cell_y, cell_z, query_weights):
    nx, ny, nz = sizes
    count = owner.shape[0]
    owners = nx * ny
    half = owners // 2
    chunks = owners * CAP // 256
    vmem = pl.BlockSpec(memory_space=pltpu.VMEM)
    hbm = pl.BlockSpec(memory_space=pltpu.HBM)
    row = pltpu.VMEM((1, count), jnp.int32)
    dma = pltpu.SemaphoreType.DMA
    return pl.pallas_call(
        functools.partial(kernel, sizes),
        out_shape=jax.ShapeDtypeStruct((6, count), F32),
        in_specs=[hbm] * 11,
        out_specs=vmem,
        scratch_shapes=[
            pltpu.VMEM((3, R * R, 128), F32),
            row, row, row, row,
            pltpu.VMEM((3, count), F32),
            pltpu.VMEM((R, 9 * R), BF16),
            pltpu.VMEM((256, 128), BF16),
            pltpu.VMEM((128, 128), BF16),
            pltpu.VMEM((3, 3 * R, R, 128), F32),
            pltpu.VMEM((9, R, 3 * R, 128), F32),
            pltpu.VMEM((9, R * R, 128), F32),
            pltpu.VMEM((9, R * R, 128), F32),
            pltpu.VMEM((2, 9, 2, R, 128), F32),
            pltpu.VMEM((2, 9, 2, R, 128), F32),
            pltpu.VMEM((256, 256), BF16),
            pltpu.VMEM((256, 256), BF16),
            pltpu.VMEM((nx, 2, ny, 128), F32),
            pltpu.VMEM((nx, 2, ny, 128), F32),
            pltpu.VMEM((ny, 2, nx, 128), F32),
            pltpu.VMEM((ny, 2, nx, 128), F32),
            pltpu.VMEM((6, half, 128), F32),
            pltpu.VMEM((chunks, 256, 256), BF16),
            pltpu.VMEM((chunks, 128, 256), F32),
            pltpu.VMEM((6, 256, 256), BF16),
            pltpu.VMEM((half, 128), F32),
            pltpu.VMEM((half, 2, 3, 128), F32),
            pltpu.VMEM((owners, 3, 128), F32),
            pltpu.VMEM((owners, count), BF16),
            pltpu.VMEM((CAP, count), F32),
            dma((3, 2)), dma((3, 2)),
            dma((9, 2)), dma((9, 2)),
            dma((9, 2)), dma((9, 2)),
            dma((nx,)), dma((nx,)),
            dma((ny,)), dma((ny,)),
            dma((half, 2)), dma((half, 2)),
            dma((13,)),
            pltpu.SemaphoreType.REGULAR((max(1, max(nx, ny) // 2 - 1),)),
            pltpu.SemaphoreType.REGULAR,
        ],
        compiler_params=pltpu.CompilerParams(
            collective_id=0, has_side_effects=True, vmem_limit_bytes=40 * 1024 * 1024
        ),
    )(
        *[
            pltpu.with_memory_space_constraint(x, pltpu.HBM)
            for x in (
                velocity.reshape(3, R * R, 128),
                owner.reshape(1, count),
                cell_x.reshape(1, count),
                cell_y.reshape(1, count),
                cell_z.reshape(1, count),
                query_weights,
                *tables(velocity.shape[3]),
            )
        ]
    )


def solution(mesh):
    sizes = (mesh.shape["gx"], mesh.shape["gy"], mesh.shape["gz"])
    placed = (
        P(None, "gz", "gx", "gy"),
        P(("gx", "gy", "gz"), None),
        P(("gx", "gy", "gz")),
        P(("gx", "gy", "gz")),
        P(("gx", "gy", "gz")),
        P(None, ("gx", "gy", "gz")),
    )
    return jax.shard_map(
        functools.partial(on_device, sizes),
        mesh=mesh,
        in_specs=placed,
        out_specs=P(None, ("gx", "gy", "gz")),
        check_vma=False,
    )
```

```python
import functools

import jax
import jax.numpy as jnp
import numpy as np
from jax import lax
from jax.experimental import pallas as pl
from jax.experimental.pallas import tpu as pltpu
from jax.sharding import PartitionSpec as P

MESH = pl.DeviceIdType.MESH
F32 = jnp.float32
BF16 = jnp.bfloat16
FW = 32
R = FW // 2
CAP = 64
FIELDS = ((0, None), (0, 0), (1, None), (0, 1), (1, 1), (2, None), (0, 2), (1, 2), (2, 2))
PAIRS = ((0, 0), (0, 1), (0, 2), (1, 1), (1, 2), (2, 2))
DONE = ((0, 0), (0, 1), (1, 1), (0, 2), (1, 2), (2, 2))


def taps():
    offsets = np.arange(2 * R + 1).astype(np.float32) - np.float32(R)
    values = np.exp(np.float32(-6.0) * offsets * offsets / np.float32(FW * FW))
    return (values / values.sum(dtype=np.float32)).astype(np.float32)


def split(x):
    hi = x.astype(BF16)
    lo = (x - hi.astype(F32)).astype(BF16)
    return hi, lo


def np_split(x):
    hi = jnp.asarray(x, F32).astype(BF16)
    lo = (jnp.asarray(x, F32) - hi.astype(F32)).astype(BF16)
    return hi, lo


def tables(by):
    g = taps()

    def band(rows, cols, shift):
        m = np.arange(rows)[:, None] - np.arange(cols)[None, :] + shift
        return np.where((m >= 0) & (m <= 2 * R), g[np.clip(m, 0, 2 * R)], np.float32(0))

    sub = band(3 * R, R, 0).T
    mid = band(by, by, R)
    left = band(R, by, 0)
    right = band(R, by, by + R)
    edge = np.zeros((256, 256), np.float32)
    for k in range(R // 2):
        edge[128 + R * k : 128 + R * k + R, 32 * k : 32 * k + R] = right[:, by - R :]
        edge[R * k : R * k + R, 32 * k + R : 32 * k + 32] = left[:, :R]
    sh, sl = np_split(sub)
    mh, ml = np_split(mid)
    eh, el = np_split(edge)
    return (
        jnp.concatenate([sh, sl, sh], axis=1),
        jnp.concatenate([mh, mh], axis=0),
        ml,
        eh,
        el,
    )


def dot(a, b):
    return jnp.dot(a, b, preferred_element_type=F32)


def kernel(
    sizes,
    v_hbm, own_hbm, cx_hbm, cy_hbm, cz_hbm, qw_hbm, sub_hbm, mid_hbm, midl_hbm, eh_hbm, el_hbm,
    out_ref,
    v_ref, own_ref, cx_ref, cy_ref, cz_ref, qw_ref, sub_ref, mid_ref, midl_ref,
    u, xb, yb, zf, pack, halo, eh, el,
    sendq, gotq, passq, haveq, rows, w1, wyb,
    st, vals, sendr, haver, onehot, rankhot,
    s1, r1, s2, r2, s3, r3, sa, ra, sb, rb, sc, rc, lsem, token, clear,
):
    nx, ny, nz = sizes
    g = [float(t) for t in taps()]
    mx, my, mz = lax.axis_index("gx"), lax.axis_index("gy"), lax.axis_index("gz")
    par = lax.rem(my, 2)
    owners = nx * ny
    count = own_ref.shape[1]

    def shifted(first, step):
        on_x = par if first else 1 - par
        on_z = 1 - on_x
        return (
            lax.rem(mx + on_x * (step % nx), nx),
            my,
            lax.rem(mz + on_z * (step % nz), nz),
        )

    def y_peer(step):
        return (mx, lax.rem(my + ny + step, ny), mz)

    def x_peer(step):
        return (lax.rem(mx + step % nx, nx), my, mz)

    def remote(src, dst, ssem, rsem, dev):
        return pltpu.make_async_remote_copy(
            src_ref=src, dst_ref=dst, send_sem=ssem, recv_sem=rsem, device_id=dev, device_id_type=MESH
        )

    loads = [
        pltpu.make_async_copy(src, dst, lsem.at[number])
        for number, (src, dst) in enumerate(
            (
                (v_hbm.at[0], v_ref.at[0]),
                (v_hbm.at[1], v_ref.at[1]),
                (v_hbm.at[2], v_ref.at[2]),
                (own_hbm, own_ref),
                (cx_hbm, cx_ref),
                (cy_hbm, cy_ref),
                (cz_hbm, cz_ref),
                (qw_hbm, qw_ref),
                (sub_hbm, sub_ref),
                (mid_hbm, mid_ref),
                (midl_hbm, midl_ref),
                (eh_hbm, eh),
                (el_hbm, el),
            )
        )
    ]
    for load in loads:
        load.start()

    barrier = pltpu.get_barrier_semaphore()
    near = (x_peer(1), x_peer(-1), y_peer(1), y_peer(-1))
    for peer in near + ((mx, my, lax.rem(mz + 1, nz)), (mx, my, lax.rem(mz + nz - 1, nz))):
        pl.semaphore_signal(barrier, inc=1, device_id=peer, device_id_type=MESH)

    rounds = max(nx, ny) // 2 - 1

    def tell(r):
        for peer in near:
            pl.semaphore_signal(token.at[r], inc=1, device_id=peer, device_id_type=MESH)

    def hear(r):
        pl.semaphore_wait(token.at[r], len(near))

    def first_copies(c):
        src = u.at[c, pl.ds(R, R)]
        return (
            remote(src, u.at[c, pl.ds(0, R)], s1.at[c, 0], r1.at[c, 0], shifted(True, 1)),
            remote(src, u.at[c, pl.ds(2 * R, R)], s1.at[c, 1], r1.at[c, 1], shifted(True, -1)),
        )

    def second_copies(f):
        src = xb.at[f, :, pl.ds(R, R)]
        return (
            remote(src, xb.at[f, :, pl.ds(0, R)], s2.at[f, 0], r2.at[f, 0], shifted(False, 1)),
            remote(src, xb.at[f, :, pl.ds(2 * R, R)], s2.at[f, 1], r2.at[f, 1], shifted(False, -1)),
        )

    def y_copies(f):
        return (
            remote(pack.at[0, f], halo.at[1, f], s3.at[f, 0], r3.at[f, 0], y_peer(-1)),
            remote(pack.at[1, f], halo.at[0, f], s3.at[f, 1], r3.at[f, 1], y_peer(1)),
        )

    def exchange(n, peer_of, me, src, dst, place, ssem, rsem):
        copies = []
        for step in range(1, n):
            copies.append(
                remote(
                    src.at[lax.rem(me + step, n)], dst.at[place[step]], ssem.at[step], rsem.at[step], peer_of(step)
                )
            )
        return copies

    far_x = [nx // 2 + m if h == 0 else nx // 2 - 1 - m for m in range(nx // 2) for h in range(2)]
    place_x = [far_x.index(step) for step in range(nx)]
    order_y = [ny // 2 + i for i in range(ny // 2)] + [ny // 2 - 1 - i for i in range(ny // 2)]
    place_y = [order_y.index(step) for step in range(ny)]

    for c in range(3):
        loads[c].wait()

        @pl.when(par == 0)
        def _():
            u[c, R : 2 * R] = v_ref[c].reshape(R, R, 128)

        @pl.when(par == 1)
        def _():
            for b in range(R):
                u[c, R + b] = v_ref[c, pl.ds(b, R, stride=R), :]

        if c == 0:
            pl.semaphore_wait(barrier, len(near) + 2)
            if rounds:
                tell(0)
        for copy in first_copies(c):
            copy.start()

    for load in loads[3:8]:
        load.wait()
    hot = (lax.broadcasted_iota(jnp.int32, (owners, count), 0) == own_ref[...]).astype(F32)
    onehot[...] = hot.astype(BF16)
    earlier = (
        lax.broadcasted_iota(jnp.int32, (128, 128), 0) < lax.broadcasted_iota(jnp.int32, (128, 128), 1)
    ).astype(BF16)
    carry = jnp.zeros((owners, 1), F32)
    ranks = []
    for block in range(count // 128):
        part = hot[:, block * 128 : block * 128 + 128]
        before = dot(part.astype(BF16), earlier) + carry
        ranks.append(jnp.sum(part * before, axis=0, keepdims=True))
        carry = carry + jnp.sum(part, axis=1, keepdims=True)
    rank = jnp.concatenate(ranks, axis=1)
    slot = lax.broadcasted_iota(jnp.int32, (CAP, count), 0).astype(F32) == rank
    rankhot[...] = slot.astype(F32)
    cell = (cz_ref[...] * R + cx_ref[...]) * 128 + cy_ref[...]

    def pieces(w):
        p0 = w.astype(BF16).astype(F32)
        p1 = (w - p0).astype(BF16).astype(F32)
        p2 = w - p0 - p1
        return p0, p1, p2

    wx = pieces(qw_ref[0:1, :])
    wy = pieces(qw_ref[1:2, :])
    wz = pieces(qw_ref[2:3, :])
    cell_hi = (cell >> 8).astype(F32)
    cell_lo = (cell & 255).astype(F32)
    zero = jnp.zeros_like(cell_lo)
    order = [
        cell_hi, wx[0], cell_lo, wx[1], zero, wx[2],
        wy[0], wz[0], wy[1], wz[1], wy[2], wz[2],
    ]
    placed = jnp.concatenate(
        [jnp.where(slot, p, jnp.zeros_like(p)).astype(BF16) for p in order], axis=0
    )
    spread = lax.dot_general(
        onehot[...], placed, (((1,), (1,)), ((), ())), preferred_element_type=F32
    )
    lane = lax.broadcasted_iota(jnp.int32, (1, 128), 1)
    scale = jnp.where(lane < CAP, 256.0, 1.0)
    head = spread[:, 0:128] * scale + spread[:, 128:256] + spread[:, 256:384]
    tail = spread[:, 384:512] + spread[:, 512:640] + spread[:, 640:768]
    for i in range(nx):
        sendq[i, 0] = head[i * ny : (i + 1) * ny]
        sendq[i, 1] = tail[i * ny : (i + 1) * ny]
    out_x = exchange(nx, x_peer, mx, sendq, gotq, place_x, sa, ra)
    gotq[place_x[0]] = sendq[mx]
    if rounds:
        hear(0)
    if rounds > 1:
        tell(1)

    for copy in first_copies(0):
        copy.wait_send()
    pl.semaphore_signal(clear, inc=1, device_id=y_peer(1 - 2 * par), device_id_type=MESH)

    def first_filter(f):
        i, j = FIELDS[f]

        def chunk(n, _):
            bs = pl.multiple_of((n // 2) * 8, 8)
            h = (n % 2) * 8
            x = u[i, pl.ds(h, 40), pl.ds(bs, 8), :]
            if j is not None:
                x = x * u[j, pl.ds(h, 40), pl.ds(bs, 8), :]
            acc = x[R : R + 8] * g[R]
            for d in range(1, R + 1):
                acc = acc + (x[R - d : R + 8 - d] + x[R + d : R + 8 + d]) * g[R + d]
            xb[f, pl.ds(h, 8), pl.ds(R + bs, 8), :] = acc
            return 0

        lax.fori_loop(0, 4, chunk, 0)
        for copy in second_copies(f):
            copy.start()

    field = 0
    for c in range(3):
        for copy in first_copies(c):
            copy.wait_recv()
        for _ in range(c + 2):
            if field == 0:
                for r in range(1, rounds - 1):
                    hear(r)
                    tell(r + 1)
                pl.semaphore_wait(clear, 1)
            first_filter(field)
            if field == 1:
                if rounds > 1:
                    hear(rounds - 1)
                for copy in out_x:
                    copy.start()
            field += 1

    for copy in out_x:
        copy.wait_recv()
    for j in range(ny):
        for k in range(2):
            passq[j, k] = gotq[:, k, j, :]
    out_y = exchange(ny, y_peer, my, passq, haveq, place_y, sb, rb)
    for copy in out_y:
        copy.start()
    haveq[place_y[0]] = passq[my]

    def hops(chunk):
        step = far_x[2 * chunk // (ny // 2)]
        return min(step, nx - step) + min(2, ny // 4) - 2 * chunk % (ny // 2) // 2

    order = sorted(range(owners * CAP // 256), key=lambda chunk: -hops(chunk))
    codes = [
        int(np.uint32(sum(c << (4 * i) for i, c in enumerate(order[at : at + 8]))).astype(np.int32))
        for at in range(0, len(order), 8)
    ]

    def natural(n):
        code = codes[0] if len(codes) == 1 else jnp.where(n < 8, codes[0], codes[1])
        return lax.shift_right_logical(jnp.int32(code), 4 * (n & 7)) & 15

    def quotient(a, b):
        return a >> (b.bit_length() - 1) if b & (b - 1) == 0 else lax.div(a, b)

    def remainder(a, b):
        return a & (b - 1) if b & (b - 1) == 0 else lax.rem(a, b)

    half = owners // 2
    low = lane < CAP
    chunks = owners * CAP // 256

    def slot_weights():
        for copy in out_y:
            copy.wait_recv()
        def table(k, start):
            return jnp.concatenate(
                [haveq[start : start + ny // 2, k, i, :] for i in range(nx)], axis=0
            )

        tops = [table(k, 0) for k in range(2)]
        bottoms = [table(k, ny // 2) for k in range(2)]

        def paired(k, second):
            top, bottom = tops[k], bottoms[k]
            if second:
                return jnp.where(low, pltpu.roll(top, CAP, 1), bottom)
            return jnp.where(low, top, pltpu.roll(bottom, CAP, 1))

        q_cell = paired(0, False).astype(jnp.int32)
        q_wx = paired(0, True)
        q_wy = paired(1, False)
        q_wz = paired(1, True)
        q_cz = (q_cell >> 11).astype(F32)
        q_cx = ((q_cell >> 7) & (R - 1)).astype(F32)
        z_first = par == 0
        rows[0] = jnp.where(z_first, q_cz, q_cx)
        rows[1] = jnp.where(z_first, q_cx, q_cz)
        rows[2] = (q_cell & 127).astype(F32)
        rows[3] = jnp.where(z_first, q_wz, q_wx)
        rows[4] = jnp.where(z_first, q_wx, q_wz)
        rows[5] = q_wy

        def weights(n, _):
            at = natural(n)

            def row(k):
                return jnp.concatenate([rows[k, pl.ds(2 * at, 1), :], rows[k, pl.ds(2 * at + 1, 1), :]], axis=1)

            def index(size):
                return lax.broadcasted_iota(jnp.int32, (size, 256), 0).astype(F32)

            def eighth(x):
                return jnp.floor(x * 256.0 + 0.5) * (1.0 / 256.0)

            ca, cb, cy = row(0), row(1), row(2)
            wa, wb, wy = eighth(row(3)), eighth(row(4)), row(5)
            both = eighth(wa * wb)
            ib = index(R)
            lower, upper = ib == cb, ib == cb + 1.0
            near = jnp.where(lower, 1.0 - wa - wb + both, jnp.where(upper, wb - both, 0.0))
            far = jnp.where(lower, wa - both, jnp.where(upper, both, 0.0))
            for a in range(R):
                part = jnp.where(ca == float(a), near, jnp.where(ca == float(a - 1), far, 0.0))
                w1[n, R * a : R * a + R, :] = part.astype(BF16)
            iy = index(128)
            wyb[n] = jnp.where(iy == cy, 1.0 - wy, jnp.where(iy == cy + 1.0, wy, 0.0))
            return 0

        lax.fori_loop(0, chunks, weights, 0)

    group = lane // R
    for load in loads[8:]:
        load.wait()

    def second_filter(f, _):
        for copy in second_copies(f):
            copy.wait_recv()

        def pair(n, _):
            x = jnp.concatenate([xb[f, 2 * n], xb[f, 2 * n + 1]], axis=1)
            hi, lo = split(x)
            o = dot(sub_ref[...], jnp.concatenate([hi, hi, lo], axis=0))
            yb[f, pl.ds(pl.multiple_of(32 * n, 32), R), :] = o[:, :128]
            yb[f, pl.ds(pl.multiple_of(32 * n, 32) + R, R), :] = o[:, 128:]
            return 0

        lax.fori_loop(0, R // 2, pair, 0, unroll=True)
        for e in range(2):
            first = jnp.zeros((R, 128), F32)
            last = jnp.zeros((R, 128), F32)
            for k in range(R // 2):
                turned = yb[f, pl.ds(2 * k + e, R, stride=R), :]
                first = jnp.where(group == k, pltpu.roll(turned, R * k, 1) if k else turned, first)
                last = jnp.where(group == k, pltpu.roll(turned, (R * k + R) % 128, 1) if k < 7 else turned, last)
            pack[0, f, e] = first
            pack[1, f, e] = last
        for copy in y_copies(f):
            copy.start()
        hi, lo = split(yb[f])
        zf[f] = dot(jnp.concatenate([hi, lo], axis=1), mid_ref[...]) + dot(hi, midl_ref[...])
        return 0

    rim = (lane >= 128 - R) | (lane < R)

    def finish(first, end):
        def wait_y(f, _):
            for copy in y_copies(f):
                copy.wait_recv()
            return 0

        lax.fori_loop(first, end, wait_y, 0)
        n = end - first
        edges = jnp.concatenate(
            [halo[side, first:end].reshape(32 * n, 128) for side in range(2)], axis=1
        )
        hi, lo = split(edges)
        part = dot(hi, eh[...]) + dot(lo, eh[...]) + dot(hi, el[...])
        for k in range(R // 2):
            q, r = k // 4, k % 4
            turned = pltpu.roll(part[:, 128 * q : 128 * q + 128], (128 - R - 32 * r) % 128, 1)
            zf[first:end, 32 * k : 32 * k + 32, :] += jnp.where(rim, turned, 0.0).reshape(n, 32, 128)

    def stress(first, end):
        for d in range(first, end):
            i, j = DONE[d]
            tau = zf[FIELDS.index((i, j))] - zf[FIELDS.index((i, None))] * zf[FIELDS.index((j, None))]
            hi, lo = split(tau.T)
            st[d, :128] = hi
            st[d, 128:] = lo

    def at_queries(n, first, end):
        acc = dot(st[first:end].reshape(256 * (end - first), 256), w1[n])
        wys = wyb[n]
        found = []
        for d in range(end - first):
            both = acc[256 * d : 256 * d + 128] + acc[256 * d + 128 : 256 * d + 256]
            found.append(jnp.sum(both * wys, axis=0, keepdims=True))
        return found

    block = min(4, chunks)

    def pack_row(at, k, a, b):
        sendr[at, 0, k : k + 1, :] = jnp.where(low, a, pltpu.roll(b, CAP, 1))
        sendr[at, 1, k : k + 1, :] = jnp.where(low, pltpu.roll(a, CAP, 1), b)

    def interpolate(first, end, number):
        for n in range(block):
            n = block * number + n
            found = at_queries(n, first, end)
            for h in range(2):
                at = 2 * n + h
                v = [w[:, 128 * h : 128 * h + 128] for w in found]
                if first == 0:
                    pack_row(at, 0, v[0], v[1])
                    vals[pl.ds(at, 1), :] = v[2]
                else:
                    pack_row(at, 1, vals[pl.ds(at, 1), :], v[0])
                    pack_row(at, 2, v[1], v[2])

    def interpolate_early(start, stop):
        def step(number, _):
            interpolate(0, 3, number)
            return 0

        lax.fori_loop(start, stop, step, 0)

    me = mx * ny + my
    per = ny // 2

    def back(n, h, side):
        at = 2 * n + h
        where = 2 * natural(n) + h
        x, y = quotient(where, per), remainder(where, per)
        step_x = nx // 2 + (1 - 2 * (x & 1)) * ((x + 1) >> 1)
        step_y = ny // 2 + y if side == 0 else ny // 2 - 1 - y
        holder = (remainder(mx + nx - step_x, nx), remainder(my + ny - step_y, ny), mz)
        return remote(
            sendr.at[at, side], haver.at[me], sc.at[at, side], rc.at[at, side], holder
        )

    def each_back(n, act):
        for h in range(2):
            for side in range(2):
                if h == 1 and side == 1:

                    @pl.when(n < chunks - 1)
                    def _():
                        act(back(n, 1, 1))

                else:
                    act(back(n, h, side))

    def send_back(number, _):
        interpolate(3, 6, number)

        def send(n, _):
            each_back(n, lambda copy: copy.start())
            return 0

        lax.fori_loop(block * number, block * number + block, send, 0)
        return 0

    early = 1 if chunks // block > 1 else 0

    def second_filters(first, end):
        lax.fori_loop(first, end, second_filter, 0)

    second_filters(0, 6)
    slot_weights()
    finish(0, 5)
    stress(0, 3)
    second_filters(6, 8)
    interpolate_early(0, early)
    second_filters(8, 9)
    interpolate_early(early, chunks // block)
    finish(5, 9)
    stress(3, 6)
    lax.fori_loop(0, chunks // block, send_back, 0)
    haver[me] = sendr[half - 1, 1]

    for c in range(1, 3):
        for copy in first_copies(c):
            copy.wait_send()

    def wait_sends(f, _):
        for copy in second_copies(f) + y_copies(f):
            copy.wait_send()
        return 0

    lax.fori_loop(0, 9, wait_sends, 0)
    for copy in out_y + out_x:
        copy.wait_send()

    def wait_sent(n, _):
        each_back(n, lambda copy: copy.wait_send())
        return 0

    lax.fori_loop(0, chunks, wait_sent, 0)

    def wait_back(n, _):
        each_back(n, lambda copy: copy.wait_recv())
        return 0

    lax.fori_loop(0, chunks, wait_back, 0)
    hot_two = jnp.concatenate([onehot[...], onehot[...]], axis=0)
    at_rank = rankhot[...]
    for k in range(3):
        piece = haver[:, k, :]
        hi = piece.astype(BF16).astype(F32)
        both = jnp.concatenate([hi, piece - hi], axis=0).T.astype(BF16)
        picked = dot(both, hot_two)
        for h in range(2):
            p = PAIRS.index(DONE[2 * k + h])
            out_ref[p : p + 1, :] = jnp.sum(
                picked[CAP * h : CAP * h + CAP] * at_rank, axis=0, keepdims=True
            )


def on_device(sizes, velocity, owner, cell_x, cell_y, cell_z, query_weights):
    nx, ny, nz = sizes
    count = owner.shape[0]
    owners = nx * ny
    half = owners // 2
    chunks = owners * CAP // 256
    vmem = pl.BlockSpec(memory_space=pltpu.VMEM)
    hbm = pl.BlockSpec(memory_space=pltpu.HBM)
    row = pltpu.VMEM((1, count), jnp.int32)
    dma = pltpu.SemaphoreType.DMA
    return pl.pallas_call(
        functools.partial(kernel, sizes),
        out_shape=jax.ShapeDtypeStruct((6, count), F32),
        in_specs=[hbm] * 11,
        out_specs=vmem,
        scratch_shapes=[
            pltpu.VMEM((3, R * R, 128), F32),
            row, row, row, row,
            pltpu.VMEM((3, count), F32),
            pltpu.VMEM((R, 9 * R), BF16),
            pltpu.VMEM((256, 128), BF16),
            pltpu.VMEM((128, 128), BF16),
            pltpu.VMEM((3, 3 * R, R, 128), F32),
            pltpu.VMEM((9, R, 3 * R, 128), F32),
            pltpu.VMEM((9, R * R, 128), F32),
            pltpu.VMEM((9, R * R, 128), F32),
            pltpu.VMEM((2, 9, 2, R, 128), F32),
            pltpu.VMEM((2, 9, 2, R, 128), F32),
            pltpu.VMEM((256, 256), BF16),
            pltpu.VMEM((256, 256), BF16),
            pltpu.VMEM((nx, 2, ny, 128), F32),
            pltpu.VMEM((nx, 2, ny, 128), F32),
            pltpu.VMEM((ny, 2, nx, 128), F32),
            pltpu.VMEM((ny, 2, nx, 128), F32),
            pltpu.VMEM((6, half, 128), F32),
            pltpu.VMEM((chunks, 256, 256), BF16),
            pltpu.VMEM((chunks, 128, 256), F32),
            pltpu.VMEM((6, 256, 256), BF16),
            pltpu.VMEM((half, 128), F32),
            pltpu.VMEM((half, 2, 3, 128), F32),
            pltpu.VMEM((owners, 3, 128), F32),
            pltpu.VMEM((owners, count), BF16),
            pltpu.VMEM((CAP, count), F32),
            dma((3, 2)), dma((3, 2)),
            dma((9, 2)), dma((9, 2)),
            dma((9, 2)), dma((9, 2)),
            dma((nx,)), dma((nx,)),
            dma((ny,)), dma((ny,)),
            dma((half, 2)), dma((half, 2)),
            dma((13,)),
            pltpu.SemaphoreType.REGULAR((max(1, max(nx, ny) // 2 - 1),)),
            pltpu.SemaphoreType.REGULAR,
        ],
        compiler_params=pltpu.CompilerParams(
            collective_id=0, has_side_effects=True, vmem_limit_bytes=40 * 1024 * 1024
        ),
    )(
        *[
            pltpu.with_memory_space_constraint(x, pltpu.HBM)
            for x in (
                velocity.reshape(3, R * R, 128),
                owner.reshape(1, count),
                cell_x.reshape(1, count),
                cell_y.reshape(1, count),
                cell_z.reshape(1, count),
                query_weights,
                *tables(velocity.shape[3]),
            )
        ]
    )


def solution(mesh):
    sizes = (mesh.shape["gx"], mesh.shape["gy"], mesh.shape["gz"])
    placed = (
        P(None, "gz", "gx", "gy"),
        P(("gx", "gy", "gz"), None),
        P(("gx", "gy", "gz")),
        P(("gx", "gy", "gz")),
        P(("gx", "gy", "gz")),
        P(None, ("gx", "gy", "gz")),
    )
    return jax.shard_map(
        functools.partial(on_device, sizes),
        mesh=mesh,
        in_specs=placed,
        out_specs=P(None, ("gx", "gy", "gz")),
        check_vma=False,
    )
```

```python
import functools

import jax
import jax.numpy as jnp
import numpy as np
from jax import lax
from jax.experimental import pallas as pl
from jax.experimental.pallas import tpu as pltpu
from jax.sharding import PartitionSpec as P

MESH = pl.DeviceIdType.MESH
F32 = jnp.float32
BF16 = jnp.bfloat16
FW = 32
R = FW // 2
CAP = 64
FIELDS = ((0, None), (0, 0), (1, None), (0, 1), (1, 1), (2, None), (0, 2), (1, 2), (2, 2))
PAIRS = ((0, 0), (0, 1), (0, 2), (1, 1), (1, 2), (2, 2))
DONE = ((0, 0), (0, 1), (1, 1), (0, 2), (1, 2), (2, 2))


def taps():
    offsets = np.arange(2 * R + 1).astype(np.float32) - np.float32(R)
    values = np.exp(np.float32(-6.0) * offsets * offsets / np.float32(FW * FW))
    return (values / values.sum(dtype=np.float32)).astype(np.float32)


def split(x):
    hi = x.astype(BF16)
    lo = (x - hi.astype(F32)).astype(BF16)
    return hi, lo


def np_split(x):
    hi = jnp.asarray(x, F32).astype(BF16)
    lo = (jnp.asarray(x, F32) - hi.astype(F32)).astype(BF16)
    return hi, lo


def tables(by):
    g = taps()

    def band(rows, cols, shift):
        m = np.arange(rows)[:, None] - np.arange(cols)[None, :] + shift
        return np.where((m >= 0) & (m <= 2 * R), g[np.clip(m, 0, 2 * R)], np.float32(0))

    sub = band(3 * R, R, 0).T
    mid = band(by, by, R)
    left = band(R, by, 0)
    right = band(R, by, by + R)
    edge = np.zeros((256, 256), np.float32)
    for k in range(R // 2):
        edge[128 + R * k : 128 + R * k + R, 32 * k : 32 * k + R] = right[:, by - R :]
        edge[R * k : R * k + R, 32 * k + R : 32 * k + 32] = left[:, :R]
    sh, sl = np_split(sub)
    mh, ml = np_split(mid)
    eh, el = np_split(edge)
    return (
        jnp.concatenate([sh, sl, sh], axis=1),
        jnp.concatenate([mh, mh], axis=0),
        ml,
        eh,
        el,
    )


def dot(a, b):
    return jnp.dot(a, b, preferred_element_type=F32)


def kernel(
    sizes,
    v_hbm, own_hbm, cx_hbm, cy_hbm, cz_hbm, qw_hbm, sub_hbm, mid_hbm, midl_hbm, eh_hbm, el_hbm,
    out_ref,
    v_ref, own_ref, cx_ref, cy_ref, cz_ref, qw_ref, sub_ref, mid_ref, midl_ref,
    u, xb, yb, zf, pack, halo, eh, el,
    sendq, gotq, passq, haveq, rows, w1, wyb,
    st, vals, sendr, haver, onehot, rankhot,
    s1, r1, s2, r2, s3, r3, sa, ra, sb, rb, sc, rc, lsem, token, clear,
):
    nx, ny, nz = sizes
    g = [float(t) for t in taps()]
    mx, my, mz = lax.axis_index("gx"), lax.axis_index("gy"), lax.axis_index("gz")
    par = lax.rem(my, 2)
    owners = nx * ny
    count = own_ref.shape[1]

    def shifted(first, step):
        on_x = par if first else 1 - par
        on_z = 1 - on_x
        return (
            lax.rem(mx + on_x * (step % nx), nx),
            my,
            lax.rem(mz + on_z * (step % nz), nz),
        )

    def y_peer(step):
        return (mx, lax.rem(my + ny + step, ny), mz)

    def x_peer(step):
        return (lax.rem(mx + step % nx, nx), my, mz)

    def remote(src, dst, ssem, rsem, dev):
        return pltpu.make_async_remote_copy(
            src_ref=src, dst_ref=dst, send_sem=ssem, recv_sem=rsem, device_id=dev, device_id_type=MESH
        )

    loads = [
        pltpu.make_async_copy(src, dst, lsem.at[number])
        for number, (src, dst) in enumerate(
            (
                (v_hbm.at[0], v_ref.at[0]),
                (v_hbm.at[1], v_ref.at[1]),
                (v_hbm.at[2], v_ref.at[2]),
                (own_hbm, own_ref),
                (cx_hbm, cx_ref),
                (cy_hbm, cy_ref),
                (cz_hbm, cz_ref),
                (qw_hbm, qw_ref),
                (sub_hbm, sub_ref),
                (mid_hbm, mid_ref),
                (midl_hbm, midl_ref),
                (eh_hbm, eh),
                (el_hbm, el),
            )
        )
    ]
    for load in loads:
        load.start()

    barrier = pltpu.get_barrier_semaphore()
    near = (x_peer(1), x_peer(-1), y_peer(1), y_peer(-1))
    for peer in near + ((mx, my, lax.rem(mz + 1, nz)), (mx, my, lax.rem(mz + nz - 1, nz))):
        pl.semaphore_signal(barrier, inc=1, device_id=peer, device_id_type=MESH)

    rounds = max(nx, ny) // 2 - 1

    def tell(r):
        for peer in near:
            pl.semaphore_signal(token.at[r], inc=1, device_id=peer, device_id_type=MESH)

    def hear(r):
        pl.semaphore_wait(token.at[r], len(near))

    def first_copies(c):
        src = u.at[c, pl.ds(R, R)]
        return (
            remote(src, u.at[c, pl.ds(0, R)], s1.at[c, 0], r1.at[c, 0], shifted(True, 1)),
            remote(src, u.at[c, pl.ds(2 * R, R)], s1.at[c, 1], r1.at[c, 1], shifted(True, -1)),
        )

    def second_copies(f):
        src = xb.at[f, :, pl.ds(R, R)]
        return (
            remote(src, xb.at[f, :, pl.ds(0, R)], s2.at[f, 0], r2.at[f, 0], shifted(False, 1)),
            remote(src, xb.at[f, :, pl.ds(2 * R, R)], s2.at[f, 1], r2.at[f, 1], shifted(False, -1)),
        )

    def y_copies(f):
        return (
            remote(pack.at[0, f], halo.at[1, f], s3.at[f, 0], r3.at[f, 0], y_peer(-1)),
            remote(pack.at[1, f], halo.at[0, f], s3.at[f, 1], r3.at[f, 1], y_peer(1)),
        )

    def exchange(n, peer_of, me, src, dst, place, ssem, rsem):
        copies = []
        for step in range(1, n):
            copies.append(
                remote(
                    src.at[lax.rem(me + step, n)], dst.at[place[step]], ssem.at[step], rsem.at[step], peer_of(step)
                )
            )
        return copies

    far_x = [nx // 2 + m if h == 0 else nx // 2 - 1 - m for m in range(nx // 2) for h in range(2)]
    place_x = [far_x.index(step) for step in range(nx)]
    order_y = [ny // 2 + i for i in range(ny // 2)] + [ny // 2 - 1 - i for i in range(ny // 2)]
    place_y = [order_y.index(step) for step in range(ny)]

    for c in range(3):
        loads[c].wait()

        @pl.when(par == 0)
        def _():
            u[c, R : 2 * R] = v_ref[c].reshape(R, R, 128)

        @pl.when(par == 1)
        def _():
            for b in range(R):
                u[c, R + b] = v_ref[c, pl.ds(b, R, stride=R), :]

        if c == 0:
            pl.semaphore_wait(barrier, len(near) + 2)
            if rounds:
                tell(0)
        for copy in first_copies(c):
            copy.start()

    for load in loads[3:8]:
        load.wait()
    hot = (lax.broadcasted_iota(jnp.int32, (owners, count), 0) == own_ref[...]).astype(F32)
    onehot[...] = hot.astype(BF16)
    earlier = (
        lax.broadcasted_iota(jnp.int32, (128, 128), 0) < lax.broadcasted_iota(jnp.int32, (128, 128), 1)
    ).astype(BF16)
    carry = jnp.zeros((owners, 1), F32)
    ranks = []
    for block in range(count // 128):
        part = hot[:, block * 128 : block * 128 + 128]
        before = dot(part.astype(BF16), earlier) + carry
        ranks.append(jnp.sum(part * before, axis=0, keepdims=True))
        carry = carry + jnp.sum(part, axis=1, keepdims=True)
    rank = jnp.concatenate(ranks, axis=1)
    slot = lax.broadcasted_iota(jnp.int32, (CAP, count), 0).astype(F32) == rank
    rankhot[...] = slot.astype(F32)
    cell = (cz_ref[...] * R + cx_ref[...]) * 128 + cy_ref[...]

    def pieces(w):
        p0 = w.astype(BF16).astype(F32)
        p1 = (w - p0).astype(BF16).astype(F32)
        p2 = w - p0 - p1
        return p0, p1, p2

    wx = pieces(qw_ref[0:1, :])
    wy = pieces(qw_ref[1:2, :])
    wz = pieces(qw_ref[2:3, :])
    cell_hi = (cell >> 8).astype(F32)
    cell_lo = (cell & 255).astype(F32)
    zero = jnp.zeros_like(cell_lo)
    order = [
        cell_hi, wx[0], cell_lo, wx[1], zero, wx[2],
        wy[0], wz[0], wy[1], wz[1], wy[2], wz[2],
    ]
    placed = jnp.concatenate(
        [jnp.where(slot, p, jnp.zeros_like(p)).astype(BF16) for p in order], axis=0
    )
    spread = lax.dot_general(
        onehot[...], placed, (((1,), (1,)), ((), ())), preferred_element_type=F32
    )
    lane = lax.broadcasted_iota(jnp.int32, (1, 128), 1)
    scale = jnp.where(lane < CAP, 256.0, 1.0)
    head = spread[:, 0:128] * scale + spread[:, 128:256] + spread[:, 256:384]
    tail = spread[:, 384:512] + spread[:, 512:640] + spread[:, 640:768]
    for i in range(nx):
        sendq[i, 0] = head[i * ny : (i + 1) * ny]
        sendq[i, 1] = tail[i * ny : (i + 1) * ny]
    out_x = exchange(nx, x_peer, mx, sendq, gotq, place_x, sa, ra)
    gotq[place_x[0]] = sendq[mx]
    if rounds:
        hear(0)
    if rounds > 1:
        tell(1)

    for copy in first_copies(0):
        copy.wait_send()
    pl.semaphore_signal(clear, inc=1, device_id=y_peer(1 - 2 * par), device_id_type=MESH)

    def first_filter(f):
        i, j = FIELDS[f]

        def chunk(n, _):
            bs = pl.multiple_of((n // 2) * 8, 8)
            h = (n % 2) * 8
            x = u[i, pl.ds(h, 40), pl.ds(bs, 8), :]
            if j is not None:
                x = x * u[j, pl.ds(h, 40), pl.ds(bs, 8), :]
            acc = x[R : R + 8] * g[R]
            for d in range(1, R + 1):
                acc = acc + (x[R - d : R + 8 - d] + x[R + d : R + 8 + d]) * g[R + d]
            xb[f, pl.ds(h, 8), pl.ds(R + bs, 8), :] = acc
            return 0

        lax.fori_loop(0, 4, chunk, 0)
        for copy in second_copies(f):
            copy.start()

    field = 0
    for c in range(3):
        for copy in first_copies(c):
            copy.wait_recv()
        for _ in range(c + 2):
            if field == 0:
                for r in range(1, rounds - 1):
                    hear(r)
                    tell(r + 1)
                pl.semaphore_wait(clear, 1)
            first_filter(field)
            if field == 1:
                if rounds > 1:
                    hear(rounds - 1)
                for copy in out_x:
                    copy.start()
            field += 1

    for copy in out_x:
        copy.wait_recv()
    for j in range(ny):
        for k in range(2):
            passq[j, k] = gotq[:, k, j, :]
    out_y = exchange(ny, y_peer, my, passq, haveq, place_y, sb, rb)
    for copy in out_y:
        copy.start()
    haveq[place_y[0]] = passq[my]

    def hops(chunk):
        step = far_x[2 * chunk // (ny // 2)]
        return min(step, nx - step) + min(2, ny // 4) - 2 * chunk % (ny // 2) // 2

    order = sorted(range(owners * CAP // 256), key=lambda chunk: -hops(chunk))
    codes = [
        int(np.uint32(sum(c << (4 * i) for i, c in enumerate(order[at : at + 8]))).astype(np.int32))
        for at in range(0, len(order), 8)
    ]

    def natural(n):
        code = codes[0] if len(codes) == 1 else jnp.where(n < 8, codes[0], codes[1])
        return lax.shift_right_logical(jnp.int32(code), 4 * (n & 7)) & 15

    def quotient(a, b):
        return a >> (b.bit_length() - 1) if b & (b - 1) == 0 else lax.div(a, b)

    def remainder(a, b):
        return a & (b - 1) if b & (b - 1) == 0 else lax.rem(a, b)

    half = owners // 2
    low = lane < CAP
    chunks = owners * CAP // 256

    def slot_weights():
        for copy in out_y:
            copy.wait_recv()
        def table(k, start):
            return jnp.concatenate(
                [haveq[start : start + ny // 2, k, i, :] for i in range(nx)], axis=0
            )

        tops = [table(k, 0) for k in range(2)]
        bottoms = [table(k, ny // 2) for k in range(2)]

        def paired(k, second):
            top, bottom = tops[k], bottoms[k]
            if second:
                return jnp.where(low, pltpu.roll(top, CAP, 1), bottom)
            return jnp.where(low, top, pltpu.roll(bottom, CAP, 1))

        q_cell = paired(0, False).astype(jnp.int32)
        q_wx = paired(0, True)
        q_wy = paired(1, False)
        q_wz = paired(1, True)
        q_cz = (q_cell >> 11).astype(F32)
        q_cx = ((q_cell >> 7) & (R - 1)).astype(F32)
        z_first = par == 0
        rows[0] = jnp.where(z_first, q_cz, q_cx)
        rows[1] = jnp.where(z_first, q_cx, q_cz)
        rows[2] = (q_cell & 127).astype(F32)
        rows[3] = jnp.where(z_first, q_wz, q_wx)
        rows[4] = jnp.where(z_first, q_wx, q_wz)
        rows[5] = q_wy

        def weights(n, _):
            at = natural(n)

            def row(k):
                return jnp.concatenate([rows[k, pl.ds(2 * at, 1), :], rows[k, pl.ds(2 * at + 1, 1), :]], axis=1)

            def index(size):
                return lax.broadcasted_iota(jnp.int32, (size, 256), 0).astype(F32)

            def eighth(x):
                return jnp.floor(x * 256.0 + 0.5) * (1.0 / 256.0)

            ca, cb, cy = row(0), row(1), row(2)
            wa, wb, wy = eighth(row(3)), eighth(row(4)), row(5)
            both = eighth(wa * wb)
            ib = index(R)
            lower, upper = ib == cb, ib == cb + 1.0
            near = jnp.where(lower, 1.0 - wa - wb + both, jnp.where(upper, wb - both, 0.0))
            far = jnp.where(lower, wa - both, jnp.where(upper, both, 0.0))
            for a in range(R):
                part = jnp.where(ca == float(a), near, jnp.where(ca == float(a - 1), far, 0.0))
                w1[n, R * a : R * a + R, :] = part.astype(BF16)
            iy = index(128)
            wyb[n] = jnp.where(iy == cy, 1.0 - wy, jnp.where(iy == cy + 1.0, wy, 0.0))
            return 0

        lax.fori_loop(0, chunks, weights, 0)

    group = lane // R
    for load in loads[8:]:
        load.wait()

    def second_filter(f, _):
        for copy in second_copies(f):
            copy.wait_recv()

        def pair(n, _):
            x = jnp.concatenate([xb[f, 2 * n], xb[f, 2 * n + 1]], axis=1)
            hi, lo = split(x)
            o = dot(sub_ref[...], jnp.concatenate([hi, hi, lo], axis=0))
            yb[f, pl.ds(pl.multiple_of(32 * n, 32), R), :] = o[:, :128]
            yb[f, pl.ds(pl.multiple_of(32 * n, 32) + R, R), :] = o[:, 128:]
            return 0

        lax.fori_loop(0, R // 2, pair, 0, unroll=True)
        for e in range(2):
            first = jnp.zeros((R, 128), F32)
            last = jnp.zeros((R, 128), F32)
            for k in range(R // 2):
                turned = yb[f, pl.ds(2 * k + e, R, stride=R), :]
                first = jnp.where(group == k, pltpu.roll(turned, R * k, 1) if k else turned, first)
                last = jnp.where(group == k, pltpu.roll(turned, (R * k + R) % 128, 1) if k < 7 else turned, last)
            pack[0, f, e] = first
            pack[1, f, e] = last
        for copy in y_copies(f):
            copy.start()
        hi, lo = split(yb[f])
        zf[f] = dot(jnp.concatenate([hi, lo], axis=1), mid_ref[...]) + dot(hi, midl_ref[...])
        return 0

    rim = (lane >= 128 - R) | (lane < R)

    def finish(first, end):
        def wait_y(f, _):
            for copy in y_copies(f):
                copy.wait_recv()
            return 0

        lax.fori_loop(first, end, wait_y, 0)
        n = end - first
        edges = jnp.concatenate(
            [halo[side, first:end].reshape(32 * n, 128) for side in range(2)], axis=1
        )
        hi, lo = split(edges)
        part = dot(hi, eh[...]) + dot(lo, eh[...]) + dot(hi, el[...])
        for k in range(R // 2):
            q, r = k // 4, k % 4
            turned = pltpu.roll(part[:, 128 * q : 128 * q + 128], (128 - R - 32 * r) % 128, 1)
            zf[first:end, 32 * k : 32 * k + 32, :] += jnp.where(rim, turned, 0.0).reshape(n, 32, 128)

    def stress(first, end):
        for d in range(first, end):
            i, j = DONE[d]
            tau = zf[FIELDS.index((i, j))] - zf[FIELDS.index((i, None))] * zf[FIELDS.index((j, None))]
            hi, lo = split(tau.T)
            st[d, :128] = hi
            st[d, 128:] = lo

    def at_queries(n, first, end):
        acc = dot(st[first:end].reshape(256 * (end - first), 256), w1[n])
        wys = wyb[n]
        found = []
        for d in range(end - first):
            both = acc[256 * d : 256 * d + 128] + acc[256 * d + 128 : 256 * d + 256]
            found.append(jnp.sum(both * wys, axis=0, keepdims=True))
        return found

    block = min(4, chunks)

    def pack_row(at, k, a, b):
        sendr[at, 0, k : k + 1, :] = jnp.where(low, a, pltpu.roll(b, CAP, 1))
        sendr[at, 1, k : k + 1, :] = jnp.where(low, pltpu.roll(a, CAP, 1), b)

    def interpolate(first, end, start, size):
        for n in range(size):
            n = start + n
            found = at_queries(n, first, end)
            for h in range(2):
                at = 2 * n + h
                v = [w[:, 128 * h : 128 * h + 128] for w in found]
                if first == 0:
                    pack_row(at, 0, v[0], v[1])
                    vals[pl.ds(at, 1), :] = v[2]
                else:
                    pack_row(at, 1, vals[pl.ds(at, 1), :], v[0])
                    pack_row(at, 2, v[1], v[2])

    def interpolate_early(start, stop):
        def step(number, _):
            interpolate(0, 3, block * number, block)
            return 0

        lax.fori_loop(start, stop, step, 0)

    me = mx * ny + my
    per = ny // 2

    def back(n, h, side):
        at = 2 * n + h
        where = 2 * natural(n) + h
        x, y = quotient(where, per), remainder(where, per)
        step_x = nx // 2 + (1 - 2 * (x & 1)) * ((x + 1) >> 1)
        step_y = ny // 2 + y if side == 0 else ny // 2 - 1 - y
        holder = (remainder(mx + nx - step_x, nx), remainder(my + ny - step_y, ny), mz)
        return remote(
            sendr.at[at, side], haver.at[me], sc.at[at, side], rc.at[at, side], holder
        )

    def each_back(n, act):
        for h in range(2):
            for side in range(2):
                if h == 1 and side == 1:

                    @pl.when(n < chunks - 1)
                    def _():
                        act(back(n, 1, 1))

                else:
                    act(back(n, h, side))

    def send_back(number, _):
        interpolate(3, 6, block * number, block)

        def send(n, _):
            each_back(n, lambda copy: copy.start())
            return 0

        lax.fori_loop(block * number, block * number + block, send, 0)
        return 0

    early = 1 if chunks // block > 1 else 0

    def second_filters(first, end):
        lax.fori_loop(first, end, second_filter, 0)

    second_filters(0, 6)
    slot_weights()
    finish(0, 5)
    stress(0, 3)
    second_filters(6, 8)
    interpolate_early(0, early)
    second_filters(8, 9)
    if chunks % 8 == 0:
        interpolate(0, 3, block, 6)
        interpolate(0, 3, block + 6, chunks - block - 6)
    else:
        interpolate_early(early, chunks // block)
    finish(5, 8)
    stress(3, 5)
    finish(8, 9)
    stress(5, 6)
    lax.fori_loop(0, chunks // block, send_back, 0)
    haver[me] = sendr[half - 1, 1]

    for c in range(1, 3):
        for copy in first_copies(c):
            copy.wait_send()

    def wait_sends(f, _):
        for copy in second_copies(f) + y_copies(f):
            copy.wait_send()
        return 0

    lax.fori_loop(0, 9, wait_sends, 0)
    for copy in out_y + out_x:
        copy.wait_send()

    def wait_sent(n, _):
        each_back(n, lambda copy: copy.wait_send())
        return 0

    lax.fori_loop(0, chunks, wait_sent, 0)

    def wait_back(n, _):
        each_back(n, lambda copy: copy.wait_recv())
        return 0

    lax.fori_loop(0, chunks, wait_back, 0)
    hot_two = jnp.concatenate([onehot[...], onehot[...]], axis=0)
    at_rank = rankhot[...]
    for k in range(3):
        piece = haver[:, k, :]
        hi = piece.astype(BF16).astype(F32)
        both = jnp.concatenate([hi, piece - hi], axis=0).T.astype(BF16)
        picked = dot(both, hot_two)
        for h in range(2):
            p = PAIRS.index(DONE[2 * k + h])
            out_ref[p : p + 1, :] = jnp.sum(
                picked[CAP * h : CAP * h + CAP] * at_rank, axis=0, keepdims=True
            )


def on_device(sizes, velocity, owner, cell_x, cell_y, cell_z, query_weights):
    nx, ny, nz = sizes
    count = owner.shape[0]
    owners = nx * ny
    half = owners // 2
    chunks = owners * CAP // 256
    vmem = pl.BlockSpec(memory_space=pltpu.VMEM)
    hbm = pl.BlockSpec(memory_space=pltpu.HBM)
    row = pltpu.VMEM((1, count), jnp.int32)
    dma = pltpu.SemaphoreType.DMA
    return pl.pallas_call(
        functools.partial(kernel, sizes),
        out_shape=jax.ShapeDtypeStruct((6, count), F32),
        in_specs=[hbm] * 11,
        out_specs=vmem,
        scratch_shapes=[
            pltpu.VMEM((3, R * R, 128), F32),
            row, row, row, row,
            pltpu.VMEM((3, count), F32),
            pltpu.VMEM((R, 9 * R), BF16),
            pltpu.VMEM((256, 128), BF16),
            pltpu.VMEM((128, 128), BF16),
            pltpu.VMEM((3, 3 * R, R, 128), F32),
            pltpu.VMEM((9, R, 3 * R, 128), F32),
            pltpu.VMEM((9, R * R, 128), F32),
            pltpu.VMEM((9, R * R, 128), F32),
            pltpu.VMEM((2, 9, 2, R, 128), F32),
            pltpu.VMEM((2, 9, 2, R, 128), F32),
            pltpu.VMEM((256, 256), BF16),
            pltpu.VMEM((256, 256), BF16),
            pltpu.VMEM((nx, 2, ny, 128), F32),
            pltpu.VMEM((nx, 2, ny, 128), F32),
            pltpu.VMEM((ny, 2, nx, 128), F32),
            pltpu.VMEM((ny, 2, nx, 128), F32),
            pltpu.VMEM((6, half, 128), F32),
            pltpu.VMEM((chunks, 256, 256), BF16),
            pltpu.VMEM((chunks, 128, 256), F32),
            pltpu.VMEM((6, 256, 256), BF16),
            pltpu.VMEM((half, 128), F32),
            pltpu.VMEM((half, 2, 3, 128), F32),
            pltpu.VMEM((owners, 3, 128), F32),
            pltpu.VMEM((owners, count), BF16),
            pltpu.VMEM((CAP, count), F32),
            dma((3, 2)), dma((3, 2)),
            dma((9, 2)), dma((9, 2)),
            dma((9, 2)), dma((9, 2)),
            dma((nx,)), dma((nx,)),
            dma((ny,)), dma((ny,)),
            dma((half, 2)), dma((half, 2)),
            dma((13,)),
            pltpu.SemaphoreType.REGULAR((max(1, max(nx, ny) // 2 - 1),)),
            pltpu.SemaphoreType.REGULAR,
        ],
        compiler_params=pltpu.CompilerParams(
            collective_id=0, has_side_effects=True, vmem_limit_bytes=40 * 1024 * 1024
        ),
    )(
        *[
            pltpu.with_memory_space_constraint(x, pltpu.HBM)
            for x in (
                velocity.reshape(3, R * R, 128),
                owner.reshape(1, count),
                cell_x.reshape(1, count),
                cell_y.reshape(1, count),
                cell_z.reshape(1, count),
                query_weights,
                *tables(velocity.shape[3]),
            )
        ]
    )


def solution(mesh):
    sizes = (mesh.shape["gx"], mesh.shape["gy"], mesh.shape["gz"])
    placed = (
        P(None, "gz", "gx", "gy"),
        P(("gx", "gy", "gz"), None),
        P(("gx", "gy", "gz")),
        P(("gx", "gy", "gz")),
        P(("gx", "gy", "gz")),
        P(None, ("gx", "gy", "gz")),
    )
    return jax.shard_map(
        functools.partial(on_device, sizes),
        mesh=mesh,
        in_specs=placed,
        out_specs=P(None, ("gx", "gy", "gz")),
        check_vma=False,
    )
```

```python
import functools

import jax
import jax.numpy as jnp
import numpy as np
from jax import lax
from jax.experimental import pallas as pl
from jax.experimental.pallas import tpu as pltpu
from jax.sharding import PartitionSpec as P

MESH = pl.DeviceIdType.MESH
F32 = jnp.float32
BF16 = jnp.bfloat16
FW = 32
R = FW // 2
CAP = 64
FIELDS = ((0, None), (0, 0), (1, None), (0, 1), (1, 1), (2, None), (0, 2), (1, 2), (2, 2))
PAIRS = ((0, 0), (0, 1), (0, 2), (1, 1), (1, 2), (2, 2))
DONE = ((0, 0), (0, 1), (1, 1), (0, 2), (1, 2), (2, 2))


def taps():
    offsets = np.arange(2 * R + 1).astype(np.float32) - np.float32(R)
    values = np.exp(np.float32(-6.0) * offsets * offsets / np.float32(FW * FW))
    return (values / values.sum(dtype=np.float32)).astype(np.float32)


def split(x):
    hi = x.astype(BF16)
    lo = (x - hi.astype(F32)).astype(BF16)
    return hi, lo


def np_split(x):
    hi = jnp.asarray(x, F32).astype(BF16)
    lo = (jnp.asarray(x, F32) - hi.astype(F32)).astype(BF16)
    return hi, lo


def tables(by):
    g = taps()

    def band(rows, cols, shift):
        m = np.arange(rows)[:, None] - np.arange(cols)[None, :] + shift
        return np.where((m >= 0) & (m <= 2 * R), g[np.clip(m, 0, 2 * R)], np.float32(0))

    sub = band(3 * R, R, 0).T
    mid = band(by, by, R)
    left = band(R, by, 0)
    right = band(R, by, by + R)
    edge = np.zeros((256, 256), np.float32)
    for k in range(R // 2):
        edge[128 + R * k : 128 + R * k + R, 32 * k : 32 * k + R] = right[:, by - R :]
        edge[R * k : R * k + R, 32 * k + R : 32 * k + 32] = left[:, :R]
    sh, sl = np_split(sub)
    mh, ml = np_split(mid)
    eh, el = np_split(edge)
    return (
        jnp.concatenate([sh, sl, sh], axis=1),
        jnp.concatenate([mh, mh], axis=0),
        ml,
        eh,
        el,
    )


def dot(a, b):
    return jnp.dot(a, b, preferred_element_type=F32)


def kernel(
    sizes,
    v_hbm, own_hbm, cx_hbm, cy_hbm, cz_hbm, qw_hbm, sub_hbm, mid_hbm, midl_hbm, eh_hbm, el_hbm,
    out_ref,
    v_ref, own_ref, cx_ref, cy_ref, cz_ref, qw_ref, sub_ref, mid_ref, midl_ref,
    u, xb, yb, zf, pack, halo, eh, el,
    sendq, gotq, passq, haveq, rows, w1, wyb,
    st, vals, sendr, haver, onehot, rankhot,
    s1, r1, s2, r2, s3, r3, sa, ra, sb, rb, sc, rc, lsem, token, clear,
):
    nx, ny, nz = sizes
    g = [float(t) for t in taps()]
    mx, my, mz = lax.axis_index("gx"), lax.axis_index("gy"), lax.axis_index("gz")
    par = lax.rem(my, 2)
    owners = nx * ny
    count = own_ref.shape[1]

    def shifted(first, step):
        on_x = par if first else 1 - par
        on_z = 1 - on_x
        return (
            lax.rem(mx + on_x * (step % nx), nx),
            my,
            lax.rem(mz + on_z * (step % nz), nz),
        )

    def y_peer(step):
        return (mx, lax.rem(my + ny + step, ny), mz)

    def x_peer(step):
        return (lax.rem(mx + step % nx, nx), my, mz)

    def remote(src, dst, ssem, rsem, dev):
        return pltpu.make_async_remote_copy(
            src_ref=src, dst_ref=dst, send_sem=ssem, recv_sem=rsem, device_id=dev, device_id_type=MESH
        )

    loads = [
        pltpu.make_async_copy(src, dst, lsem.at[number])
        for number, (src, dst) in enumerate(
            (
                (v_hbm.at[0], v_ref.at[0]),
                (v_hbm.at[1], v_ref.at[1]),
                (v_hbm.at[2], v_ref.at[2]),
                (own_hbm, own_ref),
                (cx_hbm, cx_ref),
                (cy_hbm, cy_ref),
                (cz_hbm, cz_ref),
                (qw_hbm, qw_ref),
                (sub_hbm, sub_ref),
                (mid_hbm, mid_ref),
                (midl_hbm, midl_ref),
                (eh_hbm, eh),
                (el_hbm, el),
            )
        )
    ]
    for load in loads:
        load.start()

    barrier = pltpu.get_barrier_semaphore()
    near = (x_peer(1), x_peer(-1), y_peer(1), y_peer(-1))
    for peer in near + ((mx, my, lax.rem(mz + 1, nz)), (mx, my, lax.rem(mz + nz - 1, nz))):
        pl.semaphore_signal(barrier, inc=1, device_id=peer, device_id_type=MESH)

    rounds = max(nx, ny) // 2 - 1

    def tell(r):
        for peer in near:
            pl.semaphore_signal(token.at[r], inc=1, device_id=peer, device_id_type=MESH)

    def hear(r):
        pl.semaphore_wait(token.at[r], len(near))

    def first_copies(c):
        src = u.at[c, pl.ds(R, R)]
        return (
            remote(src, u.at[c, pl.ds(0, R)], s1.at[c, 0], r1.at[c, 0], shifted(True, 1)),
            remote(src, u.at[c, pl.ds(2 * R, R)], s1.at[c, 1], r1.at[c, 1], shifted(True, -1)),
        )

    def second_copies(f):
        src = xb.at[f, :, pl.ds(R, R)]
        return (
            remote(src, xb.at[f, :, pl.ds(0, R)], s2.at[f, 0], r2.at[f, 0], shifted(False, 1)),
            remote(src, xb.at[f, :, pl.ds(2 * R, R)], s2.at[f, 1], r2.at[f, 1], shifted(False, -1)),
        )

    def y_copies(f):
        return (
            remote(pack.at[0, f], halo.at[1, f], s3.at[f, 0], r3.at[f, 0], y_peer(-1)),
            remote(pack.at[1, f], halo.at[0, f], s3.at[f, 1], r3.at[f, 1], y_peer(1)),
        )

    def exchange(n, peer_of, me, src, dst, place, ssem, rsem):
        copies = []
        for step in range(1, n):
            copies.append(
                remote(
                    src.at[lax.rem(me + step, n)], dst.at[place[step]], ssem.at[step], rsem.at[step], peer_of(step)
                )
            )
        return copies

    far_x = [nx // 2 + m if h == 0 else nx // 2 - 1 - m for m in range(nx // 2) for h in range(2)]
    place_x = [far_x.index(step) for step in range(nx)]
    order_y = [ny // 2 + i for i in range(ny // 2)] + [ny // 2 - 1 - i for i in range(ny // 2)]
    place_y = [order_y.index(step) for step in range(ny)]

    for c in range(3):
        loads[c].wait()

        @pl.when(par == 0)
        def _():
            u[c, R : 2 * R] = v_ref[c].reshape(R, R, 128)

        @pl.when(par == 1)
        def _():
            for b in range(R):
                u[c, R + b] = v_ref[c, pl.ds(b, R, stride=R), :]

        if c == 0:
            pl.semaphore_wait(barrier, len(near) + 2)
            if rounds:
                tell(0)
        for copy in first_copies(c):
            copy.start()

    for load in loads[3:8]:
        load.wait()
    hot = (lax.broadcasted_iota(jnp.int32, (owners, count), 0) == own_ref[...]).astype(F32)
    onehot[...] = hot.astype(BF16)
    earlier = (
        lax.broadcasted_iota(jnp.int32, (128, 128), 0) < lax.broadcasted_iota(jnp.int32, (128, 128), 1)
    ).astype(BF16)
    carry = jnp.zeros((owners, 1), F32)
    ranks = []
    for block in range(count // 128):
        part = hot[:, block * 128 : block * 128 + 128]
        before = dot(part.astype(BF16), earlier) + carry
        ranks.append(jnp.sum(part * before, axis=0, keepdims=True))
        carry = carry + jnp.sum(part, axis=1, keepdims=True)
    rank = jnp.concatenate(ranks, axis=1)
    slot = lax.broadcasted_iota(jnp.int32, (CAP, count), 0).astype(F32) == rank
    rankhot[...] = slot.astype(F32)
    cell = (cz_ref[...] * R + cx_ref[...]) * 128 + cy_ref[...]

    def pieces(w):
        p0 = w.astype(BF16).astype(F32)
        p1 = (w - p0).astype(BF16).astype(F32)
        p2 = w - p0 - p1
        return p0, p1, p2

    wx = pieces(qw_ref[0:1, :])
    wy = pieces(qw_ref[1:2, :])
    wz = pieces(qw_ref[2:3, :])
    cell_hi = (cell >> 8).astype(F32)
    cell_lo = (cell & 255).astype(F32)
    zero = jnp.zeros_like(cell_lo)
    order = [
        cell_hi, wx[0], cell_lo, wx[1], zero, wx[2],
        wy[0], wz[0], wy[1], wz[1], wy[2], wz[2],
    ]
    placed = jnp.concatenate(
        [jnp.where(slot, p, jnp.zeros_like(p)).astype(BF16) for p in order], axis=0
    )
    spread = lax.dot_general(
        onehot[...], placed, (((1,), (1,)), ((), ())), preferred_element_type=F32
    )
    lane = lax.broadcasted_iota(jnp.int32, (1, 128), 1)
    scale = jnp.where(lane < CAP, 256.0, 1.0)
    head = spread[:, 0:128] * scale + spread[:, 128:256] + spread[:, 256:384]
    tail = spread[:, 384:512] + spread[:, 512:640] + spread[:, 640:768]
    for i in range(nx):
        sendq[i, 0] = head[i * ny : (i + 1) * ny]
        sendq[i, 1] = tail[i * ny : (i + 1) * ny]
    out_x = exchange(nx, x_peer, mx, sendq, gotq, place_x, sa, ra)
    gotq[place_x[0]] = sendq[mx]
    if rounds:
        hear(0)
    if rounds > 1:
        tell(1)

    for copy in first_copies(0):
        copy.wait_send()
    pl.semaphore_signal(clear, inc=1, device_id=y_peer(1 - 2 * par), device_id_type=MESH)

    def first_filter(f):
        i, j = FIELDS[f]

        def chunk(n, _):
            bs = pl.multiple_of((n // 2) * 8, 8)
            h = (n % 2) * 8
            x = u[i, pl.ds(h, 40), pl.ds(bs, 8), :]
            if j is not None:
                x = x * u[j, pl.ds(h, 40), pl.ds(bs, 8), :]
            acc = x[R : R + 8] * g[R]
            for d in range(1, R + 1):
                acc = acc + (x[R - d : R + 8 - d] + x[R + d : R + 8 + d]) * g[R + d]
            xb[f, pl.ds(h, 8), pl.ds(R + bs, 8), :] = acc
            return 0

        lax.fori_loop(0, 4, chunk, 0)
        for copy in second_copies(f):
            copy.start()

    field = 0
    for c in range(3):
        for copy in first_copies(c):
            copy.wait_recv()
        for _ in range(c + 2):
            if field == 0:
                for r in range(1, rounds - 1):
                    hear(r)
                    tell(r + 1)
                pl.semaphore_wait(clear, 1)
            first_filter(field)
            if field == 0:
                if rounds > 1:
                    hear(rounds - 1)
                for copy in out_x:
                    copy.start()
            field += 1

    for copy in out_x:
        copy.wait_recv()
    for j in range(ny):
        for k in range(2):
            passq[j, k] = gotq[:, k, j, :]
    out_y = exchange(ny, y_peer, my, passq, haveq, place_y, sb, rb)
    for copy in out_y:
        copy.start()
    haveq[place_y[0]] = passq[my]

    def hops(chunk):
        step = far_x[2 * chunk // (ny // 2)]
        return min(step, nx - step) + min(2, ny // 4) - 2 * chunk % (ny // 2) // 2

    order = sorted(range(owners * CAP // 256), key=lambda chunk: -hops(chunk))
    codes = [
        int(np.uint32(sum(c << (4 * i) for i, c in enumerate(order[at : at + 8]))).astype(np.int32))
        for at in range(0, len(order), 8)
    ]

    def natural(n):
        code = codes[0] if len(codes) == 1 else jnp.where(n < 8, codes[0], codes[1])
        return lax.shift_right_logical(jnp.int32(code), 4 * (n & 7)) & 15

    def quotient(a, b):
        return a >> (b.bit_length() - 1) if b & (b - 1) == 0 else lax.div(a, b)

    def remainder(a, b):
        return a & (b - 1) if b & (b - 1) == 0 else lax.rem(a, b)

    half = owners // 2
    low = lane < CAP
    chunks = owners * CAP // 256

    def slot_weights():
        for copy in out_y:
            copy.wait_recv()
        def table(k, start):
            return jnp.concatenate(
                [haveq[start : start + ny // 2, k, i, :] for i in range(nx)], axis=0
            )

        tops = [table(k, 0) for k in range(2)]
        bottoms = [table(k, ny // 2) for k in range(2)]

        def paired(k, second):
            top, bottom = tops[k], bottoms[k]
            if second:
                return jnp.where(low, pltpu.roll(top, CAP, 1), bottom)
            return jnp.where(low, top, pltpu.roll(bottom, CAP, 1))

        q_cell = paired(0, False).astype(jnp.int32)
        q_wx = paired(0, True)
        q_wy = paired(1, False)
        q_wz = paired(1, True)
        q_cz = (q_cell >> 11).astype(F32)
        q_cx = ((q_cell >> 7) & (R - 1)).astype(F32)
        z_first = par == 0
        rows[0] = jnp.where(z_first, q_cz, q_cx)
        rows[1] = jnp.where(z_first, q_cx, q_cz)
        rows[2] = (q_cell & 127).astype(F32)
        rows[3] = jnp.where(z_first, q_wz, q_wx)
        rows[4] = jnp.where(z_first, q_wx, q_wz)
        rows[5] = q_wy

        def weights(n, _):
            at = natural(n)

            def row(k):
                return jnp.concatenate([rows[k, pl.ds(2 * at, 1), :], rows[k, pl.ds(2 * at + 1, 1), :]], axis=1)

            def index(size):
                return lax.broadcasted_iota(jnp.int32, (size, 256), 0).astype(F32)

            def eighth(x):
                return jnp.floor(x * 256.0 + 0.5) * (1.0 / 256.0)

            ca, cb, cy = row(0), row(1), row(2)
            wa, wb, wy = eighth(row(3)), eighth(row(4)), row(5)
            both = eighth(wa * wb)
            ib = index(R)
            lower, upper = ib == cb, ib == cb + 1.0
            near = jnp.where(lower, 1.0 - wa - wb + both, jnp.where(upper, wb - both, 0.0))
            far = jnp.where(lower, wa - both, jnp.where(upper, both, 0.0))
            for a in range(R):
                part = jnp.where(ca == float(a), near, jnp.where(ca == float(a - 1), far, 0.0))
                w1[n, R * a : R * a + R, :] = part.astype(BF16)
            iy = index(128)
            wyb[n] = jnp.where(iy == cy, 1.0 - wy, jnp.where(iy == cy + 1.0, wy, 0.0))
            return 0

        lax.fori_loop(0, chunks, weights, 0)

    group = lane // R
    for load in loads[8:]:
        load.wait()

    def second_filter(f, _):
        for copy in second_copies(f):
            copy.wait_recv()

        def pair(n, _):
            x = jnp.concatenate([xb[f, 2 * n], xb[f, 2 * n + 1]], axis=1)
            hi, lo = split(x)
            o = dot(sub_ref[...], jnp.concatenate([hi, hi, lo], axis=0))
            yb[f, pl.ds(pl.multiple_of(32 * n, 32), R), :] = o[:, :128]
            yb[f, pl.ds(pl.multiple_of(32 * n, 32) + R, R), :] = o[:, 128:]
            return 0

        lax.fori_loop(0, R // 2, pair, 0, unroll=True)
        for e in range(2):
            first = jnp.zeros((R, 128), F32)
            last = jnp.zeros((R, 128), F32)
            for k in range(R // 2):
                turned = yb[f, pl.ds(2 * k + e, R, stride=R), :]
                first = jnp.where(group == k, pltpu.roll(turned, R * k, 1) if k else turned, first)
                last = jnp.where(group == k, pltpu.roll(turned, (R * k + R) % 128, 1) if k < 7 else turned, last)
            pack[0, f, e] = first
            pack[1, f, e] = last
        for copy in y_copies(f):
            copy.start()
        hi, lo = split(yb[f])
        zf[f] = dot(jnp.concatenate([hi, lo], axis=1), mid_ref[...]) + dot(hi, midl_ref[...])
        return 0

    rim = (lane >= 128 - R) | (lane < R)

    def finish(first, end):
        def wait_y(f, _):
            for copy in y_copies(f):
                copy.wait_recv()
            return 0

        lax.fori_loop(first, end, wait_y, 0)
        n = end - first
        edges = jnp.concatenate(
            [halo[side, first:end].reshape(32 * n, 128) for side in range(2)], axis=1
        )
        hi, lo = split(edges)
        part = dot(hi, eh[...]) + dot(lo, eh[...]) + dot(hi, el[...])
        for k in range(R // 2):
            q, r = k // 4, k % 4
            turned = pltpu.roll(part[:, 128 * q : 128 * q + 128], (128 - R - 32 * r) % 128, 1)
            zf[first:end, 32 * k : 32 * k + 32, :] += jnp.where(rim, turned, 0.0).reshape(n, 32, 128)

    def stress(first, end):
        for d in range(first, end):
            i, j = DONE[d]
            tau = zf[FIELDS.index((i, j))] - zf[FIELDS.index((i, None))] * zf[FIELDS.index((j, None))]
            hi, lo = split(tau.T)
            st[d, :128] = hi
            st[d, 128:] = lo

    def at_queries(n, first, end):
        acc = dot(st[first:end].reshape(256 * (end - first), 256), w1[n])
        wys = wyb[n]
        found = []
        for d in range(end - first):
            both = acc[256 * d : 256 * d + 128] + acc[256 * d + 128 : 256 * d + 256]
            found.append(jnp.sum(both * wys, axis=0, keepdims=True))
        return found

    block = min(4, chunks)

    def pack_row(at, k, a, b):
        sendr[at, 0, k : k + 1, :] = jnp.where(low, a, pltpu.roll(b, CAP, 1))
        sendr[at, 1, k : k + 1, :] = jnp.where(low, pltpu.roll(a, CAP, 1), b)

    def interpolate(first, end, start, size):
        for n in range(size):
            n = start + n
            found = at_queries(n, first, end)
            for h in range(2):
                at = 2 * n + h
                v = [w[:, 128 * h : 128 * h + 128] for w in found]
                if first == 0:
                    pack_row(at, 0, v[0], v[1])
                    vals[pl.ds(at, 1), :] = v[2]
                else:
                    pack_row(at, 1, vals[pl.ds(at, 1), :], v[0])
                    pack_row(at, 2, v[1], v[2])

    def interpolate_early(start, stop):
        def step(number, _):
            interpolate(0, 3, block * number, block)
            return 0

        lax.fori_loop(start, stop, step, 0)

    me = mx * ny + my
    per = ny // 2

    def back(n, h, side):
        at = 2 * n + h
        where = 2 * natural(n) + h
        x, y = quotient(where, per), remainder(where, per)
        step_x = nx // 2 + (1 - 2 * (x & 1)) * ((x + 1) >> 1)
        step_y = ny // 2 + y if side == 0 else ny // 2 - 1 - y
        holder = (remainder(mx + nx - step_x, nx), remainder(my + ny - step_y, ny), mz)
        return remote(
            sendr.at[at, side], haver.at[me], sc.at[at, side], rc.at[at, side], holder
        )

    def each_back(n, act):
        for h in range(2):
            for side in range(2):
                if h == 1 and side == 1:

                    @pl.when(n < chunks - 1)
                    def _():
                        act(back(n, 1, 1))

                else:
                    act(back(n, h, side))

    def send_back(number, _):
        interpolate(3, 6, block * number, block)

        def send(n, _):
            each_back(n, lambda copy: copy.start())
            return 0

        lax.fori_loop(block * number, block * number + block, send, 0)
        return 0

    early = 1 if chunks // block > 1 else 0

    def second_filters(first, end):
        lax.fori_loop(first, end, second_filter, 0)

    second_filters(0, 6)
    slot_weights()
    finish(0, 5)
    stress(0, 3)
    second_filters(6, 8)
    interpolate_early(0, early)
    second_filters(8, 9)
    if chunks % 8 == 0:
        interpolate(0, 3, block, 6)
        interpolate(0, 3, block + 6, chunks - block - 6)
    else:
        interpolate_early(early, chunks // block)
    finish(5, 8)
    stress(3, 5)
    finish(8, 9)
    stress(5, 6)
    lax.fori_loop(0, chunks // block, send_back, 0)
    haver[me] = sendr[half - 1, 1]

    for c in range(1, 3):
        for copy in first_copies(c):
            copy.wait_send()

    def wait_sends(f, _):
        for copy in second_copies(f) + y_copies(f):
            copy.wait_send()
        return 0

    lax.fori_loop(0, 9, wait_sends, 0)
    for copy in out_y + out_x:
        copy.wait_send()

    def wait_sent(n, _):
        each_back(n, lambda copy: copy.wait_send())
        return 0

    lax.fori_loop(0, chunks, wait_sent, 0)

    def wait_back(n, _):
        each_back(n, lambda copy: copy.wait_recv())
        return 0

    lax.fori_loop(0, chunks, wait_back, 0)
    hot_two = jnp.concatenate([onehot[...], onehot[...]], axis=0)
    at_rank = rankhot[...]
    for k in range(3):
        piece = haver[:, k, :]
        hi = piece.astype(BF16).astype(F32)
        both = jnp.concatenate([hi, piece - hi], axis=0).T.astype(BF16)
        picked = dot(both, hot_two)
        for h in range(2):
            p = PAIRS.index(DONE[2 * k + h])
            out_ref[p : p + 1, :] = jnp.sum(
                picked[CAP * h : CAP * h + CAP] * at_rank, axis=0, keepdims=True
            )


def on_device(sizes, velocity, owner, cell_x, cell_y, cell_z, query_weights):
    nx, ny, nz = sizes
    count = owner.shape[0]
    owners = nx * ny
    half = owners // 2
    chunks = owners * CAP // 256
    vmem = pl.BlockSpec(memory_space=pltpu.VMEM)
    hbm = pl.BlockSpec(memory_space=pltpu.HBM)
    row = pltpu.VMEM((1, count), jnp.int32)
    dma = pltpu.SemaphoreType.DMA
    return pl.pallas_call(
        functools.partial(kernel, sizes),
        out_shape=jax.ShapeDtypeStruct((6, count), F32),
        in_specs=[hbm] * 11,
        out_specs=vmem,
        scratch_shapes=[
            pltpu.VMEM((3, R * R, 128), F32),
            row, row, row, row,
            pltpu.VMEM((3, count), F32),
            pltpu.VMEM((R, 9 * R), BF16),
            pltpu.VMEM((256, 128), BF16),
            pltpu.VMEM((128, 128), BF16),
            pltpu.VMEM((3, 3 * R, R, 128), F32),
            pltpu.VMEM((9, R, 3 * R, 128), F32),
            pltpu.VMEM((9, R * R, 128), F32),
            pltpu.VMEM((9, R * R, 128), F32),
            pltpu.VMEM((2, 9, 2, R, 128), F32),
            pltpu.VMEM((2, 9, 2, R, 128), F32),
            pltpu.VMEM((256, 256), BF16),
            pltpu.VMEM((256, 256), BF16),
            pltpu.VMEM((nx, 2, ny, 128), F32),
            pltpu.VMEM((nx, 2, ny, 128), F32),
            pltpu.VMEM((ny, 2, nx, 128), F32),
            pltpu.VMEM((ny, 2, nx, 128), F32),
            pltpu.VMEM((6, half, 128), F32),
            pltpu.VMEM((chunks, 256, 256), BF16),
            pltpu.VMEM((chunks, 128, 256), F32),
            pltpu.VMEM((6, 256, 256), BF16),
            pltpu.VMEM((half, 128), F32),
            pltpu.VMEM((half, 2, 3, 128), F32),
            pltpu.VMEM((owners, 3, 128), F32),
            pltpu.VMEM((owners, count), BF16),
            pltpu.VMEM((CAP, count), F32),
            dma((3, 2)), dma((3, 2)),
            dma((9, 2)), dma((9, 2)),
            dma((9, 2)), dma((9, 2)),
            dma((nx,)), dma((nx,)),
            dma((ny,)), dma((ny,)),
            dma((half, 2)), dma((half, 2)),
            dma((13,)),
            pltpu.SemaphoreType.REGULAR((max(1, max(nx, ny) // 2 - 1),)),
            pltpu.SemaphoreType.REGULAR,
        ],
        compiler_params=pltpu.CompilerParams(
            collective_id=0, has_side_effects=True, vmem_limit_bytes=40 * 1024 * 1024
        ),
    )(
        *[
            pltpu.with_memory_space_constraint(x, pltpu.HBM)
            for x in (
                velocity.reshape(3, R * R, 128),
                owner.reshape(1, count),
                cell_x.reshape(1, count),
                cell_y.reshape(1, count),
                cell_z.reshape(1, count),
                query_weights,
                *tables(velocity.shape[3]),
            )
        ]
    )


def solution(mesh):
    sizes = (mesh.shape["gx"], mesh.shape["gy"], mesh.shape["gz"])
    placed = (
        P(None, "gz", "gx", "gy"),
        P(("gx", "gy", "gz"), None),
        P(("gx", "gy", "gz")),
        P(("gx", "gy", "gz")),
        P(("gx", "gy", "gz")),
        P(None, ("gx", "gy", "gz")),
    )
    return jax.shard_map(
        functools.partial(on_device, sizes),
        mesh=mesh,
        in_specs=placed,
        out_specs=P(None, ("gx", "gy", "gz")),
        check_vma=False,
    )
```

```python
import functools

import jax
import jax.numpy as jnp
import numpy as np
from jax import lax
from jax.experimental import pallas as pl
from jax.experimental.pallas import tpu as pltpu
from jax.sharding import PartitionSpec as P

MESH = pl.DeviceIdType.MESH
F32 = jnp.float32
BF16 = jnp.bfloat16
FW = 32
R = FW // 2
CAP = 64
FIELDS = ((0, None), (0, 0), (1, None), (0, 1), (1, 1), (2, None), (0, 2), (1, 2), (2, 2))
PAIRS = ((0, 0), (0, 1), (0, 2), (1, 1), (1, 2), (2, 2))
DONE = ((0, 0), (0, 1), (1, 1), (0, 2), (1, 2), (2, 2))


def taps():
    offsets = np.arange(2 * R + 1).astype(np.float32) - np.float32(R)
    values = np.exp(np.float32(-6.0) * offsets * offsets / np.float32(FW * FW))
    return (values / values.sum(dtype=np.float32)).astype(np.float32)


def split(x):
    hi = x.astype(BF16)
    lo = (x - hi.astype(F32)).astype(BF16)
    return hi, lo


def np_split(x):
    hi = jnp.asarray(x, F32).astype(BF16)
    lo = (jnp.asarray(x, F32) - hi.astype(F32)).astype(BF16)
    return hi, lo


def tables(by):
    g = taps()

    def band(rows, cols, shift):
        m = np.arange(rows)[:, None] - np.arange(cols)[None, :] + shift
        return np.where((m >= 0) & (m <= 2 * R), g[np.clip(m, 0, 2 * R)], np.float32(0))

    sub = band(3 * R, R, 0).T
    mid = band(by, by, R)
    left = band(R, by, 0)
    right = band(R, by, by + R)
    edge = np.zeros((256, 256), np.float32)
    for k in range(R // 2):
        edge[128 + R * k : 128 + R * k + R, 32 * k : 32 * k + R] = right[:, by - R :]
        edge[R * k : R * k + R, 32 * k + R : 32 * k + 32] = left[:, :R]
    sh, sl = np_split(sub)
    mh, ml = np_split(mid)
    eh, el = np_split(edge)
    return (
        jnp.concatenate([sh, sl, sh], axis=1),
        jnp.concatenate([mh, mh], axis=0),
        ml,
        eh,
        el,
    )


def dot(a, b):
    return jnp.dot(a, b, preferred_element_type=F32)


def kernel(
    sizes,
    v_hbm, own_hbm, cx_hbm, cy_hbm, cz_hbm, qw_hbm, sub_hbm, mid_hbm, midl_hbm, eh_hbm, el_hbm,
    out_ref,
    v_ref, own_ref, cx_ref, cy_ref, cz_ref, qw_ref, sub_ref, mid_ref, midl_ref,
    u, xb, yb, zf, pack, halo, eh, el,
    sendq, gotq, passq, haveq, rows, w1, wyb,
    st, vals, sendr, haver, onehot, rankhot,
    s1, r1, s2, r2, s3, r3, sa, ra, sb, rb, sc, rc, lsem, token, clear,
):
    nx, ny, nz = sizes
    g = [float(t) for t in taps()]
    mx, my, mz = lax.axis_index("gx"), lax.axis_index("gy"), lax.axis_index("gz")
    par = lax.rem(my, 2)
    owners = nx * ny
    count = own_ref.shape[1]

    def shifted(first, step):
        on_x = par if first else 1 - par
        on_z = 1 - on_x
        return (
            lax.rem(mx + on_x * (step % nx), nx),
            my,
            lax.rem(mz + on_z * (step % nz), nz),
        )

    def y_peer(step):
        return (mx, lax.rem(my + ny + step, ny), mz)

    def x_peer(step):
        return (lax.rem(mx + step % nx, nx), my, mz)

    def remote(src, dst, ssem, rsem, dev):
        return pltpu.make_async_remote_copy(
            src_ref=src, dst_ref=dst, send_sem=ssem, recv_sem=rsem, device_id=dev, device_id_type=MESH
        )

    loads = [
        pltpu.make_async_copy(src, dst, lsem.at[number])
        for number, (src, dst) in enumerate(
            (
                (v_hbm.at[0], v_ref.at[0]),
                (v_hbm.at[1], v_ref.at[1]),
                (v_hbm.at[2], v_ref.at[2]),
                (own_hbm, own_ref),
                (cx_hbm, cx_ref),
                (cy_hbm, cy_ref),
                (cz_hbm, cz_ref),
                (qw_hbm, qw_ref),
                (sub_hbm, sub_ref),
                (mid_hbm, mid_ref),
                (midl_hbm, midl_ref),
                (eh_hbm, eh),
                (el_hbm, el),
            )
        )
    ]
    for load in loads:
        load.start()

    barrier = pltpu.get_barrier_semaphore()
    near = (x_peer(1), x_peer(-1), y_peer(1), y_peer(-1))
    for peer in near + ((mx, my, lax.rem(mz + 1, nz)), (mx, my, lax.rem(mz + nz - 1, nz))):
        pl.semaphore_signal(barrier, inc=1, device_id=peer, device_id_type=MESH)

    rounds = max(nx, ny) // 2 - 1

    def tell(r):
        for peer in near:
            pl.semaphore_signal(token.at[r], inc=1, device_id=peer, device_id_type=MESH)

    def hear(r):
        pl.semaphore_wait(token.at[r], len(near))

    def first_copies(c):
        src = u.at[c, pl.ds(R, R)]
        return (
            remote(src, u.at[c, pl.ds(0, R)], s1.at[c, 0], r1.at[c, 0], shifted(True, 1)),
            remote(src, u.at[c, pl.ds(2 * R, R)], s1.at[c, 1], r1.at[c, 1], shifted(True, -1)),
        )

    def second_copies(f):
        src = xb.at[f, :, pl.ds(R, R)]
        return (
            remote(src, xb.at[f, :, pl.ds(0, R)], s2.at[f, 0], r2.at[f, 0], shifted(False, 1)),
            remote(src, xb.at[f, :, pl.ds(2 * R, R)], s2.at[f, 1], r2.at[f, 1], shifted(False, -1)),
        )

    def y_copies(f):
        return (
            remote(pack.at[0, f], halo.at[1, f], s3.at[f, 0], r3.at[f, 0], y_peer(-1)),
            remote(pack.at[1, f], halo.at[0, f], s3.at[f, 1], r3.at[f, 1], y_peer(1)),
        )

    def exchange(n, peer_of, me, src, dst, place, ssem, rsem):
        copies = []
        for step in range(1, n):
            copies.append(
                remote(
                    src.at[lax.rem(me + step, n)], dst.at[place[step]], ssem.at[step], rsem.at[step], peer_of(step)
                )
            )
        return copies

    far_x = [nx // 2 + m if h == 0 else nx // 2 - 1 - m for m in range(nx // 2) for h in range(2)]
    place_x = [far_x.index(step) for step in range(nx)]
    order_y = [ny // 2 + i for i in range(ny // 2)] + [ny // 2 - 1 - i for i in range(ny // 2)]
    place_y = [order_y.index(step) for step in range(ny)]

    for c in range(3):
        loads[c].wait()

        @pl.when(par == 0)
        def _():
            u[c, R : 2 * R] = v_ref[c].reshape(R, R, 128)

        @pl.when(par == 1)
        def _():
            for b in range(R):
                u[c, R + b] = v_ref[c, pl.ds(b, R, stride=R), :]

        if c == 0:
            pl.semaphore_wait(barrier, len(near) + 2)
            if rounds:
                tell(0)
        for copy in first_copies(c):
            copy.start()

    for load in loads[3:8]:
        load.wait()
    hot = (lax.broadcasted_iota(jnp.int32, (owners, count), 0) == own_ref[...]).astype(F32)
    onehot[...] = hot.astype(BF16)
    earlier = (
        lax.broadcasted_iota(jnp.int32, (128, 128), 0) < lax.broadcasted_iota(jnp.int32, (128, 128), 1)
    ).astype(BF16)
    carry = jnp.zeros((owners, 1), F32)
    ranks = []
    for block in range(count // 128):
        part = hot[:, block * 128 : block * 128 + 128]
        before = dot(part.astype(BF16), earlier) + carry
        ranks.append(jnp.sum(part * before, axis=0, keepdims=True))
        carry = carry + jnp.sum(part, axis=1, keepdims=True)
    rank = jnp.concatenate(ranks, axis=1)
    slot = lax.broadcasted_iota(jnp.int32, (CAP, count), 0).astype(F32) == rank
    rankhot[...] = slot.astype(F32)
    cell = (cz_ref[...] * R + cx_ref[...]) * 128 + cy_ref[...]

    def pieces(w):
        p0 = w.astype(BF16).astype(F32)
        p1 = (w - p0).astype(BF16).astype(F32)
        p2 = w - p0 - p1
        return p0, p1, p2

    wx = pieces(qw_ref[0:1, :])
    wy = pieces(qw_ref[1:2, :])
    wz = pieces(qw_ref[2:3, :])
    cell_hi = (cell >> 8).astype(F32)
    cell_lo = (cell & 255).astype(F32)
    zero = jnp.zeros_like(cell_lo)
    order = [
        cell_hi, wx[0], cell_lo, wx[1], zero, wx[2],
        wy[0], wz[0], wy[1], wz[1], wy[2], wz[2],
    ]
    placed = jnp.concatenate(
        [jnp.where(slot, p, jnp.zeros_like(p)).astype(BF16) for p in order], axis=0
    )
    spread = lax.dot_general(
        onehot[...], placed, (((1,), (1,)), ((), ())), preferred_element_type=F32
    )
    lane = lax.broadcasted_iota(jnp.int32, (1, 128), 1)
    scale = jnp.where(lane < CAP, 256.0, 1.0)
    head = spread[:, 0:128] * scale + spread[:, 128:256] + spread[:, 256:384]
    tail = spread[:, 384:512] + spread[:, 512:640] + spread[:, 640:768]
    for i in range(nx):
        sendq[i, 0] = head[i * ny : (i + 1) * ny]
        sendq[i, 1] = tail[i * ny : (i + 1) * ny]
    out_x = exchange(nx, x_peer, mx, sendq, gotq, place_x, sa, ra)
    gotq[place_x[0]] = sendq[mx]
    if rounds:
        hear(0)
    if rounds > 1:
        tell(1)

    for copy in first_copies(0):
        copy.wait_send()
    pl.semaphore_signal(clear, inc=1, device_id=y_peer(1 - 2 * par), device_id_type=MESH)

    def first_filter(f):
        i, j = FIELDS[f]

        def chunk(n, _):
            bs = pl.multiple_of((n // 2) * 8, 8)
            h = (n % 2) * 8
            x = u[i, pl.ds(h, 40), pl.ds(bs, 8), :]
            if j is not None:
                x = x * u[j, pl.ds(h, 40), pl.ds(bs, 8), :]
            acc = x[R : R + 8] * g[R]
            for d in range(1, R + 1):
                acc = acc + (x[R - d : R + 8 - d] + x[R + d : R + 8 + d]) * g[R + d]
            xb[f, pl.ds(h, 8), pl.ds(R + bs, 8), :] = acc
            return 0

        lax.fori_loop(0, 4, chunk, 0)
        for copy in second_copies(f):
            copy.start()

    field = 0
    for c in range(3):
        for copy in first_copies(c):
            copy.wait_recv()
        for _ in range(c + 2):
            if field == 0:
                for r in range(1, rounds - 1):
                    hear(r)
                    tell(r + 1)
                pl.semaphore_wait(clear, 1)
            first_filter(field)
            if field == 1:
                if rounds > 1:
                    hear(rounds - 1)
                for copy in out_x:
                    copy.start()
            field += 1

    for copy in out_x:
        copy.wait_recv()
    for j in range(ny):
        for k in range(2):
            passq[j, k] = gotq[:, k, j, :]
    out_y = exchange(ny, y_peer, my, passq, haveq, place_y, sb, rb)
    for copy in out_y:
        copy.start()
    haveq[place_y[0]] = passq[my]

    def hops(chunk):
        step = far_x[2 * chunk // (ny // 2)]
        return min(step, nx - step) + min(2, ny // 4) - 2 * chunk % (ny // 2) // 2

    order = sorted(range(owners * CAP // 256), key=lambda chunk: -hops(chunk))
    codes = [
        int(np.uint32(sum(c << (4 * i) for i, c in enumerate(order[at : at + 8]))).astype(np.int32))
        for at in range(0, len(order), 8)
    ]

    def natural(n):
        code = codes[0] if len(codes) == 1 else jnp.where(n < 8, codes[0], codes[1])
        return lax.shift_right_logical(jnp.int32(code), 4 * (n & 7)) & 15

    def quotient(a, b):
        return a >> (b.bit_length() - 1) if b & (b - 1) == 0 else lax.div(a, b)

    def remainder(a, b):
        return a & (b - 1) if b & (b - 1) == 0 else lax.rem(a, b)

    half = owners // 2
    low = lane < CAP
    chunks = owners * CAP // 256

    def slot_weights():
        for copy in out_y:
            copy.wait_recv()
        def table(k, start):
            return jnp.concatenate(
                [haveq[start : start + ny // 2, k, i, :] for i in range(nx)], axis=0
            )

        tops = [table(k, 0) for k in range(2)]
        bottoms = [table(k, ny // 2) for k in range(2)]

        def paired(k, second):
            top, bottom = tops[k], bottoms[k]
            if second:
                return jnp.where(low, pltpu.roll(top, CAP, 1), bottom)
            return jnp.where(low, top, pltpu.roll(bottom, CAP, 1))

        q_cell = paired(0, False).astype(jnp.int32)
        q_wx = paired(0, True)
        q_wy = paired(1, False)
        q_wz = paired(1, True)
        q_cz = (q_cell >> 11).astype(F32)
        q_cx = ((q_cell >> 7) & (R - 1)).astype(F32)
        z_first = par == 0
        rows[0] = jnp.where(z_first, q_cz, q_cx)
        rows[1] = jnp.where(z_first, q_cx, q_cz)
        rows[2] = (q_cell & 127).astype(F32)
        rows[3] = jnp.where(z_first, q_wz, q_wx)
        rows[4] = jnp.where(z_first, q_wx, q_wz)
        rows[5] = q_wy

        def weights(n, _):
            at = natural(n)

            def row(k):
                return jnp.concatenate([rows[k, pl.ds(2 * at, 1), :], rows[k, pl.ds(2 * at + 1, 1), :]], axis=1)

            def index(size):
                return lax.broadcasted_iota(jnp.int32, (size, 256), 0).astype(F32)

            def eighth(x):
                return jnp.floor(x * 256.0 + 0.5) * (1.0 / 256.0)

            ca, cb, cy = row(0), row(1), row(2)
            wa, wb, wy = eighth(row(3)), eighth(row(4)), row(5)
            both = eighth(wa * wb)
            ib = index(R)
            lower, upper = ib == cb, ib == cb + 1.0
            near = jnp.where(lower, 1.0 - wa - wb + both, jnp.where(upper, wb - both, 0.0))
            far = jnp.where(lower, wa - both, jnp.where(upper, both, 0.0))
            for a in range(R):
                part = jnp.where(ca == float(a), near, jnp.where(ca == float(a - 1), far, 0.0))
                w1[n, R * a : R * a + R, :] = part.astype(BF16)
            iy = index(128)
            wyb[n] = jnp.where(iy == cy, 1.0 - wy, jnp.where(iy == cy + 1.0, wy, 0.0))
            return 0

        lax.fori_loop(0, chunks, weights, 0)

    group = lane // R
    for load in loads[8:]:
        load.wait()

    def second_filter(f, _):
        for copy in second_copies(f):
            copy.wait_recv()

        def pair(n, _):
            x = jnp.concatenate([xb[f, 2 * n], xb[f, 2 * n + 1]], axis=1)
            hi, lo = split(x)
            o = dot(sub_ref[...], jnp.concatenate([hi, hi, lo], axis=0))
            yb[f, pl.ds(pl.multiple_of(32 * n, 32), R), :] = o[:, :128]
            yb[f, pl.ds(pl.multiple_of(32 * n, 32) + R, R), :] = o[:, 128:]
            return 0

        lax.fori_loop(0, R // 2, pair, 0, unroll=True)
        for e in range(2):
            first = jnp.zeros((R, 128), F32)
            last = jnp.zeros((R, 128), F32)
            for k in range(R // 2):
                turned = yb[f, pl.ds(2 * k + e, R, stride=R), :]
                first = jnp.where(group == k, pltpu.roll(turned, R * k, 1) if k else turned, first)
                last = jnp.where(group == k, pltpu.roll(turned, (R * k + R) % 128, 1) if k < 7 else turned, last)
            pack[0, f, e] = first
            pack[1, f, e] = last
        for copy in y_copies(f):
            copy.start()
        hi, lo = split(yb[f])
        zf[f] = dot(jnp.concatenate([hi, lo], axis=1), mid_ref[...]) + dot(hi, midl_ref[...])
        return 0

    rim = (lane >= 128 - R) | (lane < R)

    def finish(first, end):
        def wait_y(f, _):
            for copy in y_copies(f):
                copy.wait_recv()
            return 0

        lax.fori_loop(first, end, wait_y, 0)
        n = end - first
        edges = jnp.concatenate(
            [halo[side, first:end].reshape(32 * n, 128) for side in range(2)], axis=1
        )
        hi, lo = split(edges)
        part = dot(hi, eh[...]) + dot(lo, eh[...]) + dot(hi, el[...])
        for k in range(R // 2):
            q, r = k // 4, k % 4
            turned = pltpu.roll(part[:, 128 * q : 128 * q + 128], (128 - R - 32 * r) % 128, 1)
            zf[first:end, 32 * k : 32 * k + 32, :] += jnp.where(rim, turned, 0.0).reshape(n, 32, 128)

    def stress(first, end):
        for d in range(first, end):
            i, j = DONE[d]
            tau = zf[FIELDS.index((i, j))] - zf[FIELDS.index((i, None))] * zf[FIELDS.index((j, None))]
            hi, lo = split(tau.T)
            st[d, :128] = hi
            st[d, 128:] = lo

    def at_queries(n, first, end):
        acc = dot(st[first:end].reshape(256 * (end - first), 256), w1[n])
        wys = wyb[n]
        found = []
        for d in range(end - first):
            both = acc[256 * d : 256 * d + 128] + acc[256 * d + 128 : 256 * d + 256]
            found.append(jnp.sum(both * wys, axis=0, keepdims=True))
        return found

    block = min(4, chunks)

    def pack_row(at, k, a, b):
        sendr[at, 0, k : k + 1, :] = jnp.where(low, a, pltpu.roll(b, CAP, 1))
        sendr[at, 1, k : k + 1, :] = jnp.where(low, pltpu.roll(a, CAP, 1), b)

    def interpolate(first, end, start, size):
        for n in range(size):
            n = start + n
            found = at_queries(n, first, end)
            for h in range(2):
                at = 2 * n + h
                v = [w[:, 128 * h : 128 * h + 128] for w in found]
                if first == 0:
                    pack_row(at, 0, v[0], v[1])
                    vals[pl.ds(at, 1), :] = v[2]
                else:
                    pack_row(at, 1, vals[pl.ds(at, 1), :], v[0])
                    pack_row(at, 2, v[1], v[2])

    def interpolate_early(start, stop):
        def step(number, _):
            interpolate(0, 3, block * number, block)
            return 0

        lax.fori_loop(start, stop, step, 0)

    me = mx * ny + my
    per = ny // 2

    def back(n, h, side):
        at = 2 * n + h
        where = 2 * natural(n) + h
        x, y = quotient(where, per), remainder(where, per)
        step_x = nx // 2 + (1 - 2 * (x & 1)) * ((x + 1) >> 1)
        step_y = ny // 2 + y if side == 0 else ny // 2 - 1 - y
        holder = (remainder(mx + nx - step_x, nx), remainder(my + ny - step_y, ny), mz)
        return remote(
            sendr.at[at, side], haver.at[me], sc.at[at, side], rc.at[at, side], holder
        )

    def each_back(n, act):
        for h in range(2):
            for side in range(2):
                if h == 1 and side == 1:

                    @pl.when(n < chunks - 1)
                    def _():
                        act(back(n, 1, 1))

                else:
                    act(back(n, h, side))

    def send_back(number, _):
        interpolate(3, 6, block * number, block)

        def send(n, _):
            each_back(n, lambda copy: copy.start())
            return 0

        lax.fori_loop(block * number, block * number + block, send, 0)
        return 0

    early = 1 if chunks // block > 1 else 0

    def second_filters(first, end):
        lax.fori_loop(first, end, second_filter, 0)

    second_filters(0, 6)
    slot_weights()
    finish(0, 5)
    stress(0, 3)
    second_filters(6, 8)
    interpolate_early(0, early)
    second_filters(8, 9)
    if chunks % 8 == 0:
        interpolate(0, 3, block, chunks - block)
    else:
        interpolate_early(early, chunks // block)
    finish(5, 8)
    stress(3, 5)
    finish(8, 9)
    stress(5, 6)
    lax.fori_loop(0, chunks // block, send_back, 0)
    haver[me] = sendr[half - 1, 1]

    for c in range(1, 3):
        for copy in first_copies(c):
            copy.wait_send()

    def wait_sends(f, _):
        for copy in second_copies(f) + y_copies(f):
            copy.wait_send()
        return 0

    lax.fori_loop(0, 9, wait_sends, 0)
    for copy in out_y + out_x:
        copy.wait_send()

    def wait_sent(n, _):
        each_back(n, lambda copy: copy.wait_send())
        return 0

    lax.fori_loop(0, chunks, wait_sent, 0)

    def wait_back(n, _):
        each_back(n, lambda copy: copy.wait_recv())
        return 0

    lax.fori_loop(0, chunks, wait_back, 0)
    hot_two = jnp.concatenate([onehot[...], onehot[...]], axis=0)
    at_rank = rankhot[...]
    for k in range(3):
        piece = haver[:, k, :]
        hi = piece.astype(BF16).astype(F32)
        both = jnp.concatenate([hi, piece - hi], axis=0).T.astype(BF16)
        picked = dot(both, hot_two)
        for h in range(2):
            p = PAIRS.index(DONE[2 * k + h])
            out_ref[p : p + 1, :] = jnp.sum(
                picked[CAP * h : CAP * h + CAP] * at_rank, axis=0, keepdims=True
            )


def on_device(sizes, velocity, owner, cell_x, cell_y, cell_z, query_weights):
    nx, ny, nz = sizes
    count = owner.shape[0]
    owners = nx * ny
    half = owners // 2
    chunks = owners * CAP // 256
    vmem = pl.BlockSpec(memory_space=pltpu.VMEM)
    hbm = pl.BlockSpec(memory_space=pltpu.HBM)
    row = pltpu.VMEM((1, count), jnp.int32)
    dma = pltpu.SemaphoreType.DMA
    return pl.pallas_call(
        functools.partial(kernel, sizes),
        out_shape=jax.ShapeDtypeStruct((6, count), F32),
        in_specs=[hbm] * 11,
        out_specs=vmem,
        scratch_shapes=[
            pltpu.VMEM((3, R * R, 128), F32),
            row, row, row, row,
            pltpu.VMEM((3, count), F32),
            pltpu.VMEM((R, 9 * R), BF16),
            pltpu.VMEM((256, 128), BF16),
            pltpu.VMEM((128, 128), BF16),
            pltpu.VMEM((3, 3 * R, R, 128), F32),
            pltpu.VMEM((9, R, 3 * R, 128), F32),
            pltpu.VMEM((9, R * R, 128), F32),
            pltpu.VMEM((9, R * R, 128), F32),
            pltpu.VMEM((2, 9, 2, R, 128), F32),
            pltpu.VMEM((2, 9, 2, R, 128), F32),
            pltpu.VMEM((256, 256), BF16),
            pltpu.VMEM((256, 256), BF16),
            pltpu.VMEM((nx, 2, ny, 128), F32),
            pltpu.VMEM((nx, 2, ny, 128), F32),
            pltpu.VMEM((ny, 2, nx, 128), F32),
            pltpu.VMEM((ny, 2, nx, 128), F32),
            pltpu.VMEM((6, half, 128), F32),
            pltpu.VMEM((chunks, 256, 256), BF16),
            pltpu.VMEM((chunks, 128, 256), F32),
            pltpu.VMEM((6, 256, 256), BF16),
            pltpu.VMEM((half, 128), F32),
            pltpu.VMEM((half, 2, 3, 128), F32),
            pltpu.VMEM((owners, 3, 128), F32),
            pltpu.VMEM((owners, count), BF16),
            pltpu.VMEM((CAP, count), F32),
            dma((3, 2)), dma((3, 2)),
            dma((9, 2)), dma((9, 2)),
            dma((9, 2)), dma((9, 2)),
            dma((nx,)), dma((nx,)),
            dma((ny,)), dma((ny,)),
            dma((half, 2)), dma((half, 2)),
            dma((13,)),
            pltpu.SemaphoreType.REGULAR((max(1, max(nx, ny) // 2 - 1),)),
            pltpu.SemaphoreType.REGULAR,
        ],
        compiler_params=pltpu.CompilerParams(
            collective_id=0, has_side_effects=True, vmem_limit_bytes=40 * 1024 * 1024
        ),
    )(
        *[
            pltpu.with_memory_space_constraint(x, pltpu.HBM)
            for x in (
                velocity.reshape(3, R * R, 128),
                owner.reshape(1, count),
                cell_x.reshape(1, count),
                cell_y.reshape(1, count),
                cell_z.reshape(1, count),
                query_weights,
                *tables(velocity.shape[3]),
            )
        ]
    )


def solution(mesh):
    sizes = (mesh.shape["gx"], mesh.shape["gy"], mesh.shape["gz"])
    placed = (
        P(None, "gz", "gx", "gy"),
        P(("gx", "gy", "gz"), None),
        P(("gx", "gy", "gz")),
        P(("gx", "gy", "gz")),
        P(("gx", "gy", "gz")),
        P(None, ("gx", "gy", "gz")),
    )
    return jax.shard_map(
        functools.partial(on_device, sizes),
        mesh=mesh,
        in_specs=placed,
        out_specs=P(None, ("gx", "gy", "gz")),
        check_vma=False,
    )
```
